32 devices in a mesh: shard: 32 (over z, y, x, core).
Axes of the slice: x: 2, y: 2, z: 4, core: 2. Of those that a mesh axis runs over, the one named last changes fastest.
Arguments:
- hidden: bfloat16 [96, 512, 768], P('shard'), may hold values from -6 to 6
- teacher_input: bfloat16 [96, 512, 768], P('shard'), may hold values from -6 to 6
- cotangent: bfloat16 [96, 512, 768], P('shard'), may hold values from -6 to 6
- lengths: int32 [96], P('shard'), may hold values from 33 to 512, as said below
- lat_qkv: float32 [768, 2304], P('shard'), as said below
- lat_out: float32 [768, 768], P('shard'), as said below
- lat_up: float32 [768, 3072], P('shard'), as said below
- lat_down: float32 [3072, 768], P('shard'), as said below
- bias_q: float32 [768], replicated, may hold values from -0.5 to 0.5
- bias_v: float32 [768], replicated, may hold values from -0.5 to 0.5
- bias_out: float32 [768], replicated, may hold values from -0.5 to 0.5
- bias_up: float32 [3072], replicated, may hold values from -0.5 to 0.5
- bias_down: float32 [768], replicated, may hold values from -0.5 to 0.5
- gain_one: float32 [768], replicated, may hold values from 0.5 to 1.5
- shift_one: float32 [768], replicated, may hold values from -0.3 to 0.3
- gain_two: float32 [768], replicated, may hold values from 0.5 to 1.5
- shift_two: float32 [768], replicated, may hold values from -0.3 to 0.3
- clips: float32 [4], replicated, as said below
- teach_qkv: bfloat16 [768, 2304], P('shard'), may hold values from -0.21875 to 0.21875
- teach_out: bfloat16 [768, 768], P('shard'), may hold values from -1.75 to 1.75
- teach_up: bfloat16 [768, 3072], P('shard'), may hold values from -0.21875 to 0.21875
- teach_down: bfloat16 [3072, 768], P('shard'), may hold values from -0.109375 to 0.109375
Outputs:
- mixed_out: bfloat16 [96, 512, 768], P('shard')
- input_grad: bfloat16 [96, 512, 768], P('shard')
- grad_lat_qkv: float32 [768, 2304], P('shard')
- grad_lat_out: float32 [768, 768], P('shard')
- grad_lat_up: float32 [768, 3072], P('shard')
- grad_lat_down: float32 [3072, 768], P('shard')
- grad_bias_q: float32 [768], replicated
- grad_bias_v: float32 [768], replicated
- grad_bias_out: float32 [768], replicated
- grad_bias_up: float32 [3072], replicated
- grad_bias_down: float32 [768], replicated
- grad_gain_one: float32 [768], replicated
- grad_shift_one: float32 [768], replicated
- grad_gain_two: float32 [768], replicated
- grad_shift_two: float32 [768], replicated
- grad_clips: float32 [4], replicated
The draws below stay inside these ranges and needn't reach their ends.
Inputs may be any that keep to these rules, and one draw needn't show every extreme that they name: `lengths`: live tokens of each row, at the start of the row; some row has all 512. `lat_qkv`: no entry is zero; within each matrix every magnitude lies within a factor of ten of the largest. `lat_out`: no entry is zero; within each matrix every magnitude lies within a factor of ten of the largest. `lat_up`: no entry is zero; within each matrix every magnitude lies within a factor of ten of the largest. `lat_down`: no entry is zero; within each matrix every magnitude lies within a factor of ten of the largest. `clips`: all four bounds are positive.
All inputs are finite; a program needn't handle non-finite values.
Results may differ from the reference program's by a relative error of at most 0.015.
The reference program's roundings to bfloat16 on the way count: a program that leaves them out, or rounds other values in their place, can miss the bound.
Values may be sent and summed in bfloat16 or wider, within the bound.
A program may use at most 320 MiB of HBM per device.

```python
import math
import jax
import jax.numpy as jnp
from jax import lax

D = 768
FF = 3072
HEADS = 12
HEAD_DIM = 64
ROW = 512
ROWS = 96


def latent_matrix(key, height, breadth, factor):
    first, second = jax.random.split(key)
    magnitude = jnp.exp(jax.random.uniform(first, (height, breadth), jnp.float32, math.log(0.1), 0.0))
    direction = (jax.random.randint(second, (height, breadth), 0, 2) * 2 - 1).astype(jnp.float32)
    return (factor / math.sqrt(height) * magnitude * direction).astype(jnp.float32)


def draw_lat_qkv(key, part):
    return latent_matrix(jax.random.fold_in(key, 11), D, 3 * D, 1.2)


def draw_lat_out(key, part):
    return latent_matrix(jax.random.fold_in(key, 12), D, D, 20.0)


def draw_lat_up(key, part):
    return latent_matrix(jax.random.fold_in(key, 13), D, FF, 2.5)


def draw_lat_down(key, part):
    return latent_matrix(jax.random.fold_in(key, 14), FF, D, 2.5)


def draw_clips(key, part):
    jitter = jax.random.uniform(jax.random.fold_in(key, 15), (4,), jnp.float32, 0.85, 1.15)
    return (jitter * jnp.array([1.6, 0.3, 1.6, 1.6], jnp.float32)).astype(jnp.float32)


def draw_lengths(key, part):
    first, second, third = jax.random.split(jax.random.fold_in(key, 16), 3)
    lowest = ROW // 16 + 1
    drawn = jax.random.randint(first, (ROWS,), lowest, ROW + 1)
    other = jax.random.randint(second, (ROWS,), lowest, ROW + 1)
    toss = jax.random.randint(third, (ROWS,), 0, 2)
    chosen = jnp.where(toss == 1, drawn, jnp.minimum(drawn, other))
    return chosen.at[0].set(ROW).astype(jnp.int32)


def block_scale(stream_key, dims, cuts, low, high):
    gain = 1.0
    for position, parts in cuts:
        heights = jax.random.uniform(jax.random.fold_in(jax.random.fold_in(stream_key, 6), position), (parts,), jnp.float32, low / len(cuts), high / len(cuts))
        gain = gain * jnp.repeat(jnp.exp(heights), dims[position] // parts).reshape((-1,) + (1,) * (len(dims) - 1 - position))
    return gain


def centred(own_key, shape, deviation, reach, cuts=(), held_as=jnp.bfloat16):
    result = jax.random.normal(own_key, shape, jnp.float32) * deviation
    if len(cuts) > 0:
        result = block_scale(own_key, shape, cuts, -0.22, 0.18) * result
    return jnp.clip(result, min=-reach, max=reach).astype(held_as)


def setup_inputs(seed: int = 0) -> dict:
    arg_keys = jax.random.split(jax.random.key(seed), 23)
    hidden = centred(arg_keys[0], (ROWS, ROW, D), 1.0, 6.0, ((0, 32),))
    teacher_input = centred(arg_keys[1], (ROWS, ROW, D), 1.0, 6.0, ((0, 32),))
    cotangent = centred(arg_keys[2], (ROWS, ROW, D), 1.0, 6.0, ((0, 32),))
    lengths = draw_lengths(jax.random.fold_in(arg_keys[22], 71), 0)
    lat_qkv = draw_lat_qkv(jax.random.fold_in(arg_keys[22], 71), 0)
    lat_out = draw_lat_out(jax.random.fold_in(arg_keys[22], 71), 0)
    lat_up = draw_lat_up(jax.random.fold_in(arg_keys[22], 71), 0)
    lat_down = draw_lat_down(jax.random.fold_in(arg_keys[22], 71), 0)
    bias_q = jnp.clip(jax.random.uniform(arg_keys[8], (D,), jnp.float32, -0.5, 0.5), -0.5, 0.5)
    bias_v = jnp.clip(jax.random.uniform(arg_keys[9], (D,), jnp.float32, -0.5, 0.5), -0.5, 0.5)
    bias_out = jnp.clip(jax.random.uniform(arg_keys[10], (D,), jnp.float32, -0.5, 0.5), -0.5, 0.5)
    bias_up = jnp.clip(jax.random.uniform(arg_keys[11], (FF,), jnp.float32, -0.5, 0.5), -0.5, 0.5)
    bias_down = jnp.clip(jax.random.uniform(arg_keys[12], (D,), jnp.float32, -0.5, 0.5), -0.5, 0.5)
    gain_one = jnp.clip(1.0 + 0.1 * jax.random.normal(arg_keys[13], (D,), jnp.float32), 0.5, 1.5)
    shift_one = jnp.clip(jax.random.uniform(arg_keys[14], (D,), jnp.float32, -0.3, 0.3), -0.3, 0.3)
    gain_two = jnp.clip(1.0 + 0.1 * jax.random.normal(arg_keys[15], (D,), jnp.float32), 0.5, 1.5)
    shift_two = jnp.clip(jax.random.uniform(arg_keys[16], (D,), jnp.float32, -0.3, 0.3), -0.3, 0.3)
    clips = draw_clips(jax.random.fold_in(arg_keys[22], 71), 0)
    teach_qkv = centred(arg_keys[18], (D, 3 * D), D ** -0.5, 0.21875, ((0, 32),))
    teach_out = centred(arg_keys[19], (D, D), (D // 64) ** -0.5, 1.75, ((0, 32),))
    teach_up = centred(arg_keys[20], (D, FF), D ** -0.5, 0.21875, ((0, 32),))
    teach_down = centred(arg_keys[21], (FF, D), FF ** -0.5, 0.109375, ((0, 32),))
    return dict(hidden=hidden, teacher_input=teacher_input, cotangent=cotangent, lengths=lengths, lat_qkv=lat_qkv, lat_out=lat_out, lat_up=lat_up, lat_down=lat_down, bias_q=bias_q, bias_v=bias_v, bias_out=bias_out, bias_up=bias_up, bias_down=bias_down, gain_one=gain_one, shift_one=shift_one, gain_two=gain_two, shift_two=shift_two, clips=clips, teach_qkv=teach_qkv, teach_out=teach_out, teach_up=teach_up, teach_down=teach_down)


EPSILON = 1e-05
MASKED = -1000000000.0

@jax.custom_vjp
def low(v):
    return lax.optimization_barrier(v.astype(jnp.bfloat16)).astype(jnp.float32)

@jax.custom_vjp
def low_back(v):
    return v

def low_keep(v):
    return (low(v), None)

def low_pass(kept, grad):
    return (grad,)

def back_keep(v):
    return (v, None)

def back_low(kept, grad):
    return (low(grad),)
low.defvjp(low_keep, low_pass)
low_back.defvjp(back_keep, back_low)

def binarize(latent):
    factor = lax.optimization_barrier(jnp.mean(jnp.abs(latent), axis=1, keepdims=True))
    return (factor * jnp.sign(latent)).astype(jnp.bfloat16).astype(jnp.float32)

def layer_norm(value):
    center = value - lax.optimization_barrier(jnp.mean(value, axis=-1, keepdims=True))
    spread = lax.optimization_barrier(jnp.mean(center * center, axis=-1, keepdims=True))
    return center * lax.rsqrt(spread + EPSILON)

def product_rows(left, weight):
    return jnp.einsum('rtd,de->rte', left, weight, precision=lax.Precision.HIGHEST)

def split_heads(value):
    return value.reshape(value.shape[0], value.shape[1], HEADS, HEAD_DIM)

def head_scores(queries, keys):
    raw = jnp.einsum('rqhe,rkhe->rhqk', split_heads(queries), split_heads(keys), precision=lax.Precision.HIGHEST)
    return raw * (1.0 / math.sqrt(HEAD_DIM))

def mix_heads(probs, values):
    mixed = jnp.einsum('rhqk,rkhe->rqhe', probs, split_heads(values), precision=lax.Precision.HIGHEST)
    return mixed.reshape(values.shape)

def softmax_live(scores, key_live):
    masked = jnp.where(key_live, scores, MASKED)
    top = lax.optimization_barrier(jnp.max(masked, axis=-1, keepdims=True))
    expo = jnp.exp(masked - top)
    return expo / lax.optimization_barrier(jnp.sum(expo, axis=-1, keepdims=True))

def teacher_pass(inputs, teach, key_live):
    t_qkv, t_out, t_up, t_down = teach
    joined = product_rows(inputs, t_qkv)
    queries = low(joined[..., :D])
    keys = low(joined[..., D:2 * D])
    values = low(joined[..., 2 * D:])
    probs = softmax_live(head_scores(queries, keys), key_live)
    context = low(mix_heads(low(probs), values))
    first = layer_norm(inputs + product_rows(context, t_out))
    inner = product_rows(low(first), t_up)
    second = layer_norm(first + product_rows(low(jax.nn.gelu(inner, approximate=False)), t_down))
    return (head_scores(queries, keys), second)

def group_pass(params, teach, slab):
    x_rows, teach_rows, lens = slab
    positions = jnp.arange(ROW, dtype=jnp.int32)
    live = positions[None, :] < lens[:, None]
    live_f = live.astype(jnp.float32)
    key_live = live[:, None, None, :]
    pair = live_f[:, None, :, None] * live_f[:, None, None, :]
    t_scores, t_out = teacher_pass(teach_rows, teach, key_live)
    bounds = params['clips']
    a_in = low(jnp.clip(x_rows, -bounds[0], bounds[0]))
    joined = product_rows(a_in, params['w_qkv'])
    queries = low_back(low(joined[..., :D] + params['bias_q']))
    keys = low_back(low(joined[..., D:2 * D]))
    values = low_back(low(joined[..., 2 * D:] + params['bias_v']))
    scores = low_back(head_scores(queries, keys))
    score_gap = scores - t_scores
    distill = 0.5 / ROW * jnp.sum(pair * score_gap * score_gap)
    probs = softmax_live(scores, key_live)
    context = low_back(mix_heads(low(probs), values))
    cut = low(jnp.clip(context, -bounds[1], bounds[1]))
    attn = low_back(product_rows(cut, params['w_out']) + params['bias_out'])
    h_one = layer_norm(x_rows + attn) * params['gain_one'] + params['shift_one']
    up_in = low(jnp.clip(h_one, -bounds[2], bounds[2]))
    pre = low_back(product_rows(up_in, params['w_up']) + params['bias_up'])
    act = low(jnp.clip(jax.nn.gelu(pre, approximate=False), -bounds[3], bounds[3]))
    down = low_back(product_rows(act, params['w_down']) + params['bias_down'])
    out = layer_norm(h_one + down) * params['gain_two'] + params['shift_two']
    gap = out - t_out
    loss = distill + 0.5 * jnp.sum(live_f[..., None] * gap * gap)
    return (out, loss)

def reference(hidden, teacher_input, cotangent, lengths, lat_qkv, lat_out, lat_up, lat_down, bias_q, bias_v, bias_out, bias_up, bias_down, gain_one, shift_one, gain_two, shift_two, clips, teach_qkv, teach_out, teach_up, teach_down):
    params = {'w_qkv': binarize(lat_qkv), 'w_out': binarize(lat_out), 'w_up': binarize(lat_up), 'w_down': binarize(lat_down), 'bias_q': bias_q, 'bias_v': bias_v, 'bias_out': bias_out, 'bias_up': bias_up, 'bias_down': bias_down, 'gain_one': gain_one, 'shift_one': shift_one, 'gain_two': gain_two, 'shift_two': shift_two, 'clips': clips, 'hidden': hidden.astype(jnp.float32)}
    teach = (teach_qkv.astype(jnp.float32), teach_out.astype(jnp.float32), teach_up.astype(jnp.float32), teach_down.astype(jnp.float32))
    groups = ROWS // 8
    teach_rows = teacher_input.astype(jnp.float32).reshape(groups, 8, ROW, D)
    lens_rows = lengths.astype(jnp.int32).reshape(groups, 8)

    def forward(params):
        x_rows = params['hidden'].reshape(groups, 8, ROW, D)

        def step(total, slab):
            out, loss = group_pass(params, teach, slab)
            return (total + loss, out)
        start = jnp.zeros((), jnp.float32) + jnp.zeros((), params['hidden'].dtype)
        total, outs = lax.scan(jax.checkpoint(step), start, (x_rows, teach_rows, lens_rows))
        return (outs.reshape(ROWS, ROW, D), total)
    (out, total), pull = jax.vjp(forward, params)
    positions = jnp.arange(ROW, dtype=jnp.int32)
    live_f = (positions[None, :] < lengths[:, None]).astype(jnp.float32)
    start_grad = (cotangent.astype(jnp.float32) * live_f[..., None]).astype(out.dtype)
    grads = pull((start_grad, jnp.ones((), total.dtype)))[0]
    return (out.astype(jnp.bfloat16), grads['hidden'].astype(jnp.bfloat16), grads['w_qkv'], grads['w_out'], grads['w_up'], grads['w_down'], grads['bias_q'], grads['bias_v'], grads['bias_out'], grads['bias_up'], grads['bias_down'], grads['gain_one'], grads['shift_one'], grads['gain_two'], grads['shift_two'], grads['clips'])
```

```python
import functools
import math

import jax
import jax.numpy as jnp
from jax import lax
from jax.experimental import pallas as pl
from jax.experimental.pallas import tpu as pltpu
from jax.sharding import PartitionSpec as P

D = 768
FF = 3072
HEAD_DIM = 64
PAIR = 2 * HEAD_DIM
PAIRS = D // PAIR
CHUNKS = FF // D

EPSILON = 1e-05
MASKED = -1000000000.0
SCALE = 1.0 / math.sqrt(HEAD_DIM)

F32 = jnp.float32
BF16 = jnp.bfloat16
MESH = pl.DeviceIdType.MESH
VMEM_LIMIT = 60 * 1024 * 1024


def nn(left, right):
    return lax.dot_general(left, right, (((1,), (0,)), ((), ())), preferred_element_type=F32)


def nt(left, right):
    return lax.dot_general(left, right, (((1,), (1,)), ((), ())), preferred_element_type=F32)


def tn(left, right):
    return lax.dot_general(left, right, (((0,), (0,)), ((), ())), preferred_element_type=F32)


def signed_mean(latent):
    factor = jnp.mean(jnp.abs(latent), axis=1, keepdims=True)
    sign = jnp.where(latent > 0, 1.0, jnp.where(latent < 0, -1.0, 0.0))
    return (factor * sign).astype(BF16)


def normalize(value):
    center = value - jnp.mean(value, axis=-1, keepdims=True)
    inverse = lax.rsqrt(jnp.mean(center * center, axis=-1, keepdims=True) + EPSILON)
    return center * inverse, inverse


def norm_back(d_normed, normed, inverse):
    first = jnp.mean(d_normed, axis=-1, keepdims=True)
    second = jnp.mean(d_normed * normed, axis=-1, keepdims=True)
    return inverse * (d_normed - first - normed * second)


def normal_cdf(value):
    return 0.5 * (1.0 + lax.erf(value * (1.0 / math.sqrt(2.0))))


def column_sum(value):
    return jnp.sum(value, axis=0, keepdims=True)


def head_halves(pair):
    first = lax.broadcasted_iota(jnp.int32, pair.shape, 1) < HEAD_DIM
    zero = jnp.zeros_like(pair)
    return jnp.where(first, pair, zero), jnp.where(first, zero, pair)


def attend_pair(queries, keys, values, length):
    tokens = queries.shape[0]
    values_t = values.T
    key_live = lax.broadcasted_iota(jnp.int32, (tokens, tokens), 0) < length
    contexts, log_totals = [], []
    for head, one in enumerate(head_halves(queries)):
        masked = jnp.where(key_live, nt(keys, one), MASKED)
        top = jnp.max(masked, axis=0, keepdims=True)
        expo = jnp.exp(masked - top)
        total = jnp.sum(expo, axis=0, keepdims=True)
        probs = (expo * (1.0 / total)).astype(BF16)
        contexts.append(nn(values_t[HEAD_DIM * head : HEAD_DIM * (head + 1)], probs))
        log_totals.append(top + jnp.log(total))
    return jnp.concatenate(contexts, axis=0).T, jnp.concatenate(log_totals, axis=0)


def attend_pair_back(queries, keys, values, t_queries, t_keys, log_totals, d_context, length):
    tokens = queries.shape[0]
    shape = (tokens, tokens)
    key_live = lax.broadcasted_iota(jnp.int32, shape, 0) < length
    pair_live = jnp.logical_and(key_live, lax.broadcasted_iota(jnp.int32, shape, 1) < length)
    keys_t = keys.T
    d_queries, d_keys, d_values = [], [], []
    heads = zip(head_halves(queries), head_halves(d_context), head_halves(t_queries))
    for head, (one, d_one, t_one) in enumerate(heads):
        scores = nt(keys, one)
        score_gap = scores - nt(t_keys, t_one)
        probs = jnp.exp(jnp.where(key_live, scores, MASKED) - log_totals[head : head + 1])
        d_probs = nt(values, d_one)
        weighted = probs * d_probs
        row_dot = jnp.sum(weighted, axis=0, keepdims=True)
        d_values.append(nn(probs.astype(BF16), d_one))
        extra = jnp.where(pair_live, score_gap, 0.0) * (1.0 / tokens)
        d_scores = (weighted - probs * row_dot + extra).astype(BF16)
        d_keys.append(nn(d_scores, one))
        d_queries.append(nn(keys_t[HEAD_DIM * head : HEAD_DIM * (head + 1)], d_scores))
    d_q = (jnp.concatenate(d_queries, axis=0).T * SCALE).astype(BF16)
    return d_q, (d_keys[0] + d_keys[1]).astype(BF16), (d_values[0] + d_values[1]).astype(BF16)


def pair_columns(base, pair):
    return pl.ds(pl.multiple_of(base + pair * PAIR, PAIR), PAIR)


def teacher_kernel(lengths, x_ref, w_qkv, w_out, w_up, w_down, tqk_ref, final_ref, values, context):
    length = lengths[pl.program_id(0)]
    x = x_ref[0]
    tqk_ref[0, :, :D] = (nn(x, w_qkv[:, :D]).astype(BF16).astype(F32) * SCALE).astype(BF16)
    tqk_ref[0, :, D:] = nn(x, w_qkv[:, D : 2 * D]).astype(BF16)
    values[...] = nn(x, w_qkv[:, 2 * D :]).astype(BF16)

    @pl.loop(0, PAIRS)
    def _(pair):
        queries, keys = tqk_ref[0, :, pair_columns(0, pair)], tqk_ref[0, :, pair_columns(D, pair)]
        mixed, _ = attend_pair(queries, keys, values[:, pair_columns(0, pair)], length)
        context[:, pair_columns(0, pair)] = mixed.astype(BF16)

    first, _ = normalize(x.astype(F32) + nn(context[...], w_out[...]))
    first_low = first.astype(BF16)
    total = first
    for c in range(CHUNKS):
        inner = nn(first_low, w_up[:, D * c : D * (c + 1)])
        total = total + nn((inner * normal_cdf(inner)).astype(BF16), w_down[D * c : D * (c + 1), :])
    final_ref[0] = normalize(total)[0]


def student_attend_kernel(lengths, clips, x_ref, w_qkv, bias_q, bias_v, qkv_ref, context_ref, log_ref):
    length = lengths[pl.program_id(0)]
    bound = clips[0]
    a_in = jnp.clip(x_ref[0].astype(F32), -bound, bound).astype(BF16)
    queries = (nn(a_in, w_qkv[:, :D]) + bias_q[...]).astype(BF16)
    qkv_ref[0, :, :D] = (queries.astype(F32) * SCALE).astype(BF16)
    qkv_ref[0, :, D : 2 * D] = nn(a_in, w_qkv[:, D : 2 * D]).astype(BF16)
    qkv_ref[0, :, 2 * D :] = (nn(a_in, w_qkv[:, 2 * D :]) + bias_v[...]).astype(BF16)

    @pl.loop(0, PAIRS)
    def _(pair):
        queries, keys, values = (qkv_ref[0, :, pair_columns(D * i, pair)] for i in range(3))
        mixed, log_totals = attend_pair(queries, keys, values, length)
        context_ref[0, :, pair_columns(0, pair)] = mixed
        log_ref[0, pair] = log_totals


(S_OUT, S_UP, S_DOWN, S_GAIN_ONE, S_SHIFT_ONE, S_GAIN_TWO, S_SHIFT_TWO, S_CLIP_ONE, S_CLIP_TWO, S_CLIP_THREE) = (
    0, 1, 5, 6, 7, 8, 9, 10, 11, 12,
)
S_ROWS = 16
(Q_QUERY, Q_VALUE, Q_CLIP) = (0, 1, 2)
Q_ROWS = 8
ABOVE, BELOW = 4.0, -4.0


def student_middle_kernel(
    lengths, clips, x_ref, cotangent_ref, final_ref, context_ref, w_out, w_up, w_down, vectors,
    mixed_ref, act_ref, d_pre_ref, up_in_ref, d_down_ref, cut_ref, d_attn_ref, d_res_ref, d_context_ref, sums_ref,
    slope,
):
    block = x_ref.shape[1]
    row, part = pl.program_id(0), pl.program_id(1)
    length = lengths[row] - part * block

    @pl.when(jnp.logical_and(row == 0, part == 0))
    def _():
        sums_ref[...] = jnp.zeros_like(sums_ref)

    def add(at, value):
        sums_ref[at : at + 1] += value

    def vector(at):
        return vectors[at : at + 1]

    cut = jnp.clip(context_ref[0], -clips[1], clips[1]).astype(BF16)
    cut_ref[0] = cut
    normed_one, inverse_one = normalize(x_ref[0].astype(F32) + nn(cut, w_out[...]) + vector(S_OUT))
    h_one = normed_one * vector(S_GAIN_ONE) + vector(S_SHIFT_ONE)
    up_in = jnp.clip(h_one, -clips[2], clips[2]).astype(BF16)
    up_in_ref[0] = up_in
    total = h_one + vector(S_DOWN)
    for c in range(CHUNKS):
        columns = slice(D * c, D * (c + 1))
        pre = nn(up_in, w_up[:, columns]) + vector(S_UP + c)
        cdf = normal_cdf(pre)
        value = pre * cdf
        rise = cdf + pre * jnp.exp(-0.5 * pre * pre) * (1.0 / math.sqrt(2.0 * math.pi))
        rise = jnp.where(value > clips[3], ABOVE, jnp.where(value < -clips[3], BELOW, rise))
        slope[:, columns] = rise
        act = jnp.clip(value, -clips[3], clips[3]).astype(BF16)
        act_ref[0, :, columns] = act
        total = total + nn(act, w_down[columns, :])
    normed_two, inverse_two = normalize(total)
    out = normed_two * vector(S_GAIN_TWO) + vector(S_SHIFT_TWO)
    mixed_ref[0] = out.astype(BF16)
    live = lax.broadcasted_iota(jnp.int32, (block, 1), 0) < length
    d_out = jnp.where(live, cotangent_ref[0].astype(F32) + out - final_ref[0], 0.0)
    add(S_GAIN_TWO, column_sum(d_out * normed_two))
    add(S_SHIFT_TWO, column_sum(d_out))
    d_res_two = norm_back(d_out * vector(S_GAIN_TWO), normed_two, inverse_two)
    d_down = d_res_two.astype(BF16)
    d_down_ref[0] = d_down
    add(S_DOWN, column_sum(d_down.astype(F32)))
    d_up_in = jnp.zeros((block, D), F32)
    for c in range(CHUNKS):
        columns = slice(D * c, D * (c + 1))
        d_act = nt(d_down, w_down[columns, :])
        rise = slope[:, columns]
        above, below = rise > 2.0, rise < -2.0
        d_pre = jnp.where(jnp.logical_or(above, below), 0.0, rise * d_act).astype(BF16)
        d_pre_ref[0, :, columns] = d_pre
        add(S_CLIP_THREE, column_sum(jnp.where(above, d_act, jnp.where(below, -d_act, 0.0))))
        add(S_UP + c, column_sum(d_pre.astype(F32)))
        d_up_in = d_up_in + nt(d_pre, w_up[:, columns])
    above, below = h_one > clips[2], h_one < -clips[2]
    add(S_CLIP_TWO, column_sum(jnp.where(above, d_up_in, jnp.where(below, -d_up_in, 0.0))))
    d_h_one = d_res_two + jnp.where(jnp.abs(h_one) < clips[2], d_up_in, 0.0)
    add(S_GAIN_ONE, column_sum(d_h_one * normed_one))
    add(S_SHIFT_ONE, column_sum(d_h_one))
    d_res_one = norm_back(d_h_one * vector(S_GAIN_ONE), normed_one, inverse_one)
    d_res_ref[0] = d_res_one
    d_attn = d_res_one.astype(BF16)
    d_attn_ref[0] = d_attn
    add(S_OUT, column_sum(d_attn.astype(F32)))
    d_cut = nt(d_attn, w_out[...])
    context = context_ref[0]
    above, below = context > clips[1], context < -clips[1]
    add(S_CLIP_ONE, column_sum(jnp.where(above, d_cut, jnp.where(below, -d_cut, 0.0))))
    d_context_ref[0] = jnp.where(jnp.abs(context) < clips[1], d_cut, 0.0).astype(BF16)


def weight_grads_kernel(act, d_down, up_in, d_pre, cut, d_attn, g_down, g_up, g_out):
    g_down[...] = tn(act[...], d_down[...]).astype(BF16)
    g_up[...] = tn(up_in[...], d_pre[...]).astype(BF16)

    @pl.when(pl.program_id(0) == 0)
    def _():
        g_out[...] = tn(cut[...], d_attn[...]).astype(BF16)


def student_back_kernel(
    lengths, clips, x_ref, qkv_ref, tqk_ref, log_ref, d_context_ref, d_res_ref, w_qkv,
    input_ref, g_qkv, sums_ref, a_in, d_joined,
):
    row = pl.program_id(0)
    tokens = x_ref.shape[1]
    length = lengths[row]
    here = pl.ds(pl.multiple_of(row * tokens, tokens), tokens)

    @pl.when(row == 0)
    def _():
        sums_ref[...] = jnp.zeros_like(sums_ref)

    @pl.loop(0, PAIRS)
    def _(pair):
        queries, keys, values = (qkv_ref[0, :, pair_columns(D * i, pair)] for i in range(3))
        t_queries, t_keys = (tqk_ref[0, :, pair_columns(D * i, pair)] for i in range(2))
        d_context = d_context_ref[0, :, pair_columns(0, pair)]
        grads = attend_pair_back(queries, keys, values, t_queries, t_keys, log_ref[0, pair], d_context, length)
        for i in range(3):
            d_joined[here, pair_columns(D * i, pair)] = grads[i]

    bound = clips[0]
    x = x_ref[0].astype(F32)
    a_in[here, :] = jnp.clip(x, -bound, bound).astype(BF16)
    sums_ref[Q_QUERY : Q_QUERY + 1] += column_sum(d_joined[here, :D].astype(F32))
    sums_ref[Q_VALUE : Q_VALUE + 1] += column_sum(d_joined[here, 2 * D :].astype(F32))
    d_a = nt(d_joined[here, :], w_qkv[...])
    inside = jnp.where(jnp.abs(x) < bound, 1.0, jnp.where(jnp.abs(x) == bound, 0.5, 0.0))
    input_ref[0] = (d_res_ref[0] + d_a * inside).astype(BF16)
    outside = (1.0 - inside) * d_a
    sums_ref[Q_CLIP : Q_CLIP + 1] += column_sum(jnp.where(x > 0, outside, -outside))

    @pl.when(row == pl.num_programs(0) - 1)
    def _():
        for i in range(3):
            g_qkv[:, D * i : D * (i + 1)] = tn(a_in[...], d_joined[:, D * i : D * (i + 1)]).astype(BF16)


def rows_spec(tokens, width):
    return pl.BlockSpec((1, tokens, width), lambda r, *_: (r, 0, 0))


def whole_spec(shape):
    return pl.BlockSpec(shape, lambda *_: (0,) * len(shape), pipeline_mode=pl.Buffered(1))


def smem_spec():
    return pl.BlockSpec(memory_space=pltpu.SMEM)


def params(**more):
    return pltpu.CompilerParams(vmem_limit_bytes=VMEM_LIMIT, **more)


def shaped(shape, dtype):
    return jax.ShapeDtypeStruct(shape, dtype)


def teacher_pass(lengths, x, w_qkv, w_out, w_up, w_down):
    rows, tokens, _ = x.shape
    return pl.pallas_call(
        teacher_kernel,
        grid=(rows,),
        in_specs=[smem_spec(), rows_spec(tokens, D)] + [whole_spec(w.shape) for w in (w_qkv, w_out, w_up, w_down)],
        out_specs=[rows_spec(tokens, 2 * D), rows_spec(tokens, D)],
        out_shape=[shaped((rows, tokens, 2 * D), BF16), shaped((rows, tokens, D), F32)],
        scratch_shapes=[pltpu.VMEM((tokens, D), BF16)] * 2,
        compiler_params=params(),
    )(lengths, x, w_qkv, w_out, w_up, w_down)


def student_attend(lengths, clips, x, w_qkv, bias_q, bias_v):
    rows, tokens, _ = x.shape
    logs = (1, PAIRS, 2, tokens)
    return pl.pallas_call(
        student_attend_kernel,
        grid=(rows,),
        in_specs=[smem_spec(), smem_spec(), rows_spec(tokens, D), whole_spec(w_qkv.shape)] + [whole_spec((1, D))] * 2,
        out_specs=[
            rows_spec(tokens, 3 * D),
            rows_spec(tokens, D),
            pl.BlockSpec(logs, lambda r: (r, 0, 0, 0)),
        ],
        out_shape=[
            shaped((rows, tokens, 3 * D), BF16),
            shaped((rows, tokens, D), F32),
            shaped((rows,) + logs[1:], F32),
        ],
        compiler_params=params(),
    )(lengths, clips, x, w_qkv, bias_q.reshape(1, D), bias_v.reshape(1, D))


def student_middle(lengths, clips, x, cotangent, final, context, w_out, w_up, w_down, vectors):
    rows, tokens, _ = x.shape
    block = tokens // 2 if tokens % 32 == 0 else tokens
    wide = {"act": FF, "d_pre": FF}
    names = ("mixed", "act", "d_pre", "up_in", "d_down", "cut", "d_attn", "d_res", "d_context")

    def spec(width):
        return pl.BlockSpec((1, block, width), lambda r, i: (r, i, 0))

    return pl.pallas_call(
        student_middle_kernel,
        grid=(rows, tokens // block),
        in_specs=[smem_spec(), smem_spec()]
        + [spec(D)] * 4
        + [whole_spec(w.shape) for w in (w_out, w_up, w_down, vectors)],
        out_specs=[spec(wide.get(name, D)) for name in names] + [whole_spec((S_ROWS, D))],
        out_shape=[
            shaped((rows, tokens, wide.get(name, D)), F32 if name == "d_res" else BF16) for name in names
        ]
        + [shaped((S_ROWS, D), F32)],
        scratch_shapes=[pltpu.VMEM((block, FF), F32)],
        compiler_params=params(),
    )(lengths, clips, x, cotangent, final, context, w_out, w_up, w_down, vectors)


def weight_grads(act, d_down, up_in, d_pre, cut, d_attn):
    flat = [v.reshape(-1, v.shape[-1]) for v in (act, d_down, up_in, d_pre, cut, d_attn)]
    tokens = flat[0].shape[0]
    chunk = pl.BlockSpec((tokens, D), lambda c: (0, c))
    same = whole_spec((tokens, D))
    return pl.pallas_call(
        weight_grads_kernel,
        grid=(CHUNKS,),
        in_specs=[chunk, same, same, chunk, same, same],
        out_specs=[
            pl.BlockSpec((D, D), lambda c: (c, 0)),
            pl.BlockSpec((D, D), lambda c: (0, c)),
            whole_spec((D, D)),
        ],
        out_shape=[shaped((FF, D), BF16), shaped((D, FF), BF16), shaped((D, D), BF16)],
        compiler_params=params(),
    )(*flat)


def student_back(lengths, clips, x, qkv, tqk, logs, d_context, d_res, w_qkv):
    rows, tokens, _ = x.shape
    return pl.pallas_call(
        student_back_kernel,
        grid=(rows,),
        in_specs=[smem_spec(), smem_spec(), rows_spec(tokens, D), rows_spec(tokens, 3 * D), rows_spec(tokens, 2 * D)]
        + [pl.BlockSpec((1,) + logs.shape[1:], lambda r: (r, 0, 0, 0))]
        + [rows_spec(tokens, D), rows_spec(tokens, D), whole_spec(w_qkv.shape)],
        out_specs=[rows_spec(tokens, D), whole_spec((D, 3 * D)), whole_spec((Q_ROWS, D))],
        out_shape=[shaped((rows, tokens, D), BF16), shaped((D, 3 * D), BF16), shaped((Q_ROWS, D), F32)],
        scratch_shapes=[pltpu.VMEM((rows * tokens, D), BF16), pltpu.VMEM((rows * tokens, 3 * D), BF16)],
        compiler_params=params(),
    )(lengths, clips, x, qkv, tqk, logs, d_context, d_res, w_qkv)


PLANES, COLUMNS, CORES = 4, 4, 2
DEVICES = PLANES * COLUMNS * CORES


class Place:
    def __init__(self):
        self.me = lax.axis_index("shard")
        self.core = self.me % 2
        self.x = (self.me // 2) % 2
        self.y = (self.me // 4) % 2
        self.z = self.me // 8
        self.column = (self.me // 2) % 4
        self.along_x = self.me + 2 - 4 * self.x
        self.along_y = self.me + 4 - 8 * self.y
        self.sibling = self.me + 1 - 2 * self.core
        self.along_a = self.along_x + (self.along_y - self.along_x) * self.core
        self.along_b = self.along_y + (self.along_x - self.along_y) * self.core

    def plane(self, step):
        return (self.me + 8 * step) % DEVICES

    def meet(self):
        partners = [self.sibling, self.along_x, self.along_y] + [self.plane(k) for k in range(1, PLANES)]
        barrier = pltpu.get_barrier_semaphore()
        for partner in partners:
            pl.semaphore_signal(barrier, inc=1, device_id=(partner,), device_id_type=MESH)
        pl.semaphore_wait(barrier, len(partners))


class Trip:
    SEMAPHORES = 12

    def __init__(self, place, source, out, send, receive):
        self.place, self.source, self.out, self.send, self.receive = place, source, out, send, receive
        self.mine = place.me % 8
        self.at_a = self.mine + place.along_a - place.me
        self.at_b = self.mine + place.along_b - place.me
        self.at_ab = self.at_a + self.at_b - self.mine

    def remote(self, source, target, slot, device):
        return pltpu.make_async_remote_copy(
            src_ref=source, dst_ref=target, send_sem=self.send.at[slot], recv_sem=self.receive.at[slot],
            device_id=(device,), device_id_type=MESH,
        )

    def own(self):
        return pltpu.make_async_copy(self.source, self.out.at[self.place.z, self.mine], self.send.at[0])

    def line(self, step):
        target = self.out.at[self.place.z, self.mine]
        return self.remote(self.source, target, step, self.place.plane(step))

    def line_from(self, step):
        target = self.out.at[(self.place.z + PLANES - step) % PLANES, self.mine]
        return self.remote(self.source, target, step, self.place.plane(step))

    def slab(self, column, slot, device):
        part = self.out.at[:, column]
        return self.remote(part, part, slot, device)

    def first(self):
        self.own().start()
        for step in range(1, PLANES):
            self.line(step).start()

    def second(self):
        place = self.place
        self.own().wait()
        for step in range(1, PLANES):
            self.line_from(step).wait_recv()
        self.slab(self.mine, 4, place.along_a).start()
        self.slab(self.mine, 5, place.along_b).start()
        self.slab(self.mine, 7, place.sibling).start()

    def third(self):
        place = self.place
        self.slab(self.at_a, 4, place.along_a).wait_recv()
        self.slab(self.at_a, 6, place.along_b).start()
        self.slab(self.at_a, 8, place.sibling).start()

    def fourth(self):
        place = self.place
        self.slab(self.at_b, 5, place.along_b).wait_recv()
        self.slab(self.at_b, 9, place.sibling).start()
        self.slab(self.at_ab, 6, place.along_b).wait_recv()
        self.slab(self.at_ab, 10, place.sibling).start()

    def fifth(self):
        for slot in range(7, 11):
            self.slab(self.mine, slot, self.place.sibling).wait_recv()

    def last(self):
        for step in range(1, PLANES):
            self.line(step).wait_send()
        for slot in range(4, 11):
            self.slab(self.mine, slot, self.place.sibling).wait_send()


def gather_kernel(*refs):
    teach, latent, outs, low = refs[:4], refs[4:8], refs[8:16], refs[16:20]
    send, receive = refs[20:]
    place = Place()
    place.meet()
    sources = list(teach) + list(low)
    trips = [Trip(place, source, outs[i], send.at[i], receive.at[i]) for i, source in enumerate(sources)]
    order = trips
    steps = [[t.first, t.second, t.third, t.fourth, t.fifth] for t in order]
    depth = len(steps[0])
    for tick in range(len(order) + depth - 1):
        for phase in reversed(range(depth)):
            if 0 <= tick - phase < len(order):
                steps[tick - phase][phase]()
        if tick == 0:
            for i in range(4):
                low[i][...] = signed_mean(latent[i][...])
    for trip in trips:
        trip.last()


def gather_weights(teach, latent):
    shapes = [(PLANES, 8) + w.shape for w in teach] * 2
    outs = pl.pallas_call(
        gather_kernel,
        in_specs=[pl.BlockSpec(memory_space=pl.ANY)] * 4 + [pl.BlockSpec(memory_space=pltpu.VMEM)] * 4,
        out_specs=[pl.BlockSpec(memory_space=pl.ANY)] * 8,
        out_shape=[shaped(shape, BF16) for shape in shapes],
        scratch_shapes=[pltpu.VMEM(w.shape, BF16) for w in latent]
        + [pltpu.SemaphoreType.DMA((8, Trip.SEMAPHORES))] * 2,
        compiler_params=params(collective_id=0, has_side_effects=True),
    )(*teach, *latent)
    whole = [out.reshape(-1, out.shape[-1]) for out in outs]
    return whole[:4], whole[4:]


class Fold:
    SEMAPHORES = 8

    def __init__(self, place, grad, out, own, from_core, to_p, from_p, to_q, from_q, to_z, from_z, send, receive):
        self.place, self.grad, self.out = place, grad, out
        self.own, self.from_core = own, from_core
        self.to_p, self.from_p, self.to_q, self.from_q = to_p, from_p, to_q, from_q
        self.to_z, self.from_z = to_z, from_z
        self.send, self.receive = send, receive
        core = place.core
        self.p_stride, self.q_stride = 1 + core, 2 - core
        self.p = place.x + (place.y - place.x) * core
        self.q = place.y + (place.x - place.y) * core

    def remote(self, source, target, slot, device):
        return pltpu.make_async_remote_copy(
            src_ref=source, dst_ref=target, send_sem=self.send.at[slot], recv_sem=self.receive.at[slot],
            device_id=(device,), device_id_type=MESH,
        )

    def column(self, p, q):
        return p * self.p_stride + q * self.q_stride

    def keep(self):
        return pltpu.make_async_copy(self.grad.at[:, :, self.place.core], self.own, self.send.at[0])

    def over_core(self):
        return self.remote(self.grad.at[:, :, 1 - self.place.core], self.from_core, 1, self.place.sibling)

    def over_p(self):
        return self.remote(self.to_p, self.from_p, 2, self.place.along_a)

    def over_q(self):
        return self.remote(self.to_q, self.from_q, 3, self.place.along_b)

    def over_z(self, step):
        return self.remote(self.to_z.at[step - 1], self.from_z.at[step - 1], 3 + step, self.place.plane(step))

    def pair_sum(self, z, column):
        return self.own[z, column].astype(F32) + self.from_core[z, column].astype(F32)

    def first(self):
        self.keep().start()
        self.over_core().start()

    def second(self):
        self.keep().wait()
        self.over_core().wait_recv()

        @pl.loop(0, 2 * PLANES)
        def _(i):
            z, q = i // 2, i % 2
            self.to_p[z, q] = self.pair_sum(z, self.column(1 - self.p, q)).astype(BF16)

        self.over_p().start()

    def third(self):
        self.over_p().wait_recv()

        @pl.loop(0, PLANES)
        def _(z):
            q = 1 - self.q
            total = self.pair_sum(z, self.column(self.p, q)) + self.from_p[z, q].astype(F32)
            self.to_q[z] = total.astype(BF16)

        self.over_q().start()

    def quad_sum(self, z):
        q = self.q
        total = self.pair_sum(z, self.column(self.p, q)) + self.from_p[z, q].astype(F32)
        return total + self.from_q[z].astype(F32)

    def fourth(self):
        self.over_q().wait_recv()
        for step in range(1, PLANES):
            self.to_z[step - 1] = self.quad_sum((self.place.z + step) % PLANES).astype(BF16)
            self.over_z(step).start()

    def fifth(self):
        total = self.quad_sum(self.place.z)
        for step in range(1, PLANES):
            self.over_z(step).wait_recv()
            total = total + self.from_z[step - 1].astype(F32)
        self.out[...] = total

    def last(self):
        self.over_core().wait_send()
        self.over_p().wait_send()
        self.over_q().wait_send()
        for step in range(1, PLANES):
            self.over_z(step).wait_send()


FOLD_BUFFERS = ((4, 4), (4, 4), (4, 2), (4, 2), (4,), (4,), (3,), (3,))


class Share:
    SEMAPHORES = 7

    def __init__(self, place, value, out, partial, received, send, receive):
        self.place, self.value, self.out = place, value, out
        self.partial, self.received, self.send, self.receive = partial, received, send, receive

    def swap(self, slot, device):
        return pltpu.make_async_remote_copy(
            src_ref=self.partial.at[min(slot, 3)], dst_ref=self.received.at[slot], send_sem=self.send.at[slot],
            recv_sem=self.receive.at[slot], device_id=(device,), device_id_type=MESH,
        )

    def partners(self):
        place = self.place
        return [place.sibling, place.along_x, place.along_y] + [place.plane(k) for k in range(1, PLANES)]

    def first(self):
        self.partial[0] = self.value[...]
        self.swap(0, self.place.sibling).start()

    def step(self, at):
        partners = self.partners()
        self.swap(at, partners[at]).wait_recv()
        self.partial[at + 1] = self.partial[at] + self.received[at]
        for slot in (at + 1,) if at < 2 else (3, 4, 5):
            self.swap(slot, partners[slot]).start()

    def finish(self):
        partners = self.partners()
        for slot in (3, 4, 5):
            self.swap(slot, partners[slot]).wait_recv()
        place = self.place
        self.received[6] = self.partial[3]
        total = jnp.zeros_like(self.value)
        for z in range(PLANES):
            behind = (place.z + PLANES - z) % PLANES
            total = total + self.received[(behind + 3) % PLANES + 3]
        self.out[...] = total
        for slot in range(6):
            self.swap(slot, partners[slot]).wait_send()


def reduce_kernel(*refs):
    grads, small = refs[:4], refs[4]
    outs, small_out = refs[5:9], refs[9]
    scratch = refs[10:]
    buffers, (partial, received, send, receive) = scratch[:-4], scratch[-4:]
    place = Place()
    place.meet()
    per = len(FOLD_BUFFERS)
    folds = [
        Fold(place, grads[i], outs[i], *buffers[per * i : per * (i + 1)], send.at[i], receive.at[i]) for i in range(4)
    ]
    share = Share(place, small, small_out, partial, received, send.at[4], receive.at[4])
    steps = [[f.first, f.second, f.third, f.fourth, f.fifth] for f in folds]
    extra = [share.first] + [functools.partial(share.step, at) for at in range(3)] + [share.finish]
    depth = len(steps[0])
    for tick in range(len(folds) + depth - 1):
        for phase in reversed(range(depth)):
            if 0 <= tick - phase < len(folds):
                steps[tick - phase][phase]()
        if tick < len(extra):
            extra[tick]()
    for fold in folds:
        fold.last()


def reduce_grads(grads, small):
    rows = [g.shape[0] // DEVICES for g in grads]
    split = [g.reshape(PLANES, COLUMNS, CORES, n, g.shape[-1]) for g, n in zip(grads, rows)]
    shapes = [(n, g.shape[-1]) for g, n in zip(grads, rows)]
    vmem = pl.BlockSpec(memory_space=pltpu.VMEM)
    return pl.pallas_call(
        reduce_kernel,
        in_specs=[pl.BlockSpec(memory_space=pl.ANY)] * 4 + [vmem],
        out_specs=[vmem] * 5,
        out_shape=[shaped(s, F32) for s in shapes] + [shaped(small.shape, F32)],
        scratch_shapes=[pltpu.VMEM(lead + s, BF16) for s in shapes for lead in FOLD_BUFFERS]
        + [pltpu.VMEM((4,) + small.shape, F32), pltpu.VMEM((7,) + small.shape, F32)]
        + [pltpu.SemaphoreType.DMA((5, Fold.SEMAPHORES))] * 2,
        compiler_params=params(collective_id=1, has_side_effects=True),
    )(*split, small)


def on_device(
    by_kernel,
    hidden, teacher_input, cotangent, lengths, lat_qkv, lat_out, lat_up, lat_down,
    bias_q, bias_v, bias_out, bias_up, bias_down, gain_one, shift_one, gain_two, shift_two, clips,
    teach_qkv, teach_out, teach_up, teach_down,
):
    latent = (lat_qkv, lat_out, lat_up, lat_down)
    teach = (teach_qkv, teach_out, teach_up, teach_down)
    if by_kernel:
        teach, (w_qkv, w_out, w_up, w_down) = gather_weights(teach, latent)
    else:
        gather = functools.partial(lax.all_gather, axis_name="shard", axis=0, tiled=True)
        teach = [gather(w) for w in teach]
        w_qkv, w_out, w_up, w_down = (gather(signed_mean(w)) for w in latent)
    tqk, final = teacher_pass(lengths, teacher_input, *teach)
    qkv, context, logs = student_attend(lengths, clips, hidden, w_qkv, bias_q, bias_v)
    vectors = jnp.concatenate(
        [
            bias_out.reshape(1, D), bias_up.reshape(CHUNKS, D), bias_down.reshape(1, D), gain_one.reshape(1, D),
            shift_one.reshape(1, D), gain_two.reshape(1, D), shift_two.reshape(1, D), jnp.zeros((S_ROWS - 10, D), F32),
        ]
    )
    mixed, act, d_pre, up_in, d_down, cut, d_attn, d_res, d_context, sums = student_middle(
        lengths, clips, hidden, cotangent, final, context, w_out, w_up, w_down, vectors
    )
    g_down, g_up, g_out = weight_grads(act, d_down, up_in, d_pre, cut, d_attn)
    input_grad, g_qkv, q_sums = student_back(lengths, clips, hidden, qkv, tqk, logs, d_context, d_res, w_qkv)
    small = jnp.concatenate([sums, q_sums])
    if by_kernel:
        g_down, g_up, g_qkv, g_out, small = reduce_grads((g_down, g_up, g_qkv, g_out), small)
    else:
        scatter = functools.partial(lax.psum_scatter, axis_name="shard", scatter_dimension=0, tiled=True)
        g_down, g_up, g_qkv, g_out = (scatter(g.astype(F32)) for g in (g_down, g_up, g_qkv, g_out))
        small = lax.psum(small, "shard")
    g_clips = jnp.stack([jnp.sum(small[at]) for at in (S_ROWS + Q_CLIP, S_CLIP_ONE, S_CLIP_TWO, S_CLIP_THREE)])
    return (
        mixed, input_grad, g_qkv, g_out, g_up, g_down,
        small[S_ROWS + Q_QUERY], small[S_ROWS + Q_VALUE], small[S_OUT], small[S_UP : S_UP + CHUNKS].reshape(FF),
        small[S_DOWN], small[S_GAIN_ONE], small[S_SHIFT_ONE], small[S_GAIN_TWO], small[S_SHIFT_TWO], g_clips,
    )


def solution(mesh):
    split, rows, same = P("shard", None), P("shard", None, None), P()
    return jax.shard_map(
        functools.partial(on_device, mesh.shape["shard"] == DEVICES),
        mesh=mesh,
        in_specs=(rows, rows, rows, P("shard")) + (split,) * 4 + (same,) * 10 + (split,) * 4,
        out_specs=(rows, rows) + (split,) * 4 + (same,) * 10,
        check_vma=False,
    )
```

```python
import functools
import math

import jax
import jax.numpy as jnp
from jax import lax
from jax.experimental import pallas as pl
from jax.experimental.pallas import tpu as pltpu
from jax.sharding import PartitionSpec as P

D = 768
FF = 3072
HEAD_DIM = 64
PAIR = 2 * HEAD_DIM
PAIRS = D // PAIR
DOUBLE, TRIPLE = 2 * PAIR, 3 * PAIR
CHUNKS = FF // D

EPSILON = 1e-05
MASKED = -1000000000.0
SCALE = 1.0 / math.sqrt(HEAD_DIM)

F32 = jnp.float32
BF16 = jnp.bfloat16
MESH = pl.DeviceIdType.MESH
VMEM_LIMIT = 63 * 1024 * 1024


def nn(left, right):
    return lax.dot_general(left, right, (((1,), (0,)), ((), ())), preferred_element_type=F32)


def nt(left, right):
    return lax.dot_general(left, right, (((1,), (1,)), ((), ())), preferred_element_type=F32)


def tn(left, right):
    return lax.dot_general(left, right, (((0,), (0,)), ((), ())), preferred_element_type=F32)


def signed_mean(latent):
    factor = jnp.mean(jnp.abs(latent), axis=1, keepdims=True)
    sign = jnp.where(latent > 0, 1.0, jnp.where(latent < 0, -1.0, 0.0))
    return (factor * sign).astype(BF16)


def normalize(value):
    center = value - jnp.mean(value, axis=-1, keepdims=True)
    inverse = lax.rsqrt(jnp.mean(center * center, axis=-1, keepdims=True) + EPSILON)
    return center * inverse, inverse


def norm_back(d_normed, normed, inverse):
    first = jnp.mean(d_normed, axis=-1, keepdims=True)
    second = jnp.mean(d_normed * normed, axis=-1, keepdims=True)
    return inverse * (d_normed - first - normed * second)


def normal_cdf(value):
    return 0.5 * (1.0 + lax.erf(value * (1.0 / math.sqrt(2.0))))


def column_sum(value):
    return jnp.sum(value, axis=0, keepdims=True)


def head_halves(pair):
    first = lax.broadcasted_iota(jnp.int32, pair.shape, 1) < HEAD_DIM
    zero = jnp.zeros_like(pair)
    return jnp.where(first, pair, zero), jnp.where(first, zero, pair)


def attend_pair(queries, keys, values, length):
    tokens = queries.shape[0]
    values_t = values.T
    key_live = lax.broadcasted_iota(jnp.int32, (tokens, tokens), 0) < length
    contexts, log_totals = [], []
    for head, one in enumerate(head_halves(queries)):
        masked = jnp.where(key_live, nt(keys, one), MASKED)
        top = jnp.max(masked, axis=0, keepdims=True)
        expo = jnp.exp(masked - top)
        total = jnp.sum(expo, axis=0, keepdims=True)
        probs = (expo * (1.0 / total)).astype(BF16)
        contexts.append(nn(values_t[HEAD_DIM * head : HEAD_DIM * (head + 1)], probs))
        log_totals.append(top + jnp.log(total))
    return jnp.concatenate(contexts, axis=0).T, jnp.concatenate(log_totals, axis=0)


def attend_pair_back(queries, keys, values, t_queries, t_keys, log_totals, row_dots, d_context, length):
    tokens = queries.shape[0]
    shape = (tokens, tokens)
    key_live = lax.broadcasted_iota(jnp.int32, shape, 0) < length
    pair_live = jnp.logical_and(key_live, lax.broadcasted_iota(jnp.int32, shape, 1) < length)
    keys_t = keys.T
    d_queries, d_keys, d_values = [], [], []
    heads = zip(head_halves(queries), head_halves(d_context), head_halves(t_queries))
    for head, (one, d_one, t_one) in enumerate(heads):
        scores = nt(keys, one)
        score_gap = scores - nt(t_keys, t_one)
        probs = jnp.exp(jnp.where(key_live, scores, MASKED) - log_totals[head : head + 1])
        d_probs = nt(values, d_one)
        d_values.append(nn(probs.astype(BF16), d_one))
        extra = jnp.where(pair_live, score_gap, 0.0) * (1.0 / tokens)
        d_scores = (probs * (d_probs - row_dots[head : head + 1]) + extra).astype(BF16)
        d_keys.append(nn(d_scores, one))
        d_queries.append(nn(keys_t[HEAD_DIM * head : HEAD_DIM * (head + 1)], d_scores))
    d_q = (jnp.concatenate(d_queries, axis=0).T * SCALE).astype(BF16)
    return d_q, (d_keys[0] + d_keys[1]).astype(BF16), (d_values[0] + d_values[1]).astype(BF16)


def pair_columns(pair, width=PAIR):
    return pl.ds(pl.multiple_of(pair * width, PAIR), width)


def by_pairs(matrix):
    split = matrix.reshape(matrix.shape[0], 3, PAIRS, PAIR)
    return split.transpose(0, 2, 1, 3).reshape(matrix.shape[0], 3 * D)


def by_kinds(matrix):
    split = matrix.reshape(matrix.shape[0], PAIRS, 3, PAIR)
    return split.transpose(0, 2, 1, 3).reshape(matrix.shape[0], 3 * D)


def teacher_pair(pair, x, length, w_qkv, tqk_ref, context_ref):
    joined = nn(x, w_qkv[:, pair_columns(pair, TRIPLE)]).astype(BF16)
    queries, keys, values = (joined[:, PAIR * i : PAIR * (i + 1)] for i in range(3))
    queries = (queries.astype(F32) * SCALE).astype(BF16)
    tqk_ref[:, pair_columns(pair, DOUBLE)] = jnp.concatenate([queries, keys], axis=1)
    mixed, _ = attend_pair(queries, keys, values, length)
    context_ref[:, pair_columns(pair)] = mixed.astype(BF16)


def teacher_last(x, context, w_out, w_up, w_down, between):
    first, _ = normalize(x.astype(F32) + nn(context, w_out[...]))
    first_low = first.astype(BF16)
    total = first
    for c in range(CHUNKS):
        between(c)
        inner = nn(first_low, w_up[:, D * c : D * (c + 1)])
        total = total + nn((inner * normal_cdf(inner)).astype(BF16), w_down[D * c : D * (c + 1), :])
    return normalize(total)[0]


def student_pair(pair, a_in, length, w_qkv, bias_q, bias_v, qkv_ref, context_ref, log_ref):
    joined = nn(a_in, w_qkv[:, pair_columns(pair, TRIPLE)])
    queries = (joined[:, :PAIR] + bias_q[:, pair_columns(pair)]).astype(BF16)
    queries = (queries.astype(F32) * SCALE).astype(BF16)
    keys = joined[:, PAIR:DOUBLE].astype(BF16)
    values = (joined[:, DOUBLE:] + bias_v[:, pair_columns(pair)]).astype(BF16)
    qkv_ref[:, pair_columns(pair, TRIPLE)] = jnp.concatenate([queries, keys, values], axis=1)
    mixed, log_totals = attend_pair(queries, keys, values, length)
    context_ref[:, pair_columns(pair)] = mixed
    log_ref[pair] = log_totals


def teacher_kernel(lengths, x_ref, w_qkv, w_out, w_up, w_down, tqk_ref, final_ref, context):
    length = lengths[pl.program_id(0)]

    @pl.loop(0, PAIRS)
    def _(pair):
        teacher_pair(pair, x_ref[0], length, w_qkv, tqk_ref.at[0], context)

    final_ref[0] = teacher_last(x_ref[0], context[...], w_out, w_up, w_down, lambda c: None)


def student_attend_kernel(lengths, clips, x_ref, w_qkv, bias_q, bias_v, qkv_ref, context_ref, log_ref, a_in):
    length = lengths[pl.program_id(0)]
    a_in[...] = jnp.clip(x_ref[0].astype(F32), -clips[0], clips[0]).astype(BF16)

    @pl.loop(0, PAIRS)
    def _(pair):
        student_pair(
            pair, a_in[...], length, w_qkv, bias_q, bias_v, qkv_ref.at[0], context_ref.at[0], log_ref.at[0]
        )


(S_OUT, S_UP, S_DOWN, S_GAIN_ONE, S_SHIFT_ONE, S_GAIN_TWO, S_SHIFT_TWO, S_CLIP_ONE, S_CLIP_TWO, S_CLIP_THREE) = (
    0, 1, 5, 6, 7, 8, 9, 10, 11, 12,
)
S_ROWS = 16
(Q_QUERY, Q_VALUE, Q_CLIP) = (0, 1, 2)
Q_ROWS = 8
ABOVE, BELOW = 4.0, -4.0


def student_middle_kernel(
    lengths, clips, x_ref, cotangent_ref, final_ref, context_ref, w_out, w_up, w_down,
    bias_out, bias_up, bias_down, gain_one, shift_one, gain_two, shift_two,
    mixed_ref, act_ref, d_pre_ref, up_in_ref, d_down_ref, cut_ref, d_attn_ref, d_res_ref, d_context_ref, dots_ref,
    sums_ref, slope,
):
    block = x_ref.shape[1]
    row, part = pl.program_id(0), pl.program_id(1)
    length = lengths[row] - part * block

    @pl.when(jnp.logical_and(row == 0, part == 0))
    def _():
        sums_ref[...] = jnp.zeros_like(sums_ref)

    def add(at, value):
        sums_ref[at : at + 1] += value

    def vector(ref):
        return ref[...].reshape(1, ref.shape[0])

    cut = jnp.clip(context_ref[0], -clips[1], clips[1]).astype(BF16)
    cut_ref[0] = cut
    normed_one, inverse_one = normalize(x_ref[0].astype(F32) + nn(cut, w_out[...]) + vector(bias_out))
    h_one = normed_one * vector(gain_one) + vector(shift_one)
    up_in = jnp.clip(h_one, -clips[2], clips[2]).astype(BF16)
    up_in_ref[0] = up_in
    total = h_one + vector(bias_down)
    for c in range(CHUNKS):
        columns = slice(D * c, D * (c + 1))
        pre = nn(up_in, w_up[:, columns]) + vector(bias_up)[:, columns]
        cdf = normal_cdf(pre)
        value = pre * cdf
        rise = cdf + pre * jnp.exp(-0.5 * pre * pre) * (1.0 / math.sqrt(2.0 * math.pi))
        rise = jnp.where(value > clips[3], ABOVE, jnp.where(value < -clips[3], BELOW, rise))
        slope[:, columns] = rise
        act = jnp.clip(value, -clips[3], clips[3]).astype(BF16)
        act_ref[0, :, columns] = act
        total = total + nn(act, w_down[columns, :])
    normed_two, inverse_two = normalize(total)
    out = normed_two * vector(gain_two) + vector(shift_two)
    mixed_ref[0] = out.astype(BF16)
    live = lax.broadcasted_iota(jnp.int32, (block, 1), 0) < length
    d_out = jnp.where(live, cotangent_ref[0].astype(F32) + out - final_ref[0], 0.0)
    add(S_GAIN_TWO, column_sum(d_out * normed_two))
    add(S_SHIFT_TWO, column_sum(d_out))
    d_res_two = norm_back(d_out * vector(gain_two), normed_two, inverse_two)
    d_down = d_res_two.astype(BF16)
    d_down_ref[0] = d_down
    add(S_DOWN, column_sum(d_down.astype(F32)))
    d_up_in = jnp.zeros((block, D), F32)
    for c in range(CHUNKS):
        columns = slice(D * c, D * (c + 1))
        d_act = nt(d_down, w_down[columns, :])
        rise = slope[:, columns]
        above, below = rise > 2.0, rise < -2.0
        d_pre = jnp.where(jnp.logical_or(above, below), 0.0, rise * d_act).astype(BF16)
        d_pre_ref[0, :, columns] = d_pre
        add(S_CLIP_THREE, column_sum(jnp.where(above, d_act, jnp.where(below, -d_act, 0.0))))
        add(S_UP + c, column_sum(d_pre.astype(F32)))
        d_up_in = d_up_in + nt(d_pre, w_up[:, columns])
    above, below = h_one > clips[2], h_one < -clips[2]
    add(S_CLIP_TWO, column_sum(jnp.where(above, d_up_in, jnp.where(below, -d_up_in, 0.0))))
    d_h_one = d_res_two + jnp.where(jnp.abs(h_one) < clips[2], d_up_in, 0.0)
    add(S_GAIN_ONE, column_sum(d_h_one * normed_one))
    add(S_SHIFT_ONE, column_sum(d_h_one))
    d_res_one = norm_back(d_h_one * vector(gain_one), normed_one, inverse_one)
    d_res_ref[0] = d_res_one
    d_attn = d_res_one.astype(BF16)
    d_attn_ref[0] = d_attn
    add(S_OUT, column_sum(d_attn.astype(F32)))
    d_cut = nt(d_attn, w_out[...])
    context = context_ref[0]
    above, below = context > clips[1], context < -clips[1]
    add(S_CLIP_ONE, column_sum(jnp.where(above, d_cut, jnp.where(below, -d_cut, 0.0))))
    d_context = jnp.where(jnp.abs(context) < clips[1], d_cut, 0.0).astype(BF16)
    d_context_ref[0] = d_context
    product = d_context.astype(F32) * context
    high = product.astype(BF16)
    low = (product - high.astype(F32)).astype(BF16)
    shape = (S_ROWS, D)
    heads = lax.broadcasted_iota(jnp.int32, shape, 1) // HEAD_DIM == lax.broadcasted_iota(jnp.int32, shape, 0)
    ones = heads.astype(F32).astype(BF16)
    dots = nt(ones, high) + nt(ones, low)
    for pair in range(PAIRS):
        dots_ref[0, pair] = dots[2 * pair : 2 * pair + 2]


def weight_grads_kernel(act, d_down, up_in, d_pre, cut, d_attn, g_down, g_up, g_out):
    g_down[...] = tn(act[...], d_down[...]).astype(BF16)
    g_up[...] = tn(up_in[...], d_pre[...]).astype(BF16)

    @pl.when(pl.program_id(0) == 0)
    def _():
        g_out[...] = tn(cut[...], d_attn[...]).astype(BF16)


def student_back_kernel(
    lengths, clips, x_ref, qkv_ref, tqk_ref, log_ref, dots_ref, d_context_ref, d_res_ref, w_qkv,
    input_ref, g_qkv, sums_ref, a_in, d_joined,
):
    row = pl.program_id(0)
    tokens = x_ref.shape[1]
    length = lengths[row]
    here = pl.ds(pl.multiple_of(row * tokens, tokens), tokens)

    @pl.when(row == 0)
    def _():
        sums_ref[...] = jnp.zeros_like(sums_ref)

    @pl.loop(0, PAIRS)
    def _(pair):
        queries, keys, values = (qkv_ref[0, :, pair_columns(3 * pair + i)] for i in range(3))
        t_queries, t_keys = (tqk_ref[0, :, pair_columns(2 * pair + i)] for i in range(2))
        d_context = d_context_ref[0, :, pair_columns(pair)]
        grads = attend_pair_back(
            queries, keys, values, t_queries, t_keys, log_ref[0, pair], dots_ref[0, pair], d_context, length
        )
        for i in range(3):
            d_joined[here, pair_columns(3 * pair + i)] = grads[i]
        for i, at in ((0, Q_QUERY), (2, Q_VALUE)):
            sums_ref[at : at + 1, pair_columns(pair)] += column_sum(grads[i].astype(F32))

    bound = clips[0]
    x = x_ref[0].astype(F32)
    a_in[here, :] = jnp.clip(x, -bound, bound).astype(BF16)
    d_a = nt(d_joined[here, :], w_qkv[...])
    inside = jnp.where(jnp.abs(x) < bound, 1.0, jnp.where(jnp.abs(x) == bound, 0.5, 0.0))
    input_ref[0] = (d_res_ref[0] + d_a * inside).astype(BF16)
    outside = (1.0 - inside) * d_a
    sums_ref[Q_CLIP : Q_CLIP + 1] += column_sum(jnp.where(x > 0, outside, -outside))

    @pl.when(row == pl.num_programs(0) - 1)
    def _():
        for i in range(3):
            g_qkv[:, D * i : D * (i + 1)] = tn(a_in[...], d_joined[:, D * i : D * (i + 1)]).astype(BF16)


def rows_spec(tokens, width):
    return pl.BlockSpec((1, tokens, width), lambda r, *_: (r, 0, 0))


def whole_spec(shape):
    return pl.BlockSpec(shape, lambda *_: (0,) * len(shape), pipeline_mode=pl.Buffered(1))


def smem_spec():
    return pl.BlockSpec(memory_space=pltpu.SMEM)


def params(**more):
    return pltpu.CompilerParams(vmem_limit_bytes=VMEM_LIMIT, **more)


def shaped(shape, dtype):
    return jax.ShapeDtypeStruct(shape, dtype)


def teacher_pass(lengths, x, w_qkv, w_out, w_up, w_down):
    rows, tokens, _ = x.shape
    return pl.pallas_call(
        teacher_kernel,
        grid=(rows,),
        in_specs=[smem_spec(), rows_spec(tokens, D)] + [whole_spec(w.shape) for w in (w_qkv, w_out, w_up, w_down)],
        out_specs=[rows_spec(tokens, 2 * D), rows_spec(tokens, D)],
        out_shape=[shaped((rows, tokens, 2 * D), BF16), shaped((rows, tokens, D), F32)],
        scratch_shapes=[pltpu.VMEM((tokens, D), BF16)],
        compiler_params=params(),
    )(lengths, x, w_qkv, w_out, w_up, w_down)


def student_attend(lengths, clips, x, w_qkv, bias_q, bias_v):
    rows, tokens, _ = x.shape
    logs = (1, PAIRS, 2, tokens)
    return pl.pallas_call(
        student_attend_kernel,
        grid=(rows,),
        in_specs=[smem_spec(), smem_spec(), rows_spec(tokens, D), whole_spec(w_qkv.shape)] + [whole_spec((1, D))] * 2,
        out_specs=[
            rows_spec(tokens, 3 * D),
            rows_spec(tokens, D),
            pl.BlockSpec(logs, lambda r: (r, 0, 0, 0)),
        ],
        out_shape=[
            shaped((rows, tokens, 3 * D), BF16),
            shaped((rows, tokens, D), F32),
            shaped((rows,) + logs[1:], F32),
        ],
        scratch_shapes=[pltpu.VMEM((tokens, D), BF16)],
        compiler_params=params(),
    )(lengths, clips, x, w_qkv, bias_q.reshape(1, D), bias_v.reshape(1, D))


def student_middle(lengths, clips, x, cotangent, final, context, weights, vectors):
    rows, tokens, _ = x.shape
    block = tokens // 2 if tokens % 32 == 0 else tokens
    wide = {"act": FF, "d_pre": FF}
    names = ("mixed", "act", "d_pre", "up_in", "d_down", "cut", "d_attn", "d_res", "d_context")

    def spec(width):
        return pl.BlockSpec((1, block, width), lambda r, i: (r, i, 0))

    return pl.pallas_call(
        student_middle_kernel,
        grid=(rows, tokens // block),
        in_specs=[smem_spec(), smem_spec()]
        + [spec(D)] * 4
        + [whole_spec(w.shape) for w in (*weights, *vectors)],
        out_specs=[spec(wide.get(name, D)) for name in names]
        + [pl.BlockSpec((1, PAIRS, 2, block), lambda r, i: (r, 0, 0, i)), whole_spec((S_ROWS, D))],
        out_shape=[
            shaped((rows, tokens, wide.get(name, D)), F32 if name == "d_res" else BF16) for name in names
        ]
        + [shaped((rows, PAIRS, 2, tokens), F32), shaped((S_ROWS, D), F32)],
        scratch_shapes=[pltpu.VMEM((block, FF), F32)],
        compiler_params=params(),
    )(lengths, clips, x, cotangent, final, context, *weights, *vectors)


def weight_grads(act, d_down, up_in, d_pre, cut, d_attn):
    flat = [v.reshape(-1, v.shape[-1]) for v in (act, d_down, up_in, d_pre, cut, d_attn)]
    tokens = flat[0].shape[0]
    chunk = pl.BlockSpec((tokens, D), lambda c: (0, c))
    same = whole_spec((tokens, D))
    return pl.pallas_call(
        weight_grads_kernel,
        grid=(CHUNKS,),
        in_specs=[chunk, same, same, chunk, same, same],
        out_specs=[
            pl.BlockSpec((D, D), lambda c: (c, 0)),
            pl.BlockSpec((D, D), lambda c: (0, c)),
            whole_spec((D, D)),
        ],
        out_shape=[shaped((FF, D), BF16), shaped((D, FF), BF16), shaped((D, D), BF16)],
        compiler_params=params(),
    )(*flat)


def student_back(lengths, clips, x, qkv, tqk, logs, dots, d_context, d_res, w_qkv):
    rows, tokens, _ = x.shape
    return pl.pallas_call(
        student_back_kernel,
        grid=(rows,),
        in_specs=[smem_spec(), smem_spec(), rows_spec(tokens, D), rows_spec(tokens, 3 * D), rows_spec(tokens, 2 * D)]
        + [pl.BlockSpec((1,) + logs.shape[1:], lambda r: (r, 0, 0, 0))] * 2
        + [rows_spec(tokens, D), rows_spec(tokens, D), whole_spec(w_qkv.shape)],
        out_specs=[rows_spec(tokens, D), whole_spec((D, 3 * D)), whole_spec((Q_ROWS, D))],
        out_shape=[shaped((rows, tokens, D), BF16), shaped((D, 3 * D), BF16), shaped((Q_ROWS, D), F32)],
        scratch_shapes=[pltpu.VMEM((rows * tokens, D), BF16), pltpu.VMEM((rows * tokens, 3 * D), BF16)],
        compiler_params=params(),
    )(lengths, clips, x, qkv, tqk, logs, dots, d_context, d_res, w_qkv)


PLANES, COLUMNS, CORES = 4, 4, 2
DEVICES = PLANES * COLUMNS * CORES


class Place:
    def __init__(self):
        self.me = lax.axis_index("shard")
        self.core = self.me % 2
        self.x = (self.me // 2) % 2
        self.y = (self.me // 4) % 2
        self.z = self.me // 8
        self.column = (self.me // 2) % 4
        self.along_x = self.me + 2 - 4 * self.x
        self.along_y = self.me + 4 - 8 * self.y
        self.sibling = self.me + 1 - 2 * self.core
        self.along_a = self.along_x + (self.along_y - self.along_x) * self.core
        self.along_b = self.along_y + (self.along_x - self.along_y) * self.core

    def plane(self, step):
        return (self.me + 8 * step) % DEVICES

    def meet(self):
        partners = [self.sibling, self.along_x, self.along_y] + [self.plane(k) for k in range(1, PLANES)]
        barrier = pltpu.get_barrier_semaphore()
        for partner in partners:
            pl.semaphore_signal(barrier, inc=1, device_id=(partner,), device_id_type=MESH)
        pl.semaphore_wait(barrier, len(partners))


class Trip:
    SEMAPHORES = 14

    def __init__(self, place, source, out, rows, columns, early, send, receive):
        self.place, self.early, self.send, self.receive = place, early, send, receive
        self.source = source.at[rows, columns]
        height, size = source.shape[0], rows.stop - rows.start

        def where(column):
            start = pl.multiple_of(height * (column % CORES) + rows.start, 8)
            return column // CORES, pl.ds(start, size)

        def one(z, column):
            chip, inside = where(column)
            return out.at[z, chip, inside, columns]

        def slab_of(column):
            chip, inside = where(column)
            return out.at[:, chip, inside, columns]

        self.one, self.all = one, slab_of
        self.mine = place.me % 8
        self.at_a = self.mine + place.along_a - place.me
        self.at_b = self.mine + place.along_b - place.me
        self.at_ab = self.at_a + self.at_b - self.mine

    def remote(self, source, target, slot, device):
        return pltpu.make_async_remote_copy(
            src_ref=source, dst_ref=target, send_sem=self.send.at[slot], recv_sem=self.receive.at[slot],
            device_id=(device,), device_id_type=MESH,
        )

    def own(self):
        return pltpu.make_async_copy(self.source, self.one(self.place.z, self.mine), self.send.at[0])

    def line(self, step, source, column, slot):
        return self.remote(source, self.one(self.place.z, column), slot, self.place.plane(step))

    def line_from(self, step, column, slot):
        part = self.one((self.place.z + PLANES - step) % PLANES, column)
        return self.remote(part, part, slot, self.place.plane(step))

    def slab(self, column, slot, device):
        part = self.all(column)
        return self.remote(part, part, slot, device)

    def across(self, source, column):
        return self.remote(source, self.one(self.place.z, column), 4, self.place.along_a)

    def first(self):
        self.own().start()
        if self.early:
            self.across(self.source, self.mine).start()
        for step in range(1, PLANES):
            self.line(step, self.source, self.mine, step).start()

    def second(self):
        place = self.place
        self.own().wait()
        if self.early:
            part = self.one(place.z, self.at_a)
            self.across(part, self.at_a).wait_recv()
            for step in range(1, PLANES):
                self.line(step, part, self.at_a, 10 + step).start()
            return
        for step in range(1, PLANES):
            self.line_from(step, self.mine, step).wait_recv()
        self.slab(self.mine, 4, place.along_a).start()
        self.slab(self.mine, 5, place.along_b).start()
        self.slab(self.mine, 7, place.sibling).start()

    def third(self):
        place = self.place
        if self.early:
            for step in range(1, PLANES):
                self.line_from(step, self.mine, step).wait_recv()
                self.line_from(step, self.at_a, 10 + step).wait_recv()
            self.slab(self.mine, 5, place.along_b).start()
            self.slab(self.mine, 7, place.sibling).start()
        else:
            self.slab(self.at_a, 4, place.along_a).wait_recv()
        self.slab(self.at_a, 6, place.along_b).start()
        self.slab(self.at_a, 8, place.sibling).start()

    def fourth(self):
        place = self.place
        self.slab(self.at_b, 5, place.along_b).wait_recv()
        self.slab(self.at_b, 9, place.sibling).start()
        self.slab(self.at_ab, 6, place.along_b).wait_recv()
        self.slab(self.at_ab, 10, place.sibling).start()

    def fifth(self):
        for slot in range(7, 11):
            self.slab(self.mine, slot, self.place.sibling).wait_recv()

    def phases(self):
        return [self.first, self.second, self.third, self.fourth, self.fifth]

    def last(self):
        one = self.one(self.place.z, self.mine)
        for step in range(1, PLANES):
            self.line(step, one, self.mine, step).wait_send()
            if self.early:
                self.line(step, one, self.mine, 10 + step).wait_send()
        if self.early:
            self.across(one, self.mine).wait_send()
        for slot in range(5 if self.early else 4, 11):
            self.slab(self.mine, slot, self.place.sibling).wait_send()


T_QKV, T_OUT, T_UP, T_DOWN, B_QKV, B_OUT, B_UP, B_DOWN = range(8)
TRAVEL = ((T_QKV, 3), (B_QKV, 1), (T_OUT, 1), (T_UP, 1), (T_DOWN, 1), (B_OUT, 1), (B_UP, 1), (B_DOWN, 1))
EARLY = (T_DOWN, B_DOWN,)
FORWARD_PLAN = (
    (0, 0, 0), (0, 1, 0), (0, 2, 0), (0, 3, 0), (0, 0, 1), (0, 1, 1), (0, 2, 1), (0, 0, 2), (0, 4, 0), (0, 1,
    2), (0, 2, 2), (0, 0, 3), (0, 5, 0), (0, 1, 3), (0, 3, 1), (0, 4, 1), (0, 0, 4), (0, 1, 4), (0, 2, 3), (2,
    2, 4), (3, 4, 2), (3, 6, 0), (5, 5, 1), (6, 3, 2), (7, 4, 3), (7, 6, 1), (9, 4, 4), (15, 3, 3), (15, 7, 0),
    (15, 5, 2), (16, 8, 0), (17, 6, 2), (18, 3, 4), (18, 7, 1), (21, 5, 3), (21, 9, 0), (23, 7, 2), (24, 5, 4),
    (24, 8, 1), (25, 9, 1), (28, 7, 3), (28, 6, 3), (30, 7, 4), (31, 6, 4), (33, 8, 2), (35, 9, 2), (40, 8, 3),
    (43, 8, 4), (44, 9, 3), (47, 9, 4),
)


def travel_parts(shapes):
    parts = []
    for weight, pieces in TRAVEL:
        rows, width = shapes[weight]
        for i in range(pieces):
            if weight in EARLY:
                parts.append((weight, slice(i * rows // pieces, (i + 1) * rows // pieces), slice(0, width)))
            else:
                lanes = width // 128
                columns = slice(i * lanes // pieces * 128, (i + 1) * lanes // pieces * 128)
                parts.append((weight, slice(0, rows), columns))
    return parts


def forward_kernel(*refs):
    lengths, clips = refs[:2]
    teacher_hbm, hidden_hbm = refs[2:4]
    teach, latent, (bias_q, bias_v) = refs[4:8], refs[8:12], refs[12:14]
    outs = refs[14:22]
    tqk_hbm, final_hbm, qkv_hbm, context_hbm, log_hbm = refs[22:27]
    low, near, biases = refs[27:32], refs[32:37], refs[37]
    t_x, a_in, tqk, t_context, final, qkv, context, logs = refs[38:46]
    send, receive, load, store = refs[46:]
    rows = t_x.shape[0]
    place = Place()
    inputs = [pltpu.make_async_copy(teacher_hbm, t_x, load.at[0]), pltpu.make_async_copy(hidden_hbm, a_in, load.at[1])]
    for copy in inputs:
        copy.start()
    for pair in range(PAIRS):
        for i in range(3):
            to, at = TRIPLE * pair + PAIR * i, D * i + PAIR * pair
            low[4][:, to : to + PAIR] = teach[0][:, at : at + PAIR]
    place.meet()
    sources = [low[4], *teach[1:], *low[:4]]
    parts = travel_parts([source.shape for source in sources])
    trips = [
        Trip(place, sources[w], outs[w], r, c, w in EARLY, send.at[i], receive.at[i])
        for i, (w, r, c) in enumerate(parts)
    ]
    weights = [w for w, _, _ in parts]

    def landing(i):
        weight, r, c = parts[i]
        if weight in EARLY:
            c = slice(0, near[weight].shape[1])
        flat = outs[weight].reshape(near[weight].shape)
        return pltpu.make_async_copy(flat.at[:, c], near[weight].at[:, c], load.at[2 + i])

    def lands(i):
        weight = weights[i]
        return weight <= B_QKV and (weight not in EARLY or weight not in weights[i + 1 :])

    def binarize():
        for i in range(1, 4):
            low[i][...] = signed_mean(latent[i][...])
        b_qkv = signed_mean(latent[0][...])
        for pair in range(PAIRS):
            for i in range(3):
                to, at = TRIPLE * pair + PAIR * i, D * i + PAIR * pair
                low[0][:, to : to + PAIR] = b_qkv[:, at : at + PAIR]
        biases[0:1] = bias_q[...].reshape(1, D)
        biases[1:2] = bias_v[...].reshape(1, D)

    phases = [trip.phases() for trip in trips]
    first_student = next(at for at, (_, i, _) in enumerate(FORWARD_PLAN) if weights[i] >= B_QKV)

    def do(at):
        _, i, phase = FORWARD_PLAN[at]
        if at == first_student:
            binarize()
        phases[i][phase]()
        if phase == 4 and lands(i):
            landing(i).start()

    counts = (PAIRS * rows, PAIRS * rows, CHUNKS * rows)
    stage_two, stage_three, end = counts[0], counts[0] + counts[1], sum(counts)
    per = {weight: [i for i, w in enumerate(weights) if w == weight and lands(i)] for weight in set(weights)}

    def stage(slot):
        for at, (when, _, _) in enumerate(FORWARD_PLAN):
            if when == slot:
                do(at)

    def turn(first_slot, count, index):
        for slot in sorted({when for when, _, _ in FORWARD_PLAN if first_slot <= when < first_slot + count}):
            pl.when(index == slot - first_slot)(functools.partial(stage, slot))

    def await_parts(weight, pair, row):
        pairs_each = PAIRS // len(per[weight])
        for n, part in enumerate(per[weight]):
            pl.when(jnp.logical_and(pair == n * pairs_each, row == 0))(landing(part).wait)

    def out_copy(source, target, slot, row):
        return pltpu.make_async_copy(source.at[row], target.at[row], store.at[slot, row])

    inputs[0].wait()
    inputs[1].wait()

    @pl.loop(0, rows)
    def _(row):
        a_in[row] = jnp.clip(a_in[row].astype(F32), -clips[0], clips[0]).astype(BF16)

    @pl.loop(0, PAIRS)
    def _(pair):
        @pl.loop(0, rows)
        def _(row):
            turn(0, counts[0], pair * rows + row)
            await_parts(T_QKV, pair, row)
            teacher_pair(pair, t_x[row], lengths[row], near[T_QKV], tqk.at[row], t_context.at[row])

    for row in range(rows):
        out_copy(tqk, tqk_hbm, 0, row).start()

    @pl.loop(0, PAIRS)
    def _(pair):
        @pl.loop(0, rows)
        def _(row):
            turn(stage_two, counts[1], pair * rows + row)
            await_parts(B_QKV, pair, row)
            student_pair(
                pair, a_in[row], lengths[row], near[B_QKV], biases.at[0:1], biases.at[1:2],
                qkv.at[row], context.at[row], logs.at[row],
            )

    for row in range(rows):
        out_copy(qkv, qkv_hbm, 2, row).start()
        out_copy(context, context_hbm, 3, row).start()
        out_copy(logs, log_hbm, 4, row).start()
    stage(stage_three)
    for weight in (T_OUT, T_UP, T_DOWN):
        for part in per[weight]:
            landing(part).wait()

    @pl.loop(0, rows)
    def _(row):
        final[row] = teacher_last(
            t_x[row], t_context[row], near[T_OUT], near[T_UP], near[T_DOWN],
            lambda c: turn(stage_three + 1, counts[2] - 1, row * CHUNKS + c - 1),
        )
        out_copy(final, final_hbm, 1, row).start()

    stage(end)
    for trip in trips:
        trip.last()

    @pl.loop(0, rows)
    def _(row):
        for slot, (source, target) in enumerate(
            ((tqk, tqk_hbm), (final, final_hbm), (qkv, qkv_hbm), (context, context_hbm), (logs, log_hbm))
        ):
            out_copy(source, target, slot, row).wait()


def forward_pass(lengths, clips, teacher_input, hidden, teach, latent, bias_q, bias_v):
    rows, tokens, _ = hidden.shape
    anywhere, vmem = pl.BlockSpec(memory_space=pl.ANY), pl.BlockSpec(memory_space=pltpu.VMEM)
    gathered = [(PLANES, COLUMNS, CORES * w.shape[0], w.shape[1]) for w in teach] * 2
    made = [
        shaped((rows, tokens, 2 * D), BF16),
        shaped((rows, tokens, D), F32),
        shaped((rows, tokens, 3 * D), BF16),
        shaped((rows, tokens, D), F32),
        shaped((rows, PAIRS, 2, tokens), F32),
    ]
    parts = sum(pieces for _, pieces in TRAVEL)
    near = [(DEVICES * w.shape[0], w.shape[1]) for w in teach] + [(DEVICES * teach[0].shape[0], 3 * D)]
    x_scratch = pltpu.VMEM((rows, tokens, D), BF16)
    outs = pl.pallas_call(
        forward_kernel,
        in_specs=[smem_spec(), smem_spec()] + [anywhere] * 2 + [vmem] * 10,
        out_specs=[anywhere] * 13,
        out_shape=[shaped(shape, BF16) for shape in gathered] + made,
        scratch_shapes=[pltpu.VMEM(w.shape, BF16) for w in (*latent, teach[0])]
        + [pltpu.VMEM(shape, BF16) for shape in near]
        + [pltpu.VMEM((8, D), F32), x_scratch, x_scratch]
        + [pltpu.VMEM(made[0].shape, BF16), x_scratch]
        + [pltpu.VMEM(m.shape, m.dtype) for m in made[1:]]
        + [pltpu.SemaphoreType.DMA((parts, Trip.SEMAPHORES))] * 2
        + [pltpu.SemaphoreType.DMA((2 + parts,)), pltpu.SemaphoreType.DMA((5, rows))],
        compiler_params=params(collective_id=0, has_side_effects=True),
    )(lengths, clips, teacher_input, hidden, *teach, *latent, bias_q, bias_v)
    weights = [out.reshape(-1, out.shape[-1]) for out in outs[4:8]]
    return weights, outs[8:]


class Fold:
    SEMAPHORES = 8

    def __init__(self, place, grad, own, finish, buffers, send, receive):
        self.place, self.grad, self.own, self.finish = place, grad, own, finish
        self.from_core, self.to_p, self.from_p, self.to_q, self.from_q, self.to_z, self.from_z = buffers
        self.send, self.receive = send, receive
        core = place.core
        self.p_stride, self.q_stride = 1 + core, 2 - core
        self.p = place.x + (place.y - place.x) * core
        self.q = place.y + (place.x - place.y) * core

    def remote(self, source, target, slot, device):
        return pltpu.make_async_remote_copy(
            src_ref=source, dst_ref=target, send_sem=self.send.at[slot], recv_sem=self.receive.at[slot],
            device_id=(device,), device_id_type=MESH,
        )

    def column(self, p, q):
        return p * self.p_stride + q * self.q_stride

    def keep(self):
        return pltpu.make_async_copy(self.grad.at[:, :, self.place.core], self.own, self.send.at[0])

    def over_core(self):
        return self.remote(self.grad.at[:, :, 1 - self.place.core], self.from_core, 1, self.place.sibling)

    def over_p(self):
        return self.remote(self.to_p, self.from_p, 2, self.place.along_a)

    def over_q(self):
        return self.remote(self.to_q, self.from_q, 3, self.place.along_b)

    def over_z(self, step):
        return self.remote(self.to_z.at[step - 1], self.from_z.at[step - 1], 3 + step, self.place.plane(step))

    def mine(self, z, column):
        return self.grad[z, column, self.place.core] if self.own is None else self.own[z, column]

    def pair_sum(self, z, column):
        return self.mine(z, column).astype(F32) + self.from_core[z, column].astype(F32)

    def first(self):
        if self.own is not None:
            self.keep().start()
        self.over_core().start()

    def second(self):
        if self.own is not None:
            self.keep().wait()
        self.over_core().wait_recv()

        @pl.loop(0, 2 * PLANES)
        def _(i):
            z, q = i // 2, i % 2
            column = self.column(1 - self.p, q)
            self.to_p[z, q] = self.mine(z, column) + self.from_core[z, column]

        self.over_p().start()

    def third(self):
        self.over_p().wait_recv()

        @pl.loop(0, PLANES)
        def _(z):
            q = 1 - self.q
            total = self.pair_sum(z, self.column(self.p, q)) + self.from_p[z, q].astype(F32)
            self.to_q[z] = total.astype(BF16)

        self.over_q().start()

    def quad_sum(self, z):
        q = self.q
        total = self.pair_sum(z, self.column(self.p, q)) + self.from_p[z, q].astype(F32)
        return total + self.from_q[z].astype(F32)

    def fourth(self):
        self.over_q().wait_recv()
        for step in range(1, PLANES):
            self.to_z[step - 1] = self.quad_sum((self.place.z + step) % PLANES).astype(BF16)
            self.over_z(step).start()

    def fifth(self):
        total = self.quad_sum(self.place.z)
        for step in range(1, PLANES):
            self.over_z(step).wait_recv()
            total = total + self.from_z[step - 1].astype(F32)
        self.finish(total)

    def phases(self):
        return [self.first, self.second, self.third, self.fourth, self.fifth]

    def last(self):
        self.over_core().wait_send()
        self.over_p().wait_send()
        self.over_q().wait_send()
        for step in range(1, PLANES):
            self.over_z(step).wait_send()


FOLD_BUFFERS = ((4, 4), (4, 2), (4, 2), (4,), (4,), (3,), (3,))


class Share:
    SEMAPHORES = 7

    def __init__(self, place, value, out, partial, received, send, receive):
        self.place, self.value, self.out = place, value, out
        self.partial, self.received, self.send, self.receive = partial, received, send, receive

    def swap(self, slot, device):
        return pltpu.make_async_remote_copy(
            src_ref=self.partial.at[min(slot, 3)], dst_ref=self.received.at[slot], send_sem=self.send.at[slot],
            recv_sem=self.receive.at[slot], device_id=(device,), device_id_type=MESH,
        )

    def partners(self):
        place = self.place
        return [place.sibling, place.along_x, place.along_y] + [place.plane(k) for k in range(1, PLANES)]

    def first(self):
        self.partial[0] = self.value[...]
        self.swap(0, self.place.sibling).start()

    def step(self, at):
        partners = self.partners()
        self.swap(at, partners[at]).wait_recv()
        self.partial[at + 1] = self.partial[at] + self.received[at]
        for slot in (at + 1,) if at < 2 else (3, 4, 5):
            self.swap(slot, partners[slot]).start()

    def finish(self):
        partners = self.partners()
        for slot in (3, 4, 5):
            self.swap(slot, partners[slot]).wait_recv()
        place = self.place
        self.received[6] = self.partial[3]
        total = jnp.zeros(self.value.shape, F32)
        for z in range(PLANES):
            behind = (place.z + PLANES - z) % PLANES
            total = total + self.received[(behind + 3) % PLANES + 3]
        self.out[...] = total

    def phases(self):
        return [self.first] + [functools.partial(self.step, at) for at in range(3)] + [self.finish]

    def last(self):
        for slot, partner in enumerate(self.partners()):
            self.swap(slot, partner).wait_send()


FOLDED = ((0, 2), (1, 2), (2, 1))
FOLD_PARTS = sum(pieces for _, pieces in FOLDED)
BACKWARD_PLAN = (
    (0, 0, 0), (0, 1, 0), (0, 2, 0), (0, 3, 0), (0, 4, 0), (3, 5, 0), (3, 4, 1), (4, 0, 1), (4, 5, 1), (5, 4,
    2), (6, 6, 0), (6, 1, 1), (6, 5, 2), (7, 4, 3), (7, 2, 1), (7, 6, 1), (8, 0, 2), (8, 5, 3), (9, 7, 0), (9,
    4, 4), (9, 5, 4), (9, 6, 2), (10, 7, 1), (11, 6, 3), (12, 8, 0), (12, 0, 3), (12, 1, 2), (12, 3, 1), (12, 6,
    4), (12, 7, 2), (13, 2, 2), (13, 8, 1), (14, 7, 3), (15, 9, 0), (15, 0, 4), (15, 7, 4), (16, 1, 3), (16, 8,
    2), (16, 9, 1), (17, 2, 3), (17, 3, 2), (18, 10, 0), (18, 8, 3), (18, 9, 2), (19, 3, 3), (20, 10, 1), (21,
    1, 4), (21, 9, 3), (21, 8, 4), (21, 10, 2), (21, 10, 3), (21, 9, 4), (21, 2, 4), (21, 10, 4), (21, 3, 4),
)
SHARE_SLOTS = (1, 4, 7, 10, 13)


def fold_parts(shapes):
    parts = []
    for i, pieces in FOLDED:
        rows, width = shapes[i]
        for at in range(pieces):
            if i == 0:
                size = rows // pieces
                parts.append((i, slice(at * size, (at + 1) * size), slice(0, width), (size, width)))
            else:
                size = width // pieces
                parts.append((i, slice(0, rows), slice(at * size, (at + 1) * size), (rows, size)))
    return parts


def backward_kernel(*refs):
    lengths, clips = refs[:2]
    qkv, tqk, logs, dots, d_context, w_triple = refs[2:8]
    (x_hbm, d_res_hbm), grads, sums = refs[8:10], refs[10:13], refs[13]
    input_hbm, g_down, g_up, g_out, g_qkv, sums_out, q_sums_out = refs[14:21]
    x, a_in_t, d_pair, d_a, d_res, g_pair, q_sums = refs[21:28]
    scratch = refs[28:]
    rows, tokens = qkv.shape[0], qkv.shape[1]
    place = Place()
    at_step = pl.program_id(0)
    parts = fold_parts([g_down.shape, g_up.shape, g_out.shape])
    owns, scratch = scratch[:FOLD_PARTS], scratch[FOLD_PARTS:]
    per = len(FOLD_BUFFERS)
    taken = (FOLD_PARTS + PAIRS) * per
    buffers, (s_partial, s_received, q_partial, q_received, send, receive, load) = scratch[:taken], scratch[taken:]

    def set_part(target, r, c):
        def finish(total):
            target[r, c] = total

        return finish

    def set_triple(pair):
        def finish(total):
            for i in range(3):
                at = D * i + PAIR * pair
                g_qkv[:, at : at + PAIR] = total[:, PAIR * i : PAIR * (i + 1)]

        return finish

    folds = []
    for n, (i, r, c, _) in enumerate(parts):
        target = (g_down, g_up, g_out)[i]
        source = grads[i].at[:, :, :, r, c]
        folds.append(
            Fold(place, source, owns[n], set_part(target, r, c), buffers[per * n : per * n + per], send.at[n], receive.at[n])
        )
    for pair in range(PAIRS):
        n = FOLD_PARTS + pair
        folds.append(
            Fold(
                place, g_pair.at[pair], None, set_triple(pair), buffers[per * n : per * n + per], send.at[n], receive.at[n]
            )
        )
    n = len(folds)
    share = Share(place, sums, sums_out, s_partial, s_received, send.at[n], receive.at[n])
    q_share = Share(place, q_sums, q_sums_out, q_partial, q_received, send.at[n + 1], receive.at[n + 1])
    inputs = [pltpu.make_async_copy(x_hbm, x, load.at[0]), pltpu.make_async_copy(d_res_hbm, d_res, load.at[1])]

    slots = PAIRS * rows
    phases = [fold.phases() for fold in folds]
    timed = [(slot, phases[i][phase]) for slot, i, phase in BACKWARD_PLAN if i < FOLD_PARTS or phase]
    timed += list(zip(SHARE_SLOTS, share.phases()))

    def stage(slot):
        for when, act in timed:
            if when == slot:
                act()

    def turn(index):
        for slot in sorted({when for when, _ in timed if when < slots}):
            pl.when(index == slot)(functools.partial(stage, slot))

    @pl.when(at_step == 0)
    def _():
        for copy in inputs:
            copy.start()
        place.meet()
        q_sums[...] = jnp.zeros_like(q_sums)
        d_a[...] = jnp.zeros_like(d_a)

    @pl.loop(0, rows)
    def _(row):
        turn(at_step * rows + row)
        queries, keys, values = (qkv[row, :, PAIR * i : PAIR * (i + 1)] for i in range(3))
        t_queries, t_keys = (tqk[row, :, PAIR * i : PAIR * (i + 1)] for i in range(2))
        grads_here = attend_pair_back(
            queries, keys, values, t_queries, t_keys, logs[row, 0], dots[row, 0], d_context[row], lengths[row]
        )
        here = pl.ds(pl.multiple_of(row * tokens, tokens), tokens)
        for i in range(3):
            d_pair[here, PAIR * i : PAIR * (i + 1)] = grads_here[i]

    bound = clips[0]

    @pl.when(at_step == 0)
    def _():
        inputs[0].wait()
        for row in range(rows):
            clipped = jnp.clip(x[row].astype(F32), -bound, bound)
            a_in_t[:, tokens * row : tokens * (row + 1)] = clipped.T.astype(BF16)

    g_now = nn(a_in_t[...], d_pair[...])
    height = g_qkv.shape[0]
    for device in range(DEVICES):
        z, column, core = device // 8, device // 2 % COLUMNS, device % CORES
        g_pair[at_step, z, column, core] = g_now[height * device : height * (device + 1)].astype(BF16)
    for pair, fold in enumerate(folds[FOLD_PARTS:]):
        pl.when(at_step == pair)(fold.first)
    here = pair_columns(at_step)
    q_sums[Q_QUERY : Q_QUERY + 1, here] = column_sum(d_pair[:, :PAIR].astype(F32))
    q_sums[Q_VALUE : Q_VALUE + 1, here] = column_sum(d_pair[:, 2 * PAIR :].astype(F32))
    d_a[...] += nt(d_pair[...], w_triple[...])

    @pl.when(at_step == PAIRS - 1)
    def _():
        inputs[1].wait()
        for row in range(rows):
            stage(slots + row)
            value = x[row].astype(F32)
            d_row = d_a[tokens * row : tokens * (row + 1)]
            inside = jnp.where(jnp.abs(value) < bound, 1.0, jnp.where(jnp.abs(value) == bound, 0.5, 0.0))
            outside = (1.0 - inside) * d_row
            q_sums[Q_CLIP : Q_CLIP + 1] += column_sum(jnp.where(value > 0, outside, -outside))
            x[row] = (d_res[row] + d_row * inside).astype(BF16)
        out = pltpu.make_async_copy(x, input_hbm, load.at[0])
        out.start()
        q_acts = q_share.phases()
        ending = [act for when, act in timed if when >= slots + rows]
        for i in range(max(len(ending), len(q_acts))):
            if i < len(q_acts):
                q_acts[i]()
            if i < len(ending):
                ending[i]()
        for fold in folds:
            fold.last()
        share.last()
        q_share.last()
        out.wait()


def backward_pass(lengths, clips, hidden, qkv, tqk, logs, dots, d_context, d_res, w_qkv, grads, sums):
    rows, tokens, _ = hidden.shape
    heights = [g.shape[0] // DEVICES for g in grads]
    split = [g.reshape(PLANES, COLUMNS, CORES, n, g.shape[-1]) for g, n in zip(grads, heights)]
    shapes = [(n, g.shape[-1]) for g, n in zip(grads, heights)]
    height = w_qkv.shape[0] // DEVICES
    part_shapes = [part[3] for part in fold_parts(shapes)]
    fold_shapes = part_shapes + [(height, TRIPLE)] * PAIRS
    anywhere = pl.BlockSpec(memory_space=pl.ANY)

    def of_pair(width):
        return pl.BlockSpec((rows, tokens, width), lambda p: (0, 0, p))

    stat = pl.BlockSpec((rows, 1, 2, tokens), lambda p: (0, p, 0, 0))
    small = [shaped(sums.shape, F32), shaped((Q_ROWS, D), F32)]
    made = [shaped(s, F32) for s in shapes] + [shaped((height, 3 * D), F32)] + small
    return pl.pallas_call(
        backward_kernel,
        grid=(PAIRS,),
        in_specs=[smem_spec(), smem_spec()]
        + [of_pair(TRIPLE), of_pair(DOUBLE), stat, stat, of_pair(PAIR), pl.BlockSpec((D, TRIPLE), lambda p: (0, p))]
        + [anywhere] * 5
        + [whole_spec(sums.shape)],
        out_specs=[anywhere] + [whole_spec(m.shape) for m in made],
        out_shape=[shaped(hidden.shape, BF16)] + made,
        scratch_shapes=[
            pltpu.VMEM((rows, tokens, D), BF16),
            pltpu.VMEM((D, rows * tokens), BF16),
            pltpu.VMEM((rows * tokens, TRIPLE), BF16),
            pltpu.VMEM((rows * tokens, D), F32),
            pltpu.VMEM((rows, tokens, D), F32),
            pltpu.VMEM((PAIRS, PLANES, COLUMNS, CORES, height, TRIPLE), BF16),
            pltpu.VMEM((Q_ROWS, D), F32),
        ]
        + [pltpu.VMEM((PLANES, COLUMNS) + s, BF16) for s in part_shapes]
        + [pltpu.VMEM(lead + s, BF16) for s in fold_shapes for lead in FOLD_BUFFERS]
        + [pltpu.VMEM((n,) + m.shape, F32) for m in small for n in (4, 7)]
        + [pltpu.SemaphoreType.DMA((len(fold_shapes) + 2, Fold.SEMAPHORES))] * 2
        + [pltpu.SemaphoreType.DMA((2,))],
        compiler_params=params(collective_id=1, has_side_effects=True),
    )(
        lengths, clips, qkv, tqk, logs, dots, d_context, w_qkv, hidden, d_res, *split, sums
    )


def finish_kernel(sums, q_sums, *refs):
    grads, input_hbm = refs[:4], refs[4]
    outs, input_out = refs[5:9], refs[9]
    b_q, b_v, b_out, b_up, b_down, gain_one, shift_one, gain_two, shift_two, clips = refs[10:20]
    held, arrive = refs[20:]
    copy = pltpu.make_async_copy(input_hbm, held, arrive)
    copy.start()

    def row(ref, at):
        return ref[at : at + 1].reshape(D)

    for source, target in zip(grads, outs):
        target[...] = source[...]
    b_q[...] = row(q_sums, Q_QUERY)
    b_v[...] = row(q_sums, Q_VALUE)
    b_out[...] = row(sums, S_OUT)
    b_up[...] = jnp.concatenate([sums[S_UP + c : S_UP + c + 1] for c in range(CHUNKS)], axis=1).reshape(FF)
    b_down[...] = row(sums, S_DOWN)
    gain_one[...] = row(sums, S_GAIN_ONE)
    shift_one[...] = row(sums, S_SHIFT_ONE)
    gain_two[...] = row(sums, S_GAIN_TWO)
    shift_two[...] = row(sums, S_SHIFT_TWO)
    clips[0] = jnp.sum(q_sums[Q_CLIP : Q_CLIP + 1])
    for i, at in enumerate((S_CLIP_ONE, S_CLIP_TWO, S_CLIP_THREE)):
        clips[1 + i] = jnp.sum(sums[at : at + 1])
    copy.wait()
    back = pltpu.make_async_copy(held, input_out, arrive)
    back.start()
    back.wait()


def finish(sums, q_sums, grads, input_grad):
    vmem, anywhere = pl.BlockSpec(memory_space=pltpu.VMEM), pl.BlockSpec(memory_space=pl.ANY)
    lengths = [D, D, D, FF, D, D, D, D, D]
    return pl.pallas_call(
        finish_kernel,
        in_specs=[vmem] * 6 + [anywhere],
        out_specs=[vmem] * 4 + [anywhere] + [vmem] * 9 + [smem_spec()],
        out_shape=[shaped(g.shape, F32) for g in grads]
        + [shaped(input_grad.shape, BF16)]
        + [shaped((n,), F32) for n in lengths]
        + [shaped((4,), F32)],
        scratch_shapes=[pltpu.VMEM(input_grad.shape, BF16), pltpu.SemaphoreType.DMA],
        compiler_params=params(),
    )(sums, q_sums, *grads, input_grad)


def on_device(
    by_kernel,
    hidden, teacher_input, cotangent, lengths, lat_qkv, lat_out, lat_up, lat_down,
    bias_q, bias_v, bias_out, bias_up, bias_down, gain_one, shift_one, gain_two, shift_two, clips,
    teach_qkv, teach_out, teach_up, teach_down,
):
    latent = (lat_qkv, lat_out, lat_up, lat_down)
    teach = (teach_qkv, teach_out, teach_up, teach_down)
    if by_kernel:
        (w_qkv, *weights), (tqk, final, qkv, context, logs) = forward_pass(
            lengths, clips, teacher_input, hidden, teach, latent, bias_q, bias_v
        )
    else:
        gather = functools.partial(lax.all_gather, axis_name="shard", axis=0, tiled=True)
        w_qkv, *weights = (gather(signed_mean(w)) for w in latent)
        w_qkv = by_pairs(w_qkv)
        t_qkv, *t_weights = (gather(w) for w in teach)
        tqk, final = teacher_pass(lengths, teacher_input, by_pairs(t_qkv), *t_weights)
        qkv, context, logs = student_attend(lengths, clips, hidden, w_qkv, bias_q, bias_v)
    vectors = (bias_out, bias_up, bias_down, gain_one, shift_one, gain_two, shift_two)
    mixed, act, d_pre, up_in, d_down, cut, d_attn, d_res, d_context, dots, sums = student_middle(
        lengths, clips, hidden, cotangent, final, context, weights, vectors
    )
    g_down, g_up, g_out = weight_grads(act, d_down, up_in, d_pre, cut, d_attn)
    if by_kernel:
        input_grad, g_down, g_up, g_out, g_qkv, sums, q_sums = backward_pass(
            lengths, clips, hidden, qkv, tqk, logs, dots, d_context, d_res, w_qkv, (g_down, g_up, g_out), sums
        )
    else:
        input_grad, g_qkv, q_sums = student_back(lengths, clips, hidden, qkv, tqk, logs, dots, d_context, d_res, w_qkv)
        scatter = functools.partial(lax.psum_scatter, axis_name="shard", scatter_dimension=0, tiled=True)
        g_down, g_up, g_qkv, g_out = (scatter(g.astype(F32)) for g in (g_down, g_up, by_kinds(g_qkv), g_out))
        sums, q_sums = lax.psum((sums, q_sums), "shard")
    g_qkv, g_out, g_up, g_down, input_grad, *small = finish(sums, q_sums, (g_qkv, g_out, g_up, g_down), input_grad)
    return mixed, input_grad, g_qkv, g_out, g_up, g_down, *small


def solution(mesh):
    split, rows, same = P("shard", None), P("shard", None, None), P()
    return jax.shard_map(
        functools.partial(on_device, mesh.shape["shard"] == DEVICES),
        mesh=mesh,
        in_specs=(rows, rows, rows, P("shard")) + (split,) * 4 + (same,) * 10 + (split,) * 4,
        out_specs=(rows, rows) + (split,) * 4 + (same,) * 10,
        check_vma=False,
    )
```

```python
import functools
import math

import jax
import jax.numpy as jnp
from jax import lax
from jax.experimental import pallas as pl
from jax.experimental.pallas import tpu as pltpu
from jax.sharding import PartitionSpec as P

D = 768
FF = 3072
HEAD_DIM = 64
PAIR = 2 * HEAD_DIM
PAIRS = D // PAIR
DOUBLE, TRIPLE = 2 * PAIR, 3 * PAIR
CHUNKS = FF // D

EPSILON = 1e-05
MASKED = -1000000000.0
SCALE = 1.0 / math.sqrt(HEAD_DIM)

F32 = jnp.float32
BF16 = jnp.bfloat16
MESH = pl.DeviceIdType.MESH
VMEM_LIMIT = 63 * 1024 * 1024


def nn(left, right):
    return lax.dot_general(left, right, (((1,), (0,)), ((), ())), preferred_element_type=F32)


def nt(left, right):
    return lax.dot_general(left, right, (((1,), (1,)), ((), ())), preferred_element_type=F32)


def tn(left, right):
    return lax.dot_general(left, right, (((0,), (0,)), ((), ())), preferred_element_type=F32)


def signed_mean(latent):
    factor = jnp.mean(jnp.abs(latent), axis=1, keepdims=True)
    sign = jnp.where(latent > 0, 1.0, jnp.where(latent < 0, -1.0, 0.0))
    return (factor * sign).astype(BF16)


def normalize(value):
    center = value - jnp.mean(value, axis=-1, keepdims=True)
    inverse = lax.rsqrt(jnp.mean(center * center, axis=-1, keepdims=True) + EPSILON)
    return center * inverse, inverse


def norm_back(d_normed, normed, inverse):
    first = jnp.mean(d_normed, axis=-1, keepdims=True)
    second = jnp.mean(d_normed * normed, axis=-1, keepdims=True)
    return inverse * (d_normed - first - normed * second)


def normal_cdf(value):
    return 0.5 * (1.0 + lax.erf(value * (1.0 / math.sqrt(2.0))))


def column_sum(value):
    return jnp.sum(value, axis=0, keepdims=True)


def head_halves(pair):
    first = lax.broadcasted_iota(jnp.int32, pair.shape, 1) < HEAD_DIM
    zero = jnp.zeros_like(pair)
    return jnp.where(first, pair, zero), jnp.where(first, zero, pair)


def mask_columns(tokens, length):
    shape = (tokens, PAIR)
    first = lax.broadcasted_iota(jnp.int32, shape, 1) == 0
    dead = jnp.logical_and(first, lax.broadcasted_iota(jnp.int32, shape, 0) >= length)
    return jnp.where(dead, MASKED, 0.0).astype(BF16), jnp.where(first, 1.0, 0.0).astype(BF16)


def attend_pair(queries, keys, values, length):
    values_t = values.T
    beside_keys, beside_queries = mask_columns(queries.shape[0], length)
    wide_keys = jnp.concatenate([keys, beside_keys], axis=1)
    contexts, log_totals = [], []
    for head, one in enumerate(head_halves(queries)):
        masked = nt(wide_keys, jnp.concatenate([one, beside_queries], axis=1))
        top = jnp.max(masked, axis=0, keepdims=True)
        expo = jnp.exp(masked - top)
        total = jnp.sum(expo, axis=0, keepdims=True)
        probs = (expo * (1.0 / total)).astype(BF16)
        contexts.append(nn(values_t[HEAD_DIM * head : HEAD_DIM * (head + 1)], probs))
        log_totals.append(top + jnp.log(total))
    return jnp.concatenate(contexts, axis=0).T, jnp.concatenate(log_totals, axis=0)


def attend_pair_back(queries, keys, values, t_queries, t_keys, log_totals, row_dots, d_context, length):
    tokens = queries.shape[0]
    beside_keys, beside_queries = mask_columns(tokens, length)
    wide_keys = jnp.concatenate([keys, beside_keys], axis=1)
    live = lax.broadcasted_iota(jnp.int32, (tokens, DOUBLE), 0) < length
    both_keys = jnp.where(live, jnp.concatenate([keys, -t_keys], axis=1), 0.0).astype(BF16)
    share = jnp.where(live, 1.0 / tokens, 0.0).astype(BF16)
    keys_t = keys.T
    d_queries, d_keys, d_values = [], [], []
    heads = zip(head_halves(queries), head_halves(d_context), head_halves(t_queries))
    for head, (one, d_one, t_one) in enumerate(heads):
        masked = nt(wide_keys, jnp.concatenate([one, beside_queries], axis=1))
        extra = nt(both_keys, jnp.concatenate([one, t_one], axis=1) * share)
        probs = jnp.exp(masked - log_totals[head : head + 1])
        d_probs = nt(values, d_one)
        d_values.append(nn(probs.astype(BF16), d_one))
        d_scores = (probs * (d_probs - row_dots[head : head + 1]) + extra).astype(BF16)
        d_keys.append(nn(d_scores, one))
        d_queries.append(nn(keys_t[HEAD_DIM * head : HEAD_DIM * (head + 1)], d_scores))
    d_q = (jnp.concatenate(d_queries, axis=0).T * SCALE).astype(BF16)
    return d_q, (d_keys[0] + d_keys[1]).astype(BF16), (d_values[0] + d_values[1]).astype(BF16)


def pair_columns(pair, width=PAIR):
    return pl.ds(pl.multiple_of(pair * width, PAIR), width)


def by_pairs(matrix):
    split = matrix.reshape(matrix.shape[0], 3, PAIRS, PAIR)
    return split.transpose(0, 2, 1, 3).reshape(matrix.shape[0], 3 * D)


def by_kinds(matrix):
    split = matrix.reshape(matrix.shape[0], PAIRS, 3, PAIR)
    return split.transpose(0, 2, 1, 3).reshape(matrix.shape[0], 3 * D)


def teacher_pair(pair, x, length, w_qkv, tqk_ref, context_ref):
    joined = nn(x, w_qkv[:, pair_columns(pair, TRIPLE)]).astype(BF16)
    queries, keys, values = (joined[:, PAIR * i : PAIR * (i + 1)] for i in range(3))
    queries = (queries.astype(F32) * SCALE).astype(BF16)
    tqk_ref[:, pair_columns(pair, DOUBLE)] = jnp.concatenate([queries, keys], axis=1)
    mixed, _ = attend_pair(queries, keys, values, length)
    context_ref[:, pair_columns(pair)] = mixed.astype(BF16)


def teacher_last(x, context, w_out, w_up, w_down, between):
    first, _ = normalize(x.astype(F32) + nn(context, w_out[...]))
    first_low = first.astype(BF16)
    total = first
    for c in range(CHUNKS):
        between(c)
        inner = nn(first_low, w_up[:, D * c : D * (c + 1)])
        total = total + nn((inner * normal_cdf(inner)).astype(BF16), w_down[D * c : D * (c + 1), :])
    return normalize(total)[0]


def student_pair(pair, a_in, length, w_qkv, bias_q, bias_v, qkv_ref, context_ref, log_ref):
    joined = nn(a_in, w_qkv[:, pair_columns(pair, TRIPLE)])
    queries = (joined[:, :PAIR] + bias_q[:, pair_columns(pair)]).astype(BF16)
    queries = (queries.astype(F32) * SCALE).astype(BF16)
    keys = joined[:, PAIR:DOUBLE].astype(BF16)
    values = (joined[:, DOUBLE:] + bias_v[:, pair_columns(pair)]).astype(BF16)
    qkv_ref[:, pair_columns(pair, TRIPLE)] = jnp.concatenate([queries, keys, values], axis=1)
    mixed, log_totals = attend_pair(queries, keys, values, length)
    context_ref[:, pair_columns(pair)] = mixed
    log_ref[pair] = log_totals


def teacher_kernel(lengths, x_ref, w_qkv, w_out, w_up, w_down, tqk_ref, final_ref, context):
    length = lengths[pl.program_id(0)]

    @pl.loop(0, PAIRS)
    def _(pair):
        teacher_pair(pair, x_ref[0], length, w_qkv, tqk_ref.at[0], context)

    final_ref[0] = teacher_last(x_ref[0], context[...], w_out, w_up, w_down, lambda c: None)


def student_attend_kernel(lengths, clips, x_ref, w_qkv, bias_q, bias_v, qkv_ref, context_ref, log_ref, a_in):
    length = lengths[pl.program_id(0)]
    a_in[...] = jnp.clip(x_ref[0].astype(F32), -clips[0], clips[0]).astype(BF16)

    @pl.loop(0, PAIRS)
    def _(pair):
        student_pair(
            pair, a_in[...], length, w_qkv, bias_q, bias_v, qkv_ref.at[0], context_ref.at[0], log_ref.at[0]
        )


(S_OUT, S_UP, S_DOWN, S_GAIN_ONE, S_SHIFT_ONE, S_GAIN_TWO, S_SHIFT_TWO, S_CLIP_ONE, S_CLIP_TWO, S_CLIP_THREE) = (
    0, 1, 5, 6, 7, 8, 9, 10, 11, 12,
)
S_ROWS = 16
(Q_QUERY, Q_VALUE, Q_CLIP) = (0, 1, 2)
Q_ROWS = 8
ABOVE, BELOW = 4.0, -4.0


def student_middle_kernel(
    lengths, clips, x_ref, cotangent_ref, final_ref, context_ref, w_out, w_up, w_down,
    bias_out, bias_up, bias_down, gain_one, shift_one, gain_two, shift_two,
    mixed_ref, act_ref, d_pre_ref, up_in_ref, d_down_ref, cut_ref, d_attn_ref, d_res_ref, d_context_ref, dots_ref,
    sums_ref, slope,
):
    block = x_ref.shape[1]
    row, part = pl.program_id(0), pl.program_id(1)
    length = lengths[row] - part * block

    @pl.when(jnp.logical_and(row == 0, part == 0))
    def _():
        sums_ref[...] = jnp.zeros_like(sums_ref)

    def add(at, value):
        sums_ref[at : at + 1] += value

    def vector(ref):
        return ref[...].reshape(1, ref.shape[0])

    cut = jnp.clip(context_ref[0], -clips[1], clips[1]).astype(BF16)
    cut_ref[0] = cut
    normed_one, inverse_one = normalize(x_ref[0].astype(F32) + nn(cut, w_out[...]) + vector(bias_out))
    h_one = normed_one * vector(gain_one) + vector(shift_one)
    up_in = jnp.clip(h_one, -clips[2], clips[2]).astype(BF16)
    up_in_ref[0] = up_in
    total = h_one + vector(bias_down)
    for c in range(CHUNKS):
        columns = slice(D * c, D * (c + 1))
        pre = nn(up_in, w_up[:, columns]) + vector(bias_up)[:, columns]
        cdf = normal_cdf(pre)
        value = pre * cdf
        rise = cdf + pre * jnp.exp(-0.5 * pre * pre) * (1.0 / math.sqrt(2.0 * math.pi))
        rise = jnp.where(value > clips[3], ABOVE, jnp.where(value < -clips[3], BELOW, rise))
        slope[:, columns] = rise
        act = jnp.clip(value, -clips[3], clips[3]).astype(BF16)
        act_ref[0, :, columns] = act
        total = total + nn(act, w_down[columns, :])
    normed_two, inverse_two = normalize(total)
    out = normed_two * vector(gain_two) + vector(shift_two)
    mixed_ref[0] = out.astype(BF16)
    live = lax.broadcasted_iota(jnp.int32, (block, 1), 0) < length
    d_out = jnp.where(live, cotangent_ref[0].astype(F32) + out - final_ref[0], 0.0)
    add(S_GAIN_TWO, column_sum(d_out * normed_two))
    add(S_SHIFT_TWO, column_sum(d_out))
    d_res_two = norm_back(d_out * vector(gain_two), normed_two, inverse_two)
    d_down = d_res_two.astype(BF16)
    d_down_ref[0] = d_down
    add(S_DOWN, column_sum(d_down.astype(F32)))
    d_up_in = jnp.zeros((block, D), F32)
    for c in range(CHUNKS):
        columns = slice(D * c, D * (c + 1))
        d_act = nt(d_down, w_down[columns, :])
        rise = slope[:, columns]
        above, below = rise > 2.0, rise < -2.0
        d_pre = jnp.where(jnp.logical_or(above, below), 0.0, rise * d_act).astype(BF16)
        d_pre_ref[0, :, columns] = d_pre
        add(S_CLIP_THREE, column_sum(jnp.where(above, d_act, jnp.where(below, -d_act, 0.0))))
        add(S_UP + c, column_sum(d_pre.astype(F32)))
        d_up_in = d_up_in + nt(d_pre, w_up[:, columns])
    above, below = h_one > clips[2], h_one < -clips[2]
    add(S_CLIP_TWO, column_sum(jnp.where(above, d_up_in, jnp.where(below, -d_up_in, 0.0))))
    d_h_one = d_res_two + jnp.where(jnp.abs(h_one) < clips[2], d_up_in, 0.0)
    add(S_GAIN_ONE, column_sum(d_h_one * normed_one))
    add(S_SHIFT_ONE, column_sum(d_h_one))
    d_res_one = norm_back(d_h_one * vector(gain_one), normed_one, inverse_one)
    d_res_ref[0] = d_res_one
    d_attn = d_res_one.astype(BF16)
    d_attn_ref[0] = d_attn
    add(S_OUT, column_sum(d_attn.astype(F32)))
    d_cut = nt(d_attn, w_out[...])
    context = context_ref[0]
    above, below = context > clips[1], context < -clips[1]
    add(S_CLIP_ONE, column_sum(jnp.where(above, d_cut, jnp.where(below, -d_cut, 0.0))))
    d_context = jnp.where(jnp.abs(context) < clips[1], d_cut, 0.0).astype(BF16)
    d_context_ref[0] = d_context
    product = d_context.astype(F32) * context
    high = product.astype(BF16)
    low = (product - high.astype(F32)).astype(BF16)
    shape = (S_ROWS, D)
    heads = lax.broadcasted_iota(jnp.int32, shape, 1) // HEAD_DIM == lax.broadcasted_iota(jnp.int32, shape, 0)
    ones = heads.astype(F32).astype(BF16)
    dots = nt(ones, high) + nt(ones, low)
    for pair in range(PAIRS):
        dots_ref[0, pair] = dots[2 * pair : 2 * pair + 2]


def weight_grads_kernel(act, d_down, up_in, d_pre, cut, d_attn, g_down, g_up, g_out):
    g_down[...] = tn(act[...], d_down[...]).astype(BF16)
    g_up[...] = tn(up_in[...], d_pre[...]).astype(BF16)

    @pl.when(pl.program_id(0) == 0)
    def _():
        g_out[...] = tn(cut[...], d_attn[...]).astype(BF16)


def student_back_kernel(
    lengths, clips, x_ref, qkv_ref, tqk_ref, log_ref, dots_ref, d_context_ref, d_res_ref, w_qkv,
    input_ref, g_qkv, sums_ref, a_in, d_joined,
):
    row = pl.program_id(0)
    tokens = x_ref.shape[1]
    length = lengths[row]
    here = pl.ds(pl.multiple_of(row * tokens, tokens), tokens)

    @pl.when(row == 0)
    def _():
        sums_ref[...] = jnp.zeros_like(sums_ref)

    @pl.loop(0, PAIRS)
    def _(pair):
        queries, keys, values = (qkv_ref[0, :, pair_columns(3 * pair + i)] for i in range(3))
        t_queries, t_keys = (tqk_ref[0, :, pair_columns(2 * pair + i)] for i in range(2))
        d_context = d_context_ref[0, :, pair_columns(pair)]
        grads = attend_pair_back(
            queries, keys, values, t_queries, t_keys, log_ref[0, pair], dots_ref[0, pair], d_context, length
        )
        for i in range(3):
            d_joined[here, pair_columns(3 * pair + i)] = grads[i]
        for i, at in ((0, Q_QUERY), (2, Q_VALUE)):
            sums_ref[at : at + 1, pair_columns(pair)] += column_sum(grads[i].astype(F32))

    bound = clips[0]
    x = x_ref[0].astype(F32)
    a_in[here, :] = jnp.clip(x, -bound, bound).astype(BF16)
    d_a = nt(d_joined[here, :], w_qkv[...])
    inside = jnp.where(jnp.abs(x) < bound, 1.0, jnp.where(jnp.abs(x) == bound, 0.5, 0.0))
    input_ref[0] = (d_res_ref[0] + d_a * inside).astype(BF16)
    outside = (1.0 - inside) * d_a
    sums_ref[Q_CLIP : Q_CLIP + 1] += column_sum(jnp.where(x > 0, outside, -outside))

    @pl.when(row == pl.num_programs(0) - 1)
    def _():
        for i in range(3):
            g_qkv[:, D * i : D * (i + 1)] = tn(a_in[...], d_joined[:, D * i : D * (i + 1)]).astype(BF16)


def rows_spec(tokens, width):
    return pl.BlockSpec((1, tokens, width), lambda r, *_: (r, 0, 0))


def whole_spec(shape):
    return pl.BlockSpec(shape, lambda *_: (0,) * len(shape), pipeline_mode=pl.Buffered(1))


def smem_spec():
    return pl.BlockSpec(memory_space=pltpu.SMEM)


def params(**more):
    return pltpu.CompilerParams(vmem_limit_bytes=VMEM_LIMIT, **more)


def shaped(shape, dtype):
    return jax.ShapeDtypeStruct(shape, dtype)


def teacher_pass(lengths, x, w_qkv, w_out, w_up, w_down):
    rows, tokens, _ = x.shape
    return pl.pallas_call(
        teacher_kernel,
        grid=(rows,),
        in_specs=[smem_spec(), rows_spec(tokens, D)] + [whole_spec(w.shape) for w in (w_qkv, w_out, w_up, w_down)],
        out_specs=[rows_spec(tokens, 2 * D), rows_spec(tokens, D)],
        out_shape=[shaped((rows, tokens, 2 * D), BF16), shaped((rows, tokens, D), F32)],
        scratch_shapes=[pltpu.VMEM((tokens, D), BF16)],
        compiler_params=params(),
    )(lengths, x, w_qkv, w_out, w_up, w_down)


def student_attend(lengths, clips, x, w_qkv, bias_q, bias_v):
    rows, tokens, _ = x.shape
    logs = (1, PAIRS, 2, tokens)
    return pl.pallas_call(
        student_attend_kernel,
        grid=(rows,),
        in_specs=[smem_spec(), smem_spec(), rows_spec(tokens, D), whole_spec(w_qkv.shape)] + [whole_spec((1, D))] * 2,
        out_specs=[
            rows_spec(tokens, 3 * D),
            rows_spec(tokens, D),
            pl.BlockSpec(logs, lambda r: (r, 0, 0, 0)),
        ],
        out_shape=[
            shaped((rows, tokens, 3 * D), BF16),
            shaped((rows, tokens, D), F32),
            shaped((rows,) + logs[1:], F32),
        ],
        scratch_shapes=[pltpu.VMEM((tokens, D), BF16)],
        compiler_params=params(),
    )(lengths, clips, x, w_qkv, bias_q.reshape(1, D), bias_v.reshape(1, D))


def student_middle(lengths, clips, x, cotangent, final, context, weights, vectors):
    rows, tokens, _ = x.shape
    block = tokens // 2 if tokens % 32 == 0 else tokens
    wide = {"act": FF, "d_pre": FF}
    names = ("mixed", "act", "d_pre", "up_in", "d_down", "cut", "d_attn", "d_res", "d_context")

    def spec(width):
        return pl.BlockSpec((1, block, width), lambda r, i: (r, i, 0))

    return pl.pallas_call(
        student_middle_kernel,
        grid=(rows, tokens // block),
        in_specs=[smem_spec(), smem_spec()]
        + [spec(D)] * 4
        + [whole_spec(w.shape) for w in (*weights, *vectors)],
        out_specs=[spec(wide.get(name, D)) for name in names]
        + [pl.BlockSpec((1, PAIRS, 2, block), lambda r, i: (r, 0, 0, i)), whole_spec((S_ROWS, D))],
        out_shape=[
            shaped((rows, tokens, wide.get(name, D)), F32 if name == "d_res" else BF16) for name in names
        ]
        + [shaped((rows, PAIRS, 2, tokens), F32), shaped((S_ROWS, D), F32)],
        scratch_shapes=[pltpu.VMEM((block, FF), F32)],
        compiler_params=params(),
    )(lengths, clips, x, cotangent, final, context, *weights, *vectors)


def weight_grads(act, d_down, up_in, d_pre, cut, d_attn):
    flat = [v.reshape(-1, v.shape[-1]) for v in (act, d_down, up_in, d_pre, cut, d_attn)]
    tokens = flat[0].shape[0]
    chunk = pl.BlockSpec((tokens, D), lambda c: (0, c))
    same = whole_spec((tokens, D))
    return pl.pallas_call(
        weight_grads_kernel,
        grid=(CHUNKS,),
        in_specs=[chunk, same, same, chunk, same, same],
        out_specs=[
            pl.BlockSpec((D, D), lambda c: (c, 0)),
            pl.BlockSpec((D, D), lambda c: (0, c)),
            whole_spec((D, D)),
        ],
        out_shape=[shaped((FF, D), BF16), shaped((D, FF), BF16), shaped((D, D), BF16)],
        compiler_params=params(),
    )(*flat)


def student_back(lengths, clips, x, qkv, tqk, logs, dots, d_context, d_res, w_qkv):
    rows, tokens, _ = x.shape
    return pl.pallas_call(
        student_back_kernel,
        grid=(rows,),
        in_specs=[smem_spec(), smem_spec(), rows_spec(tokens, D), rows_spec(tokens, 3 * D), rows_spec(tokens, 2 * D)]
        + [pl.BlockSpec((1,) + logs.shape[1:], lambda r: (r, 0, 0, 0))] * 2
        + [rows_spec(tokens, D), rows_spec(tokens, D), whole_spec(w_qkv.shape)],
        out_specs=[rows_spec(tokens, D), whole_spec((D, 3 * D)), whole_spec((Q_ROWS, D))],
        out_shape=[shaped((rows, tokens, D), BF16), shaped((D, 3 * D), BF16), shaped((Q_ROWS, D), F32)],
        scratch_shapes=[pltpu.VMEM((rows * tokens, D), BF16), pltpu.VMEM((rows * tokens, 3 * D), BF16)],
        compiler_params=params(),
    )(lengths, clips, x, qkv, tqk, logs, dots, d_context, d_res, w_qkv)


PLANES, COLUMNS, CORES = 4, 4, 2
DEVICES = PLANES * COLUMNS * CORES


class Place:
    def __init__(self):
        self.me = lax.axis_index("shard")
        self.core = self.me % 2
        self.x = (self.me // 2) % 2
        self.y = (self.me // 4) % 2
        self.z = self.me // 8
        self.column = (self.me // 2) % 4
        self.along_x = self.me + 2 - 4 * self.x
        self.along_y = self.me + 4 - 8 * self.y
        self.sibling = self.me + 1 - 2 * self.core
        self.along_a = self.along_x + (self.along_y - self.along_x) * self.core
        self.along_b = self.along_y + (self.along_x - self.along_y) * self.core

    def plane(self, step):
        return (self.me + 8 * step) % DEVICES

    def meet(self):
        partners = [self.sibling, self.along_x, self.along_y] + [self.plane(k) for k in range(1, PLANES)]
        barrier = pltpu.get_barrier_semaphore()
        for partner in partners:
            pl.semaphore_signal(barrier, inc=1, device_id=(partner,), device_id_type=MESH)
        pl.semaphore_wait(barrier, len(partners))


class Trip:
    SEMAPHORES = 14

    def __init__(self, place, source, out, rows, columns, early, send, receive):
        self.place, self.early, self.send, self.receive = place, early, send, receive
        self.source = source.at[rows, columns]
        height, size = source.shape[0], rows.stop - rows.start

        def where(column):
            start = pl.multiple_of(height * (column % CORES) + rows.start, 8)
            return column // CORES, pl.ds(start, size)

        def one(z, column):
            chip, inside = where(column)
            return out.at[z, chip, inside, columns]

        def slab_of(column):
            chip, inside = where(column)
            return out.at[:, chip, inside, columns]

        self.one, self.all = one, slab_of
        self.mine = place.me % 8
        self.at_a = self.mine + place.along_a - place.me
        self.at_b = self.mine + place.along_b - place.me
        self.at_ab = self.at_a + self.at_b - self.mine

    def remote(self, source, target, slot, device):
        return pltpu.make_async_remote_copy(
            src_ref=source, dst_ref=target, send_sem=self.send.at[slot], recv_sem=self.receive.at[slot],
            device_id=(device,), device_id_type=MESH,
        )

    def own(self):
        return pltpu.make_async_copy(self.source, self.one(self.place.z, self.mine), self.send.at[0])

    def line(self, step, source, column, slot):
        return self.remote(source, self.one(self.place.z, column), slot, self.place.plane(step))

    def line_from(self, step, column, slot):
        part = self.one((self.place.z + PLANES - step) % PLANES, column)
        return self.remote(part, part, slot, self.place.plane(step))

    def slab(self, column, slot, device):
        part = self.all(column)
        return self.remote(part, part, slot, device)

    def across(self, source, column):
        return self.remote(source, self.one(self.place.z, column), 4, self.place.along_a)

    def first(self):
        self.own().start()
        if self.early:
            self.across(self.source, self.mine).start()
        for step in range(1, PLANES):
            self.line(step, self.source, self.mine, step).start()

    def second(self):
        place = self.place
        self.own().wait()
        if self.early:
            part = self.one(place.z, self.at_a)
            self.across(part, self.at_a).wait_recv()
            for step in range(1, PLANES):
                self.line(step, part, self.at_a, 10 + step).start()
            return
        for step in range(1, PLANES):
            self.line_from(step, self.mine, step).wait_recv()
        self.slab(self.mine, 4, place.along_a).start()
        self.slab(self.mine, 5, place.along_b).start()
        self.slab(self.mine, 7, place.sibling).start()

    def third(self):
        place = self.place
        if self.early:
            for step in range(1, PLANES):
                self.line_from(step, self.mine, step).wait_recv()
                self.line_from(step, self.at_a, 10 + step).wait_recv()
            self.slab(self.mine, 5, place.along_b).start()
            self.slab(self.mine, 7, place.sibling).start()
        else:
            self.slab(self.at_a, 4, place.along_a).wait_recv()
        self.slab(self.at_a, 6, place.along_b).start()
        self.slab(self.at_a, 8, place.sibling).start()

    def fourth(self):
        place = self.place
        self.slab(self.at_b, 5, place.along_b).wait_recv()
        self.slab(self.at_b, 9, place.sibling).start()
        self.slab(self.at_ab, 6, place.along_b).wait_recv()
        self.slab(self.at_ab, 10, place.sibling).start()

    def fifth(self):
        for slot in range(7, 11):
            self.slab(self.mine, slot, self.place.sibling).wait_recv()

    def phases(self):
        return [self.first, self.second, self.third, self.fourth, self.fifth]

    def last(self):
        one = self.one(self.place.z, self.mine)
        for step in range(1, PLANES):
            self.line(step, one, self.mine, step).wait_send()
            if self.early:
                self.line(step, one, self.mine, 10 + step).wait_send()
        if self.early:
            self.across(one, self.mine).wait_send()
        for slot in range(5 if self.early else 4, 11):
            self.slab(self.mine, slot, self.place.sibling).wait_send()


T_QKV, T_OUT, T_UP, T_DOWN, B_QKV, B_OUT, B_UP, B_DOWN = range(8)
TRAVEL = ((T_QKV, 6), (B_QKV, 2), (T_DOWN, 2), (T_OUT, 1), (T_UP, 2), (B_OUT, 1), (B_DOWN, 1), (B_UP, 2))
EARLY = (T_OUT, B_OUT, B_UP,)
TALL = (T_DOWN, B_DOWN)
FORWARD_PLAN = (
    (0, 0, 0), (0, 1, 0), (0, 2, 0), (0, 3, 0), (0, 0, 1), (0, 4, 0), (0, 1, 1), (0, 5, 0), (0, 2, 1), (0, 6,
    0), (0, 0, 2), (0, 3, 1), (0, 1, 2), (0, 4, 1), (0, 2, 2), (0, 5, 1), (0, 0, 3), (0, 7, 0), (0, 3, 2), (0,
    6, 1), (0, 1, 3), (0, 0, 4), (0, 2, 3), (0, 4, 2), (0, 5, 2), (0, 8, 0), (0, 3, 3), (0, 1, 4), (1, 7, 1),
    (2, 2, 4), (2, 3, 4), (2, 6, 2), (3, 4, 3), (3, 5, 3), (3, 9, 0), (4, 8, 1), (5, 4, 4), (5, 5, 4), (5, 7,
    2), (6, 6, 3), (6, 10, 0), (8, 6, 4), (8, 9, 1), (8, 11, 0), (9, 10, 1), (10, 7, 3), (10, 8, 2), (13, 7, 4),
    (13, 12, 0), (14, 9, 2), (14, 10, 2), (14, 8, 3), (14, 11, 1), (16, 13, 0), (17, 8, 4), (18, 12, 1), (18,
    14, 0), (19, 13, 1), (19, 10, 3), (21, 10, 4), (23, 9, 3), (23, 11, 2), (24, 13, 2), (25, 12, 2), (25, 9,
    4), (25, 15, 0), (27, 11, 3), (27, 14, 1), (28, 13, 3), (28, 15, 1), (29, 11, 4), (30, 12, 3), (30, 13, 4),
    (31, 16, 0), (32, 12, 4), (33, 15, 2), (34, 16, 1), (36, 14, 2), (39, 15, 3), (39, 16, 2), (42, 14, 3), (42,
    15, 4), (44, 16, 3), (45, 14, 4), (46, 16, 4),
)


def travel_parts(shapes):
    parts = []
    for weight, pieces in TRAVEL:
        rows, width = shapes[weight]
        for i in range(pieces):
            if weight in TALL:
                parts.append((weight, slice(i * rows // pieces, (i + 1) * rows // pieces), slice(0, width)))
            else:
                lanes = width // 128
                columns = slice(i * lanes // pieces * 128, (i + 1) * lanes // pieces * 128)
                parts.append((weight, slice(0, rows), columns))
    return parts


def forward_kernel(*refs):
    lengths, clips = refs[:2]
    teacher_hbm, hidden_hbm = refs[2:4]
    teach, latent, (bias_q, bias_v) = refs[4:8], refs[8:12], refs[12:14]
    outs = refs[14:22]
    tqk_hbm, final_hbm, qkv_hbm, context_hbm, log_hbm = refs[22:27]
    low, near, biases = refs[27:32], refs[32:37], refs[37]
    t_x, a_in, tqk, t_context, final, qkv, context, logs = refs[38:46]
    send, receive, load, store = refs[46:]
    rows = t_x.shape[0]
    place = Place()
    inputs = [pltpu.make_async_copy(teacher_hbm, t_x, load.at[0]), pltpu.make_async_copy(hidden_hbm, a_in, load.at[1])]
    for copy in inputs:
        copy.start()
    for pair in range(PAIRS):
        for i in range(3):
            to, at = TRIPLE * pair + PAIR * i, D * i + PAIR * pair
            low[4][:, to : to + PAIR] = teach[0][:, at : at + PAIR]
    place.meet()
    sources = [low[4], *teach[1:], *low[:4]]
    parts = travel_parts([source.shape for source in sources])
    trips = [
        Trip(place, sources[w], outs[w], r, c, w in EARLY, send.at[i], receive.at[i])
        for i, (w, r, c) in enumerate(parts)
    ]
    weights = [w for w, _, _ in parts]

    def landing(i):
        weight, r, c = parts[i]
        if weight in TALL:
            c = slice(0, near[weight].shape[1])
        flat = outs[weight].reshape(near[weight].shape)
        return pltpu.make_async_copy(flat.at[:, c], near[weight].at[:, c], load.at[2 + i])

    def lands(i):
        weight = weights[i]
        return weight <= B_QKV and (weight not in TALL or weight not in weights[i + 1 :])

    def binarize():
        for i in range(1, 4):
            low[i][...] = signed_mean(latent[i][...])
        b_qkv = signed_mean(latent[0][...])
        for pair in range(PAIRS):
            for i in range(3):
                to, at = TRIPLE * pair + PAIR * i, D * i + PAIR * pair
                low[0][:, to : to + PAIR] = b_qkv[:, at : at + PAIR]
        biases[0:1] = bias_q[...].reshape(1, D)
        biases[1:2] = bias_v[...].reshape(1, D)

    phases = [trip.phases() for trip in trips]
    first_student = next(at for at, (_, i, _) in enumerate(FORWARD_PLAN) if weights[i] >= B_QKV)

    def do(at):
        _, i, phase = FORWARD_PLAN[at]
        if at == first_student:
            binarize()
        phases[i][phase]()
        if phase == 4 and lands(i):
            landing(i).start()

    counts = (PAIRS * rows, PAIRS * rows, CHUNKS * rows)
    stage_two, stage_three, end = counts[0], counts[0] + counts[1], sum(counts)
    per = {weight: [i for i, w in enumerate(weights) if w == weight and lands(i)] for weight in set(weights)}

    def stage(slot):
        for at, (when, _, _) in enumerate(FORWARD_PLAN):
            if when == slot:
                do(at)

    def turn(first_slot, count, index):
        for slot in sorted({when for when, _, _ in FORWARD_PLAN if first_slot <= when < first_slot + count}):
            pl.when(index == slot - first_slot)(functools.partial(stage, slot))

    def await_parts(weight, pair, row):
        pairs_each = PAIRS // len(per[weight])
        for n, part in enumerate(per[weight]):
            pl.when(jnp.logical_and(pair == n * pairs_each, row == 0))(landing(part).wait)

    def out_copy(source, target, slot, row):
        return pltpu.make_async_copy(source.at[row], target.at[row], store.at[slot, row])

    inputs[0].wait()
    inputs[1].wait()

    @pl.loop(0, rows)
    def _(row):
        a_in[row] = jnp.clip(a_in[row].astype(F32), -clips[0], clips[0]).astype(BF16)

    @pl.loop(0, PAIRS)
    def _(pair):
        @pl.loop(0, rows)
        def _(row):
            turn(0, counts[0], pair * rows + row)
            await_parts(T_QKV, pair, row)
            teacher_pair(pair, t_x[row], lengths[row], near[T_QKV], tqk.at[row], t_context.at[row])

    for row in range(rows):
        out_copy(tqk, tqk_hbm, 0, row).start()

    @pl.loop(0, PAIRS)
    def _(pair):
        @pl.loop(0, rows)
        def _(row):
            turn(stage_two, counts[1], pair * rows + row)
            await_parts(B_QKV, pair, row)
            student_pair(
                pair, a_in[row], lengths[row], near[B_QKV], biases.at[0:1], biases.at[1:2],
                qkv.at[row], context.at[row], logs.at[row],
            )

    for row in range(rows):
        out_copy(qkv, qkv_hbm, 2, row).start()
        out_copy(context, context_hbm, 3, row).start()
        out_copy(logs, log_hbm, 4, row).start()
    stage(stage_three)
    for weight in (T_OUT, T_UP, T_DOWN):
        for part in per[weight]:
            landing(part).wait()

    @pl.loop(0, rows)
    def _(row):
        final[row] = teacher_last(
            t_x[row], t_context[row], near[T_OUT], near[T_UP], near[T_DOWN],
            lambda c: turn(stage_three + 1, counts[2] - 1, row * CHUNKS + c - 1),
        )
        out_copy(final, final_hbm, 1, row).start()

    stage(end)
    for trip in trips:
        trip.last()

    @pl.loop(0, rows)
    def _(row):
        for slot, (source, target) in enumerate(
            ((tqk, tqk_hbm), (final, final_hbm), (qkv, qkv_hbm), (context, context_hbm), (logs, log_hbm))
        ):
            out_copy(source, target, slot, row).wait()


def forward_pass(lengths, clips, teacher_input, hidden, teach, latent, bias_q, bias_v):
    rows, tokens, _ = hidden.shape
    anywhere, vmem = pl.BlockSpec(memory_space=pl.ANY), pl.BlockSpec(memory_space=pltpu.VMEM)
    gathered = [(PLANES, COLUMNS, CORES * w.shape[0], w.shape[1]) for w in teach] * 2
    made = [
        shaped((rows, tokens, 2 * D), BF16),
        shaped((rows, tokens, D), F32),
        shaped((rows, tokens, 3 * D), BF16),
        shaped((rows, tokens, D), F32),
        shaped((rows, PAIRS, 2, tokens), F32),
    ]
    parts = sum(pieces for _, pieces in TRAVEL)
    near = [(DEVICES * w.shape[0], w.shape[1]) for w in teach] + [(DEVICES * teach[0].shape[0], 3 * D)]
    x_scratch = pltpu.VMEM((rows, tokens, D), BF16)
    outs = pl.pallas_call(
        forward_kernel,
        in_specs=[smem_spec(), smem_spec()] + [anywhere] * 2 + [vmem] * 10,
        out_specs=[anywhere] * 13,
        out_shape=[shaped(shape, BF16) for shape in gathered] + made,
        scratch_shapes=[pltpu.VMEM(w.shape, BF16) for w in (*latent, teach[0])]
        + [pltpu.VMEM(shape, BF16) for shape in near]
        + [pltpu.VMEM((8, D), F32), x_scratch, x_scratch]
        + [pltpu.VMEM(made[0].shape, BF16), x_scratch]
        + [pltpu.VMEM(m.shape, m.dtype) for m in made[1:]]
        + [pltpu.SemaphoreType.DMA((parts, Trip.SEMAPHORES))] * 2
        + [pltpu.SemaphoreType.DMA((2 + parts,)), pltpu.SemaphoreType.DMA((5, rows))],
        compiler_params=params(collective_id=0, has_side_effects=True),
    )(lengths, clips, teacher_input, hidden, *teach, *latent, bias_q, bias_v)
    weights = [out.reshape(-1, out.shape[-1]) for out in outs[4:8]]
    return weights, outs[8:]


class Fold:
    SEMAPHORES = 8

    def __init__(self, place, grad, own, finish, buffers, send, receive):
        self.place, self.grad, self.own, self.finish = place, grad, own, finish
        self.from_core, self.to_p, self.from_p, self.to_q, self.from_q, self.to_z, self.from_z = buffers
        self.send, self.receive = send, receive
        core = place.core
        self.p_stride, self.q_stride = 1 + core, 2 - core
        self.p = place.x + (place.y - place.x) * core
        self.q = place.y + (place.x - place.y) * core

    def remote(self, source, target, slot, device):
        return pltpu.make_async_remote_copy(
            src_ref=source, dst_ref=target, send_sem=self.send.at[slot], recv_sem=self.receive.at[slot],
            device_id=(device,), device_id_type=MESH,
        )

    def column(self, p, q):
        return p * self.p_stride + q * self.q_stride

    def keep(self):
        return pltpu.make_async_copy(self.grad.at[:, :, self.place.core], self.own, self.send.at[0])

    def over_core(self):
        return self.remote(self.grad.at[:, :, 1 - self.place.core], self.from_core, 1, self.place.sibling)

    def over_p(self):
        return self.remote(self.to_p, self.from_p, 2, self.place.along_a)

    def over_q(self):
        return self.remote(self.to_q, self.from_q, 3, self.place.along_b)

    def over_z(self, step):
        return self.remote(self.to_z.at[step - 1], self.from_z.at[step - 1], 3 + step, self.place.plane(step))

    def mine(self, z, column):
        return self.grad[z, column, self.place.core] if self.own is None else self.own[z, column]

    def pair_sum(self, z, column):
        return self.mine(z, column).astype(F32) + self.from_core[z, column].astype(F32)

    def first(self):
        if self.own is not None:
            self.keep().start()
        self.over_core().start()

    def second(self):
        if self.own is not None:
            self.keep().wait()
        self.over_core().wait_recv()

        @pl.loop(0, 2 * PLANES)
        def _(i):
            z, q = i // 2, i % 2
            column = self.column(1 - self.p, q)
            self.to_p[z, q] = self.mine(z, column) + self.from_core[z, column]

        self.over_p().start()

    def third(self):
        self.over_p().wait_recv()

        @pl.loop(0, PLANES)
        def _(z):
            q = 1 - self.q
            total = self.pair_sum(z, self.column(self.p, q)) + self.from_p[z, q].astype(F32)
            self.to_q[z] = total.astype(BF16)

        self.over_q().start()

    def quad_sum(self, z):
        q = self.q
        total = self.pair_sum(z, self.column(self.p, q)) + self.from_p[z, q].astype(F32)
        return total + self.from_q[z].astype(F32)

    def fourth(self):
        self.over_q().wait_recv()
        for step in range(1, PLANES):
            self.to_z[step - 1] = self.quad_sum((self.place.z + step) % PLANES).astype(BF16)
            self.over_z(step).start()

    def fifth(self):
        total = self.quad_sum(self.place.z)
        for step in range(1, PLANES):
            self.over_z(step).wait_recv()
            total = total + self.from_z[step - 1].astype(F32)
        self.finish(total)

    def phases(self):
        return [self.first, self.second, self.third, self.fourth, self.fifth]

    def last(self):
        self.over_core().wait_send()
        self.over_p().wait_send()
        self.over_q().wait_send()
        for step in range(1, PLANES):
            self.over_z(step).wait_send()


FOLD_BUFFERS = ((4, 4), (4, 2), (4, 2), (4,), (4,), (3,), (3,))


class Share:
    SEMAPHORES = 7

    def __init__(self, place, value, out, partial, received, send, receive):
        self.place, self.value, self.out = place, value, out
        self.partial, self.received, self.send, self.receive = partial, received, send, receive

    def swap(self, slot, device):
        return pltpu.make_async_remote_copy(
            src_ref=self.partial.at[min(slot, 3)], dst_ref=self.received.at[slot], send_sem=self.send.at[slot],
            recv_sem=self.receive.at[slot], device_id=(device,), device_id_type=MESH,
        )

    def partners(self):
        place = self.place
        return [place.sibling, place.along_x, place.along_y] + [place.plane(k) for k in range(1, PLANES)]

    def first(self):
        self.partial[0] = self.value[...]
        self.swap(0, self.place.sibling).start()

    def step(self, at):
        partners = self.partners()
        self.swap(at, partners[at]).wait_recv()
        self.partial[at + 1] = self.partial[at] + self.received[at]
        for slot in (at + 1,) if at < 2 else (3, 4, 5):
            self.swap(slot, partners[slot]).start()

    def finish(self):
        partners = self.partners()
        for slot in (3, 4, 5):
            self.swap(slot, partners[slot]).wait_recv()
        place = self.place
        self.received[6] = self.partial[3]
        total = jnp.zeros(self.value.shape, F32)
        for z in range(PLANES):
            behind = (place.z + PLANES - z) % PLANES
            total = total + self.received[(behind + 3) % PLANES + 3]
        self.out[...] = total

    def phases(self):
        return [self.first] + [functools.partial(self.step, at) for at in range(3)] + [self.finish]

    def last(self):
        for slot, partner in enumerate(self.partners()):
            self.swap(slot, partner).wait_send()


FOLDED = ((0, 4), (1, 4), (2, 1))
FOLD_PARTS = sum(pieces for _, pieces in FOLDED)
BACKWARD_PLAN = (
    (0, 0, 0), (0, 1, 0), (0, 2, 0), (0, 3, 0), (0, 4, 0), (0, 5, 0), (0, 6, 0), (0, 7, 0), (0, 8, 0), (3, 9,
    0), (4, 0, 1), (4, 1, 1), (4, 15, 0), (4, 9, 1), (6, 10, 0), (6, 2, 1), (6, 3, 1), (6, 15, 1), (6, 9, 2),
    (7, 0, 2), (7, 1, 2), (7, 10, 1), (8, 9, 3), (8, 15, 2), (9, 11, 0), (9, 9, 4), (10, 4, 1), (10, 5, 1), (10,
    11, 1), (10, 0, 3), (10, 15, 3), (10, 1, 3), (10, 10, 2), (11, 2, 2), (11, 3, 2), (12, 12, 0), (12, 10, 3),
    (12, 15, 4), (13, 0, 4), (13, 1, 4), (13, 6, 1), (13, 7, 1), (13, 11, 2), (13, 12, 1), (14, 2, 3), (14, 3,
    3), (14, 4, 2), (14, 5, 2), (14, 10, 4), (15, 13, 0), (15, 11, 3), (16, 12, 2), (16, 13, 1), (17, 2, 4),
    (17, 3, 4), (17, 4, 3), (17, 5, 3), (17, 6, 2), (17, 7, 2), (17, 8, 1), (17, 11, 4), (18, 14, 0), (18, 12,
    3), (18, 13, 2), (20, 6, 3), (20, 7, 3), (20, 14, 1), (21, 4, 4), (21, 5, 4), (21, 8, 2), (21, 12, 4), (21,
    13, 3), (21, 16, 0), (21, 14, 2), (21, 16, 1), (21, 8, 3), (21, 14, 3), (21, 16, 2), (21, 13, 4), (21, 16,
    3), (21, 6, 4), (21, 7, 4), (21, 14, 4), (21, 16, 4), (21, 8, 4),
)


def fold_parts(shapes):
    parts = []
    for i, pieces in FOLDED:
        rows, width = shapes[i]
        for at in range(pieces):
            if i == 0:
                size = rows // pieces
                parts.append((i, slice(at * size, (at + 1) * size), slice(0, width), (size, width)))
            else:
                size = width // pieces
                parts.append((i, slice(0, rows), slice(at * size, (at + 1) * size), (rows, size)))
    return parts


def backward_kernel(*refs):
    lengths, clips = refs[:2]
    qkv, tqk, logs, dots, d_context, w_triple = refs[2:8]
    (x_hbm, d_res_hbm), grads, sums = refs[8:10], refs[10:13], refs[13]
    input_hbm, g_down, g_up, g_out, g_qkv, sums_out, q_sums_out = refs[14:21]
    x, a_in_t, d_pair, d_a, d_res, g_pair, q_sums = refs[21:28]
    scratch = refs[28:]
    rows, tokens = qkv.shape[0], qkv.shape[1]
    place = Place()
    at_step = pl.program_id(0)
    parts = fold_parts([g_down.shape, g_up.shape, g_out.shape])
    owns, scratch = scratch[:FOLD_PARTS], scratch[FOLD_PARTS:]
    per = len(FOLD_BUFFERS)
    taken = (FOLD_PARTS + PAIRS) * per
    buffers, (s_partial, s_received, q_partial, q_received, send, receive, load) = scratch[:taken], scratch[taken:]

    def set_part(target, r, c):
        def finish(total):
            target[r, c] = total

        return finish

    def set_triple(pair):
        def finish(total):
            for i in range(3):
                at = D * i + PAIR * pair
                g_qkv[:, at : at + PAIR] = total[:, PAIR * i : PAIR * (i + 1)]

        return finish

    folds = []
    for n, (i, r, c, _) in enumerate(parts):
        target = (g_down, g_up, g_out)[i]
        source = grads[i].at[:, :, :, r, c]
        folds.append(
            Fold(place, source, owns[n], set_part(target, r, c), buffers[per * n : per * n + per], send.at[n], receive.at[n])
        )
    for pair in range(PAIRS):
        n = FOLD_PARTS + pair
        folds.append(
            Fold(
                place, g_pair.at[pair], None, set_triple(pair), buffers[per * n : per * n + per], send.at[n], receive.at[n]
            )
        )
    n = len(folds)
    share = Share(place, sums, sums_out, s_partial, s_received, send.at[n], receive.at[n])
    q_share = Share(place, q_sums, q_sums_out, q_partial, q_received, send.at[n + 1], receive.at[n + 1])
    inputs = [pltpu.make_async_copy(x_hbm, x, load.at[0]), pltpu.make_async_copy(d_res_hbm, d_res, load.at[1])]

    slots = PAIRS * rows
    phases = [fold.phases() for fold in folds] + [share.phases(), q_share.phases()]
    timed = [
        (slot, phases[i][phase]) for slot, i, phase in BACKWARD_PLAN if phase or not FOLD_PARTS <= i < FOLD_PARTS + PAIRS
    ]

    def stage(slot):
        for when, act in timed:
            if when == slot:
                act()

    def turn(index):
        for slot in sorted({when for when, _ in timed if when < slots}):
            pl.when(index == slot)(functools.partial(stage, slot))

    @pl.when(at_step == 0)
    def _():
        for copy in inputs:
            copy.start()
        place.meet()
        q_sums[...] = jnp.zeros_like(q_sums)
        d_a[...] = jnp.zeros_like(d_a)

    @pl.loop(0, rows)
    def _(row):
        turn(at_step * rows + row)
        queries, keys, values = (qkv[row, :, PAIR * i : PAIR * (i + 1)] for i in range(3))
        t_queries, t_keys = (tqk[row, :, PAIR * i : PAIR * (i + 1)] for i in range(2))
        grads_here = attend_pair_back(
            queries, keys, values, t_queries, t_keys, logs[row, 0], dots[row, 0], d_context[row], lengths[row]
        )
        here = pl.ds(pl.multiple_of(row * tokens, tokens), tokens)
        for i in range(3):
            d_pair[here, PAIR * i : PAIR * (i + 1)] = grads_here[i]

    bound = clips[0]

    @pl.when(at_step == 0)
    def _():
        inputs[0].wait()
        for row in range(rows):
            clipped = jnp.clip(x[row].astype(F32), -bound, bound)
            a_in_t[:, tokens * row : tokens * (row + 1)] = clipped.T.astype(BF16)

    g_now = nn(a_in_t[...], d_pair[...])
    height = g_qkv.shape[0]
    for device in range(DEVICES):
        z, column, core = device // 8, device // 2 % COLUMNS, device % CORES
        g_pair[at_step, z, column, core] = g_now[height * device : height * (device + 1)].astype(BF16)
    for pair, fold in enumerate(folds[FOLD_PARTS:]):
        pl.when(at_step == pair)(fold.first)
    here = pair_columns(at_step)
    q_sums[Q_QUERY : Q_QUERY + 1, here] = column_sum(d_pair[:, :PAIR].astype(F32))
    q_sums[Q_VALUE : Q_VALUE + 1, here] = column_sum(d_pair[:, 2 * PAIR :].astype(F32))
    d_a[...] += nt(d_pair[...], w_triple[...])

    @pl.when(at_step == PAIRS - 1)
    def _():
        inputs[1].wait()
        for row in range(rows):
            stage(slots + row)
            value = x[row].astype(F32)
            d_row = d_a[tokens * row : tokens * (row + 1)]
            inside = jnp.where(jnp.abs(value) < bound, 1.0, jnp.where(jnp.abs(value) == bound, 0.5, 0.0))
            outside = (1.0 - inside) * d_row
            q_sums[Q_CLIP : Q_CLIP + 1] += column_sum(jnp.where(value > 0, outside, -outside))
            x[row] = (d_res[row] + d_row * inside).astype(BF16)
        out = pltpu.make_async_copy(x, input_hbm, load.at[0])
        out.start()
        for when, act in timed:
            if when >= slots + rows:
                act()
        for fold in folds:
            fold.last()
        share.last()
        q_share.last()
        out.wait()


def backward_pass(lengths, clips, hidden, qkv, tqk, logs, dots, d_context, d_res, w_qkv, grads, sums):
    rows, tokens, _ = hidden.shape
    heights = [g.shape[0] // DEVICES for g in grads]
    split = [g.reshape(PLANES, COLUMNS, CORES, n, g.shape[-1]) for g, n in zip(grads, heights)]
    shapes = [(n, g.shape[-1]) for g, n in zip(grads, heights)]
    height = w_qkv.shape[0] // DEVICES
    part_shapes = [part[3] for part in fold_parts(shapes)]
    fold_shapes = part_shapes + [(height, TRIPLE)] * PAIRS
    anywhere = pl.BlockSpec(memory_space=pl.ANY)

    def of_pair(width):
        return pl.BlockSpec((rows, tokens, width), lambda p: (0, 0, p))

    stat = pl.BlockSpec((rows, 1, 2, tokens), lambda p: (0, p, 0, 0))
    small = [shaped(sums.shape, F32), shaped((Q_ROWS, D), F32)]
    made = [shaped(s, F32) for s in shapes] + [shaped((height, 3 * D), F32)] + small
    return pl.pallas_call(
        backward_kernel,
        grid=(PAIRS,),
        in_specs=[smem_spec(), smem_spec()]
        + [of_pair(TRIPLE), of_pair(DOUBLE), stat, stat, of_pair(PAIR), pl.BlockSpec((D, TRIPLE), lambda p: (0, p))]
        + [anywhere] * 5
        + [whole_spec(sums.shape)],
        out_specs=[anywhere] + [whole_spec(m.shape) for m in made],
        out_shape=[shaped(hidden.shape, BF16)] + made,
        scratch_shapes=[
            pltpu.VMEM((rows, tokens, D), BF16),
            pltpu.VMEM((D, rows * tokens), BF16),
            pltpu.VMEM((rows * tokens, TRIPLE), BF16),
            pltpu.VMEM((rows * tokens, D), F32),
            pltpu.VMEM((rows, tokens, D), F32),
            pltpu.VMEM((PAIRS, PLANES, COLUMNS, CORES, height, TRIPLE), BF16),
            pltpu.VMEM((Q_ROWS, D), F32),
        ]
        + [pltpu.VMEM((PLANES, COLUMNS) + s, BF16) for s in part_shapes]
        + [pltpu.VMEM(lead + s, BF16) for s in fold_shapes for lead in FOLD_BUFFERS]
        + [pltpu.VMEM((n,) + m.shape, F32) for m in small for n in (4, 7)]
        + [pltpu.SemaphoreType.DMA((len(fold_shapes) + 2, Fold.SEMAPHORES))] * 2
        + [pltpu.SemaphoreType.DMA((2,))],
        compiler_params=params(collective_id=1, has_side_effects=True),
    )(
        lengths, clips, qkv, tqk, logs, dots, d_context, w_qkv, hidden, d_res, *split, sums
    )


def finish_kernel(sums, q_sums, *refs):
    grads, input_hbm = refs[:4], refs[4]
    outs, input_out = refs[5:9], refs[9]
    b_q, b_v, b_out, b_up, b_down, gain_one, shift_one, gain_two, shift_two, clips = refs[10:20]
    held, arrive = refs[20:]
    copy = pltpu.make_async_copy(input_hbm, held, arrive)
    copy.start()

    def row(ref, at):
        return ref[at : at + 1].reshape(D)

    for source, target in zip(grads, outs):
        target[...] = source[...]
    b_q[...] = row(q_sums, Q_QUERY)
    b_v[...] = row(q_sums, Q_VALUE)
    b_out[...] = row(sums, S_OUT)
    b_up[...] = jnp.concatenate([sums[S_UP + c : S_UP + c + 1] for c in range(CHUNKS)], axis=1).reshape(FF)
    b_down[...] = row(sums, S_DOWN)
    gain_one[...] = row(sums, S_GAIN_ONE)
    shift_one[...] = row(sums, S_SHIFT_ONE)
    gain_two[...] = row(sums, S_GAIN_TWO)
    shift_two[...] = row(sums, S_SHIFT_TWO)
    clips[0] = jnp.sum(q_sums[Q_CLIP : Q_CLIP + 1])
    for i, at in enumerate((S_CLIP_ONE, S_CLIP_TWO, S_CLIP_THREE)):
        clips[1 + i] = jnp.sum(sums[at : at + 1])
    copy.wait()
    back = pltpu.make_async_copy(held, input_out, arrive)
    back.start()
    back.wait()


def finish(sums, q_sums, grads, input_grad):
    vmem, anywhere = pl.BlockSpec(memory_space=pltpu.VMEM), pl.BlockSpec(memory_space=pl.ANY)
    lengths = [D, D, D, FF, D, D, D, D, D]
    return pl.pallas_call(
        finish_kernel,
        in_specs=[vmem] * 6 + [anywhere],
        out_specs=[vmem] * 4 + [anywhere] + [vmem] * 9 + [smem_spec()],
        out_shape=[shaped(g.shape, F32) for g in grads]
        + [shaped(input_grad.shape, BF16)]
        + [shaped((n,), F32) for n in lengths]
        + [shaped((4,), F32)],
        scratch_shapes=[pltpu.VMEM(input_grad.shape, BF16), pltpu.SemaphoreType.DMA],
        compiler_params=params(),
    )(sums, q_sums, *grads, input_grad)


def on_device(
    by_kernel,
    hidden, teacher_input, cotangent, lengths, lat_qkv, lat_out, lat_up, lat_down,
    bias_q, bias_v, bias_out, bias_up, bias_down, gain_one, shift_one, gain_two, shift_two, clips,
    teach_qkv, teach_out, teach_up, teach_down,
):
    latent = (lat_qkv, lat_out, lat_up, lat_down)
    teach = (teach_qkv, teach_out, teach_up, teach_down)
    if by_kernel:
        (w_qkv, *weights), (tqk, final, qkv, context, logs) = forward_pass(
            lengths, clips, teacher_input, hidden, teach, latent, bias_q, bias_v
        )
    else:
        gather = functools.partial(lax.all_gather, axis_name="shard", axis=0, tiled=True)
        w_qkv, *weights = (gather(signed_mean(w)) for w in latent)
        w_qkv = by_pairs(w_qkv)
        t_qkv, *t_weights = (gather(w) for w in teach)
        tqk, final = teacher_pass(lengths, teacher_input, by_pairs(t_qkv), *t_weights)
        qkv, context, logs = student_attend(lengths, clips, hidden, w_qkv, bias_q, bias_v)
    vectors = (bias_out, bias_up, bias_down, gain_one, shift_one, gain_two, shift_two)
    mixed, act, d_pre, up_in, d_down, cut, d_attn, d_res, d_context, dots, sums = student_middle(
        lengths, clips, hidden, cotangent, final, context, weights, vectors
    )
    g_down, g_up, g_out = weight_grads(act, d_down, up_in, d_pre, cut, d_attn)
    if by_kernel:
        input_grad, g_down, g_up, g_out, g_qkv, sums, q_sums = backward_pass(
            lengths, clips, hidden, qkv, tqk, logs, dots, d_context, d_res, w_qkv, (g_down, g_up, g_out), sums
        )
    else:
        input_grad, g_qkv, q_sums = student_back(lengths, clips, hidden, qkv, tqk, logs, dots, d_context, d_res, w_qkv)
        scatter = functools.partial(lax.psum_scatter, axis_name="shard", scatter_dimension=0, tiled=True)
        g_down, g_up, g_qkv, g_out = (scatter(g.astype(F32)) for g in (g_down, g_up, by_kinds(g_qkv), g_out))
        sums, q_sums = lax.psum((sums, q_sums), "shard")
    g_qkv, g_out, g_up, g_down, input_grad, *small = finish(sums, q_sums, (g_qkv, g_out, g_up, g_down), input_grad)
    return mixed, input_grad, g_qkv, g_out, g_up, g_down, *small


def solution(mesh):
    split, rows, same = P("shard", None), P("shard", None, None), P()
    return jax.shard_map(
        functools.partial(on_device, mesh.shape["shard"] == DEVICES),
        mesh=mesh,
        in_specs=(rows, rows, rows, P("shard")) + (split,) * 4 + (same,) * 10 + (split,) * 4,
        out_specs=(rows, rows) + (split,) * 4 + (same,) * 10,
        check_vma=False,
    )
```

```python
import functools
import math

import jax
import jax.numpy as jnp
from jax import lax
from jax.experimental import pallas as pl
from jax.experimental.pallas import tpu as pltpu
from jax.sharding import PartitionSpec as P

D = 768
FF = 3072
HEAD_DIM = 64
PAIR = 2 * HEAD_DIM
PAIRS = D // PAIR
DOUBLE, TRIPLE = 2 * PAIR, 3 * PAIR
CHUNKS = FF // D

EPSILON = 1e-05
MASKED = -1000000000.0
SCALE = 1.0 / math.sqrt(HEAD_DIM)

F32 = jnp.float32
BF16 = jnp.bfloat16
MESH = pl.DeviceIdType.MESH
VMEM_LIMIT = 63 * 1024 * 1024


def nn(left, right):
    return lax.dot_general(left, right, (((1,), (0,)), ((), ())), preferred_element_type=F32)


def nt(left, right):
    return lax.dot_general(left, right, (((1,), (1,)), ((), ())), preferred_element_type=F32)


def tn(left, right):
    return lax.dot_general(left, right, (((0,), (0,)), ((), ())), preferred_element_type=F32)


def signed_mean(latent):
    factor = jnp.mean(jnp.abs(latent), axis=1, keepdims=True)
    sign = jnp.where(latent > 0, 1.0, jnp.where(latent < 0, -1.0, 0.0))
    return (factor * sign).astype(BF16)


def normalize(value):
    center = value - jnp.mean(value, axis=-1, keepdims=True)
    inverse = lax.rsqrt(jnp.mean(center * center, axis=-1, keepdims=True) + EPSILON)
    return center * inverse, inverse


def norm_back(d_normed, normed, inverse):
    first = jnp.mean(d_normed, axis=-1, keepdims=True)
    second = jnp.mean(d_normed * normed, axis=-1, keepdims=True)
    return inverse * (d_normed - first - normed * second)


def normal_cdf(value):
    return 0.5 * (1.0 + lax.erf(value * (1.0 / math.sqrt(2.0))))


def column_sum(value):
    return jnp.sum(value, axis=0, keepdims=True)


def head_halves(pair):
    first = lax.broadcasted_iota(jnp.int32, pair.shape, 1) < HEAD_DIM
    zero = jnp.zeros_like(pair)
    return jnp.where(first, pair, zero), jnp.where(first, zero, pair)


def mask_columns(tokens, length):
    shape = (tokens, PAIR)
    first = lax.broadcasted_iota(jnp.int32, shape, 1) == 0
    dead = jnp.logical_and(first, lax.broadcasted_iota(jnp.int32, shape, 0) >= length)
    return jnp.where(dead, MASKED, 0.0).astype(BF16), jnp.where(first, 1.0, 0.0).astype(BF16)


def attend_pair(queries, keys, values, length):
    values_t = values.T
    beside_keys, beside_queries = mask_columns(queries.shape[0], length)
    wide_keys = jnp.concatenate([keys, beside_keys], axis=1)
    contexts, log_totals = [], []
    for head, one in enumerate(head_halves(queries)):
        masked = nt(wide_keys, jnp.concatenate([one, beside_queries], axis=1))
        top = jnp.max(masked, axis=0, keepdims=True)
        expo = jnp.exp(masked - top)
        total = jnp.sum(expo, axis=0, keepdims=True)
        probs = (expo * (1.0 / total)).astype(BF16)
        contexts.append(nn(values_t[HEAD_DIM * head : HEAD_DIM * (head + 1)], probs))
        log_totals.append(top + jnp.log(total))
    return jnp.concatenate(contexts, axis=0).T, jnp.concatenate(log_totals, axis=0)


def attend_pair_back(queries, keys, values, t_queries, t_keys, log_totals, row_dots, d_context, length):
    tokens = queries.shape[0]
    beside_keys, beside_queries = mask_columns(tokens, length)
    wide_keys = jnp.concatenate([keys, beside_keys], axis=1)
    live = lax.broadcasted_iota(jnp.int32, (tokens, DOUBLE), 0) < length
    both_keys = jnp.where(live, jnp.concatenate([keys, -t_keys], axis=1), 0.0).astype(BF16)
    share = jnp.where(live, 1.0 / tokens, 0.0).astype(BF16)
    keys_t = keys.T
    d_queries, d_keys, d_values = [], [], []
    heads = zip(head_halves(queries), head_halves(d_context), head_halves(t_queries))
    for head, (one, d_one, t_one) in enumerate(heads):
        masked = nt(wide_keys, jnp.concatenate([one, beside_queries], axis=1))
        extra = nt(both_keys, jnp.concatenate([one, t_one], axis=1) * share)
        probs = jnp.exp(masked - log_totals[head : head + 1])
        d_probs = nt(values, d_one)
        d_values.append(nn(probs.astype(BF16), d_one))
        d_scores = (probs * (d_probs - row_dots[head : head + 1]) + extra).astype(BF16)
        d_keys.append(nn(d_scores, one))
        d_queries.append(nn(keys_t[HEAD_DIM * head : HEAD_DIM * (head + 1)], d_scores))
    d_q = (jnp.concatenate(d_queries, axis=0).T * SCALE).astype(BF16)
    return d_q, (d_keys[0] + d_keys[1]).astype(BF16), (d_values[0] + d_values[1]).astype(BF16)


def pair_columns(pair, width=PAIR):
    return pl.ds(pl.multiple_of(pair * width, PAIR), width)


def by_pairs(matrix):
    split = matrix.reshape(matrix.shape[0], 3, PAIRS, PAIR)
    return split.transpose(0, 2, 1, 3).reshape(matrix.shape[0], 3 * D)


def by_kinds(matrix):
    split = matrix.reshape(matrix.shape[0], PAIRS, 3, PAIR)
    return split.transpose(0, 2, 1, 3).reshape(matrix.shape[0], 3 * D)


def teacher_pair(pair, x, length, w_qkv, tqk_ref, context_ref):
    joined = nn(x, w_qkv[:, pair_columns(pair, TRIPLE)]).astype(BF16)
    queries, keys, values = (joined[:, PAIR * i : PAIR * (i + 1)] for i in range(3))
    queries = (queries.astype(F32) * SCALE).astype(BF16)
    tqk_ref[:, pair_columns(pair, DOUBLE)] = jnp.concatenate([queries, keys], axis=1)
    mixed, _ = attend_pair(queries, keys, values, length)
    context_ref[:, pair_columns(pair)] = mixed.astype(BF16)


def teacher_last(x, context, w_out, w_up, w_down, between):
    first, _ = normalize(x.astype(F32) + nn(context, w_out[...]))
    first_low = first.astype(BF16)
    total = first
    for c in range(CHUNKS):
        between(c)
        inner = nn(first_low, w_up[:, D * c : D * (c + 1)])
        total = total + nn((inner * normal_cdf(inner)).astype(BF16), w_down[D * c : D * (c + 1), :])
    return normalize(total)[0]


def student_pair(pair, a_in, length, w_qkv, bias_q, bias_v, qkv_ref, context_ref, log_ref):
    joined = nn(a_in, w_qkv[:, pair_columns(pair, TRIPLE)])
    queries = (joined[:, :PAIR] + bias_q[:, pair_columns(pair)]).astype(BF16)
    queries = (queries.astype(F32) * SCALE).astype(BF16)
    keys = joined[:, PAIR:DOUBLE].astype(BF16)
    values = (joined[:, DOUBLE:] + bias_v[:, pair_columns(pair)]).astype(BF16)
    qkv_ref[:, pair_columns(pair, TRIPLE)] = jnp.concatenate([queries, keys, values], axis=1)
    mixed, log_totals = attend_pair(queries, keys, values, length)
    context_ref[:, pair_columns(pair)] = mixed
    log_ref[pair] = log_totals


def teacher_kernel(lengths, x_ref, w_qkv, w_out, w_up, w_down, tqk_ref, final_ref, context):
    length = lengths[pl.program_id(0)]

    @pl.loop(0, PAIRS)
    def _(pair):
        teacher_pair(pair, x_ref[0], length, w_qkv, tqk_ref.at[0], context)

    final_ref[0] = teacher_last(x_ref[0], context[...], w_out, w_up, w_down, lambda c: None)


def student_attend_kernel(lengths, clips, x_ref, w_qkv, bias_q, bias_v, qkv_ref, context_ref, log_ref, a_in):
    length = lengths[pl.program_id(0)]
    a_in[...] = jnp.clip(x_ref[0].astype(F32), -clips[0], clips[0]).astype(BF16)

    @pl.loop(0, PAIRS)
    def _(pair):
        student_pair(
            pair, a_in[...], length, w_qkv, bias_q, bias_v, qkv_ref.at[0], context_ref.at[0], log_ref.at[0]
        )


(S_OUT, S_UP, S_DOWN, S_GAIN_ONE, S_SHIFT_ONE, S_GAIN_TWO, S_SHIFT_TWO, S_CLIP_ONE, S_CLIP_TWO, S_CLIP_THREE) = (
    0, 1, 5, 6, 7, 8, 9, 10, 11, 12,
)
S_ROWS = 16
(Q_QUERY, Q_VALUE, Q_CLIP) = (0, 1, 2)
Q_ROWS = 8
ABOVE, BELOW = 4.0, -4.0


def student_middle_kernel(
    lengths, clips, x_ref, cotangent_ref, final_ref, context_ref, w_out, w_up, w_down,
    bias_out, bias_up, bias_down, gain_one, shift_one, gain_two, shift_two,
    mixed_ref, act_ref, d_pre_ref, up_in_ref, d_down_ref, cut_ref, d_attn_ref, d_res_ref, d_context_ref, dots_ref,
    sums_ref, slope,
):
    block = x_ref.shape[1]
    row, part = pl.program_id(0), pl.program_id(1)
    length = lengths[row] - part * block

    @pl.when(jnp.logical_and(row == 0, part == 0))
    def _():
        sums_ref[...] = jnp.zeros_like(sums_ref)

    def add(at, value):
        sums_ref[at : at + 1] += value

    def vector(ref):
        return ref[...].reshape(1, ref.shape[0])

    cut = jnp.clip(context_ref[0], -clips[1], clips[1]).astype(BF16)
    cut_ref[0] = cut
    normed_one, inverse_one = normalize(x_ref[0].astype(F32) + nn(cut, w_out[...]) + vector(bias_out))
    h_one = normed_one * vector(gain_one) + vector(shift_one)
    up_in = jnp.clip(h_one, -clips[2], clips[2]).astype(BF16)
    up_in_ref[0] = up_in
    total = h_one + vector(bias_down)
    for c in range(CHUNKS):
        columns = slice(D * c, D * (c + 1))
        pre = nn(up_in, w_up[:, columns]) + vector(bias_up)[:, columns]
        cdf = normal_cdf(pre)
        value = pre * cdf
        rise = cdf + pre * jnp.exp(-0.5 * pre * pre) * (1.0 / math.sqrt(2.0 * math.pi))
        rise = jnp.where(value > clips[3], ABOVE, jnp.where(value < -clips[3], BELOW, rise))
        slope[:, columns] = rise
        act = jnp.clip(value, -clips[3], clips[3]).astype(BF16)
        act_ref[0, :, columns] = act
        total = total + nn(act, w_down[columns, :])
    normed_two, inverse_two = normalize(total)
    out = normed_two * vector(gain_two) + vector(shift_two)
    mixed_ref[0] = out.astype(BF16)
    live = lax.broadcasted_iota(jnp.int32, (block, 1), 0) < length
    d_out = jnp.where(live, cotangent_ref[0].astype(F32) + out - final_ref[0], 0.0)
    add(S_GAIN_TWO, column_sum(d_out * normed_two))
    add(S_SHIFT_TWO, column_sum(d_out))
    d_res_two = norm_back(d_out * vector(gain_two), normed_two, inverse_two)
    d_down = d_res_two.astype(BF16)
    d_down_ref[0] = d_down
    add(S_DOWN, column_sum(d_down.astype(F32)))
    d_up_in = jnp.zeros((block, D), F32)
    for c in range(CHUNKS):
        columns = slice(D * c, D * (c + 1))
        d_act = nt(d_down, w_down[columns, :])
        rise = slope[:, columns]
        above, below = rise > 2.0, rise < -2.0
        d_pre = jnp.where(jnp.logical_or(above, below), 0.0, rise * d_act).astype(BF16)
        d_pre_ref[0, :, columns] = d_pre
        add(S_CLIP_THREE, column_sum(jnp.where(above, d_act, jnp.where(below, -d_act, 0.0))))
        add(S_UP + c, column_sum(d_pre.astype(F32)))
        d_up_in = d_up_in + nt(d_pre, w_up[:, columns])
    above, below = h_one > clips[2], h_one < -clips[2]
    add(S_CLIP_TWO, column_sum(jnp.where(above, d_up_in, jnp.where(below, -d_up_in, 0.0))))
    d_h_one = d_res_two + jnp.where(jnp.abs(h_one) < clips[2], d_up_in, 0.0)
    add(S_GAIN_ONE, column_sum(d_h_one * normed_one))
    add(S_SHIFT_ONE, column_sum(d_h_one))
    d_res_one = norm_back(d_h_one * vector(gain_one), normed_one, inverse_one)
    d_res_ref[0] = d_res_one
    d_attn = d_res_one.astype(BF16)
    d_attn_ref[0] = d_attn
    add(S_OUT, column_sum(d_attn.astype(F32)))
    d_cut = nt(d_attn, w_out[...])
    context = context_ref[0]
    above, below = context > clips[1], context < -clips[1]
    add(S_CLIP_ONE, column_sum(jnp.where(above, d_cut, jnp.where(below, -d_cut, 0.0))))
    d_context = jnp.where(jnp.abs(context) < clips[1], d_cut, 0.0).astype(BF16)
    d_context_ref[0] = d_context
    product = d_context.astype(F32) * context
    high = product.astype(BF16)
    low = (product - high.astype(F32)).astype(BF16)
    shape = (S_ROWS, D)
    heads = lax.broadcasted_iota(jnp.int32, shape, 1) // HEAD_DIM == lax.broadcasted_iota(jnp.int32, shape, 0)
    ones = heads.astype(F32).astype(BF16)
    dots = nt(ones, high) + nt(ones, low)
    for pair in range(PAIRS):
        dots_ref[0, pair] = dots[2 * pair : 2 * pair + 2]


def weight_grads_kernel(act, d_down, up_in, d_pre, cut, d_attn, g_down, g_up, g_out):
    g_down[...] = tn(act[...], d_down[...]).astype(BF16)
    g_up[...] = tn(up_in[...], d_pre[...]).astype(BF16)

    @pl.when(pl.program_id(0) == 0)
    def _():
        g_out[...] = tn(cut[...], d_attn[...]).astype(BF16)


def student_back_kernel(
    lengths, clips, x_ref, qkv_ref, tqk_ref, log_ref, dots_ref, d_context_ref, d_res_ref, w_qkv,
    input_ref, g_qkv, sums_ref, a_in, d_joined,
):
    row = pl.program_id(0)
    tokens = x_ref.shape[1]
    length = lengths[row]
    here = pl.ds(pl.multiple_of(row * tokens, tokens), tokens)

    @pl.when(row == 0)
    def _():
        sums_ref[...] = jnp.zeros_like(sums_ref)

    @pl.loop(0, PAIRS)
    def _(pair):
        queries, keys, values = (qkv_ref[0, :, pair_columns(3 * pair + i)] for i in range(3))
        t_queries, t_keys = (tqk_ref[0, :, pair_columns(2 * pair + i)] for i in range(2))
        d_context = d_context_ref[0, :, pair_columns(pair)]
        grads = attend_pair_back(
            queries, keys, values, t_queries, t_keys, log_ref[0, pair], dots_ref[0, pair], d_context, length
        )
        for i in range(3):
            d_joined[here, pair_columns(3 * pair + i)] = grads[i]
        for i, at in ((0, Q_QUERY), (2, Q_VALUE)):
            sums_ref[at : at + 1, pair_columns(pair)] += column_sum(grads[i].astype(F32))

    bound = clips[0]
    x = x_ref[0].astype(F32)
    a_in[here, :] = jnp.clip(x, -bound, bound).astype(BF16)
    d_a = nt(d_joined[here, :], w_qkv[...])
    inside = jnp.where(jnp.abs(x) < bound, 1.0, jnp.where(jnp.abs(x) == bound, 0.5, 0.0))
    input_ref[0] = (d_res_ref[0] + d_a * inside).astype(BF16)
    outside = (1.0 - inside) * d_a
    sums_ref[Q_CLIP : Q_CLIP + 1] += column_sum(jnp.where(x > 0, outside, -outside))

    @pl.when(row == pl.num_programs(0) - 1)
    def _():
        for i in range(3):
            g_qkv[:, D * i : D * (i + 1)] = tn(a_in[...], d_joined[:, D * i : D * (i + 1)]).astype(BF16)


def rows_spec(tokens, width):
    return pl.BlockSpec((1, tokens, width), lambda r, *_: (r, 0, 0))


def whole_spec(shape):
    return pl.BlockSpec(shape, lambda *_: (0,) * len(shape), pipeline_mode=pl.Buffered(1))


def smem_spec():
    return pl.BlockSpec(memory_space=pltpu.SMEM)


def params(**more):
    return pltpu.CompilerParams(vmem_limit_bytes=VMEM_LIMIT, **more)


def shaped(shape, dtype):
    return jax.ShapeDtypeStruct(shape, dtype)


def teacher_pass(lengths, x, w_qkv, w_out, w_up, w_down):
    rows, tokens, _ = x.shape
    return pl.pallas_call(
        teacher_kernel,
        grid=(rows,),
        in_specs=[smem_spec(), rows_spec(tokens, D)] + [whole_spec(w.shape) for w in (w_qkv, w_out, w_up, w_down)],
        out_specs=[rows_spec(tokens, 2 * D), rows_spec(tokens, D)],
        out_shape=[shaped((rows, tokens, 2 * D), BF16), shaped((rows, tokens, D), F32)],
        scratch_shapes=[pltpu.VMEM((tokens, D), BF16)],
        compiler_params=params(),
    )(lengths, x, w_qkv, w_out, w_up, w_down)


def student_attend(lengths, clips, x, w_qkv, bias_q, bias_v):
    rows, tokens, _ = x.shape
    logs = (1, PAIRS, 2, tokens)
    return pl.pallas_call(
        student_attend_kernel,
        grid=(rows,),
        in_specs=[smem_spec(), smem_spec(), rows_spec(tokens, D), whole_spec(w_qkv.shape)] + [whole_spec((1, D))] * 2,
        out_specs=[
            rows_spec(tokens, 3 * D),
            rows_spec(tokens, D),
            pl.BlockSpec(logs, lambda r: (r, 0, 0, 0)),
        ],
        out_shape=[
            shaped((rows, tokens, 3 * D), BF16),
            shaped((rows, tokens, D), F32),
            shaped((rows,) + logs[1:], F32),
        ],
        scratch_shapes=[pltpu.VMEM((tokens, D), BF16)],
        compiler_params=params(),
    )(lengths, clips, x, w_qkv, bias_q.reshape(1, D), bias_v.reshape(1, D))


def student_middle(lengths, clips, x, cotangent, final, context, weights, vectors):
    rows, tokens, _ = x.shape
    block = tokens // 2 if tokens % 32 == 0 else tokens
    wide = {"act": FF, "d_pre": FF}
    names = ("mixed", "act", "d_pre", "up_in", "d_down", "cut", "d_attn", "d_res", "d_context")

    def spec(width):
        return pl.BlockSpec((1, block, width), lambda r, i: (r, i, 0))

    return pl.pallas_call(
        student_middle_kernel,
        grid=(rows, tokens // block),
        in_specs=[smem_spec(), smem_spec()]
        + [spec(D)] * 4
        + [whole_spec(w.shape) for w in (*weights, *vectors)],
        out_specs=[spec(wide.get(name, D)) for name in names]
        + [pl.BlockSpec((1, PAIRS, 2, block), lambda r, i: (r, 0, 0, i)), whole_spec((S_ROWS, D))],
        out_shape=[
            shaped((rows, tokens, wide.get(name, D)), F32 if name == "d_res" else BF16) for name in names
        ]
        + [shaped((rows, PAIRS, 2, tokens), F32), shaped((S_ROWS, D), F32)],
        scratch_shapes=[pltpu.VMEM((block, FF), F32)],
        compiler_params=params(),
    )(lengths, clips, x, cotangent, final, context, *weights, *vectors)


def weight_grads(act, d_down, up_in, d_pre, cut, d_attn):
    flat = [v.reshape(-1, v.shape[-1]) for v in (act, d_down, up_in, d_pre, cut, d_attn)]
    tokens = flat[0].shape[0]
    chunk = pl.BlockSpec((tokens, D), lambda c: (0, c))
    same = whole_spec((tokens, D))
    return pl.pallas_call(
        weight_grads_kernel,
        grid=(CHUNKS,),
        in_specs=[chunk, same, same, chunk, same, same],
        out_specs=[
            pl.BlockSpec((D, D), lambda c: (c, 0)),
            pl.BlockSpec((D, D), lambda c: (0, c)),
            whole_spec((D, D)),
        ],
        out_shape=[shaped((FF, D), BF16), shaped((D, FF), BF16), shaped((D, D), BF16)],
        compiler_params=params(),
    )(*flat)


def student_back(lengths, clips, x, qkv, tqk, logs, dots, d_context, d_res, w_qkv):
    rows, tokens, _ = x.shape
    return pl.pallas_call(
        student_back_kernel,
        grid=(rows,),
        in_specs=[smem_spec(), smem_spec(), rows_spec(tokens, D), rows_spec(tokens, 3 * D), rows_spec(tokens, 2 * D)]
        + [pl.BlockSpec((1,) + logs.shape[1:], lambda r: (r, 0, 0, 0))] * 2
        + [rows_spec(tokens, D), rows_spec(tokens, D), whole_spec(w_qkv.shape)],
        out_specs=[rows_spec(tokens, D), whole_spec((D, 3 * D)), whole_spec((Q_ROWS, D))],
        out_shape=[shaped((rows, tokens, D), BF16), shaped((D, 3 * D), BF16), shaped((Q_ROWS, D), F32)],
        scratch_shapes=[pltpu.VMEM((rows * tokens, D), BF16), pltpu.VMEM((rows * tokens, 3 * D), BF16)],
        compiler_params=params(),
    )(lengths, clips, x, qkv, tqk, logs, dots, d_context, d_res, w_qkv)


PLANES, COLUMNS, CORES = 4, 4, 2
DEVICES = PLANES * COLUMNS * CORES


class Place:
    def __init__(self):
        self.me = lax.axis_index("shard")
        self.core = self.me % 2
        self.x = (self.me // 2) % 2
        self.y = (self.me // 4) % 2
        self.z = self.me // 8
        self.column = (self.me // 2) % 4
        self.along_x = self.me + 2 - 4 * self.x
        self.along_y = self.me + 4 - 8 * self.y
        self.sibling = self.me + 1 - 2 * self.core
        self.along_a = self.along_x + (self.along_y - self.along_x) * self.core
        self.along_b = self.along_y + (self.along_x - self.along_y) * self.core

    def plane(self, step):
        return (self.me + 8 * step) % DEVICES

    def meet(self):
        partners = [self.sibling, self.along_x, self.along_y] + [self.plane(k) for k in range(1, PLANES)]
        barrier = pltpu.get_barrier_semaphore()
        for partner in partners:
            pl.semaphore_signal(barrier, inc=1, device_id=(partner,), device_id_type=MESH)
        pl.semaphore_wait(barrier, len(partners))


class Trip:
    SEMAPHORES = 14

    def __init__(self, place, source, out, rows, columns, early, send, receive):
        self.place, self.early, self.send, self.receive = place, early, send, receive
        self.source = source.at[rows, columns]
        height, size = source.shape[0], rows.stop - rows.start

        def where(column):
            start = pl.multiple_of(height * (column % CORES) + rows.start, 8)
            return column // CORES, pl.ds(start, size)

        def one(z, column):
            chip, inside = where(column)
            return out.at[z, chip, inside, columns]

        def slab_of(column):
            chip, inside = where(column)
            return out.at[:, chip, inside, columns]

        self.one, self.all = one, slab_of
        self.mine = place.me % 8
        self.at_a = self.mine + place.along_a - place.me
        self.at_b = self.mine + place.along_b - place.me
        self.at_ab = self.at_a + self.at_b - self.mine

    def remote(self, source, target, slot, device):
        return pltpu.make_async_remote_copy(
            src_ref=source, dst_ref=target, send_sem=self.send.at[slot], recv_sem=self.receive.at[slot],
            device_id=(device,), device_id_type=MESH,
        )

    def own(self):
        return pltpu.make_async_copy(self.source, self.one(self.place.z, self.mine), self.send.at[0])

    def line(self, step, source, column, slot):
        return self.remote(source, self.one(self.place.z, column), slot, self.place.plane(step))

    def line_from(self, step, column, slot):
        part = self.one((self.place.z + PLANES - step) % PLANES, column)
        return self.remote(part, part, slot, self.place.plane(step))

    def slab(self, column, slot, device):
        part = self.all(column)
        return self.remote(part, part, slot, device)

    def across(self, source, column):
        return self.remote(source, self.one(self.place.z, column), 4, self.place.along_a)

    def first(self):
        self.own().start()
        if self.early:
            self.across(self.source, self.mine).start()
        for step in range(1, PLANES):
            self.line(step, self.source, self.mine, step).start()

    def second(self):
        place = self.place
        self.own().wait()
        if self.early:
            part = self.one(place.z, self.at_a)
            self.across(part, self.at_a).wait_recv()
            for step in range(1, PLANES):
                self.line(step, part, self.at_a, 10 + step).start()
            return
        for step in range(1, PLANES):
            self.line_from(step, self.mine, step).wait_recv()
        self.slab(self.mine, 4, place.along_a).start()
        self.slab(self.mine, 5, place.along_b).start()
        self.slab(self.mine, 7, place.sibling).start()

    def third(self):
        place = self.place
        if self.early:
            for step in range(1, PLANES):
                self.line_from(step, self.mine, step).wait_recv()
                self.line_from(step, self.at_a, 10 + step).wait_recv()
            self.slab(self.mine, 5, place.along_b).start()
            self.slab(self.mine, 7, place.sibling).start()
        else:
            self.slab(self.at_a, 4, place.along_a).wait_recv()
        self.slab(self.at_a, 6, place.along_b).start()
        self.slab(self.at_a, 8, place.sibling).start()

    def fourth(self):
        place = self.place
        self.slab(self.at_b, 5, place.along_b).wait_recv()
        self.slab(self.at_b, 9, place.sibling).start()
        self.slab(self.at_ab, 6, place.along_b).wait_recv()
        self.slab(self.at_ab, 10, place.sibling).start()

    def fifth(self):
        for slot in range(7, 11):
            self.slab(self.mine, slot, self.place.sibling).wait_recv()

    def phases(self):
        return [self.first, self.second, self.third, self.fourth, self.fifth]

    def last(self):
        one = self.one(self.place.z, self.mine)
        for step in range(1, PLANES):
            self.line(step, one, self.mine, step).wait_send()
            if self.early:
                self.line(step, one, self.mine, 10 + step).wait_send()
        if self.early:
            self.across(one, self.mine).wait_send()
        for slot in range(5 if self.early else 4, 11):
            self.slab(self.mine, slot, self.place.sibling).wait_send()


T_QKV, T_OUT, T_UP, T_DOWN, B_QKV, B_OUT, B_UP, B_DOWN = range(8)
TRAVEL = ((T_QKV, 6), (B_QKV, 2), (T_DOWN, 2), (T_OUT, 1), (T_UP, 2), (B_OUT, 1), (B_DOWN, 1), (B_UP, 2))
EARLY = (T_OUT, B_OUT, B_UP,)
TALL = (T_DOWN, B_DOWN)
FORWARD_PLAN = (
    (0, 0, 0), (0, 1, 0), (0, 2, 0), (0, 3, 0), (0, 0, 1), (0, 4, 0), (0, 1, 1), (0, 5, 0), (0, 2, 1), (0, 6,
    0), (0, 0, 2), (0, 3, 1), (0, 1, 2), (0, 4, 1), (0, 2, 2), (0, 5, 1), (0, 0, 3), (0, 7, 0), (0, 3, 2), (0,
    6, 1), (0, 1, 3), (0, 0, 4), (0, 2, 3), (0, 4, 2), (0, 5, 2), (0, 8, 0), (0, 3, 3), (0, 1, 4), (1, 7, 1),
    (2, 2, 4), (2, 3, 4), (2, 6, 2), (3, 4, 3), (3, 5, 3), (3, 9, 0), (4, 8, 1), (5, 4, 4), (5, 5, 4), (5, 7,
    2), (6, 6, 3), (6, 10, 0), (8, 6, 4), (8, 9, 1), (8, 11, 0), (9, 10, 1), (10, 7, 3), (10, 8, 2), (13, 7, 4),
    (13, 12, 0), (14, 9, 2), (14, 10, 2), (14, 8, 3), (14, 11, 1), (16, 13, 0), (17, 8, 4), (18, 12, 1), (18,
    14, 0), (19, 13, 1), (19, 10, 3), (21, 10, 4), (23, 9, 3), (23, 11, 2), (24, 13, 2), (25, 12, 2), (25, 9,
    4), (25, 15, 0), (27, 11, 3), (27, 14, 1), (28, 13, 3), (28, 15, 1), (29, 11, 4), (30, 12, 3), (30, 13, 4),
    (31, 16, 0), (32, 12, 4), (33, 15, 2), (34, 16, 1), (36, 14, 2), (39, 15, 3), (39, 16, 2), (42, 14, 3), (42,
    15, 4), (44, 16, 3), (45, 14, 4), (46, 16, 4),
)


def travel_parts(shapes):
    parts = []
    for weight, pieces in TRAVEL:
        rows, width = shapes[weight]
        for i in range(pieces):
            if weight in TALL:
                parts.append((weight, slice(i * rows // pieces, (i + 1) * rows // pieces), slice(0, width)))
            else:
                lanes = width // 128
                columns = slice(i * lanes // pieces * 128, (i + 1) * lanes // pieces * 128)
                parts.append((weight, slice(0, rows), columns))
    return parts


def forward_kernel(*refs):
    lengths, clips = refs[:2]
    teacher_hbm, hidden_hbm = refs[2:4]
    teach, latent, (bias_q, bias_v) = refs[4:8], refs[8:12], refs[12:14]
    outs = refs[14:22]
    tqk_hbm, final_hbm, qkv_hbm, context_hbm, log_hbm = refs[22:27]
    low, near, biases = refs[27:32], refs[32:37], refs[37]
    t_x, a_in, tqk, t_context, final, qkv, context, logs = refs[38:46]
    send, receive, load, store = refs[46:]
    rows = t_x.shape[0]
    place = Place()
    inputs = [pltpu.make_async_copy(teacher_hbm, t_x, load.at[0]), pltpu.make_async_copy(hidden_hbm, a_in, load.at[1])]
    for copy in inputs:
        copy.start()
    for pair in range(PAIRS):
        for i in range(3):
            to, at = TRIPLE * pair + PAIR * i, D * i + PAIR * pair
            low[4][:, to : to + PAIR] = teach[0][:, at : at + PAIR]
    place.meet()
    sources = [low[4], *teach[1:], *low[:4]]
    parts = travel_parts([source.shape for source in sources])
    trips = [
        Trip(place, sources[w], outs[w], r, c, w in EARLY, send.at[i], receive.at[i])
        for i, (w, r, c) in enumerate(parts)
    ]
    weights = [w for w, _, _ in parts]

    def landing(i):
        weight, r, c = parts[i]
        if weight in TALL:
            c = slice(0, near[weight].shape[1])
        flat = outs[weight].reshape(near[weight].shape)
        return pltpu.make_async_copy(flat.at[:, c], near[weight].at[:, c], load.at[2 + i])

    def lands(i):
        weight = weights[i]
        return weight <= B_QKV and (weight not in TALL or weight not in weights[i + 1 :])

    def binarize():
        for i in range(1, 4):
            low[i][...] = signed_mean(latent[i][...])
        b_qkv = signed_mean(latent[0][...])
        for pair in range(PAIRS):
            for i in range(3):
                to, at = TRIPLE * pair + PAIR * i, D * i + PAIR * pair
                low[0][:, to : to + PAIR] = b_qkv[:, at : at + PAIR]
        biases[0:1] = bias_q[...].reshape(1, D)
        biases[1:2] = bias_v[...].reshape(1, D)

    phases = [trip.phases() for trip in trips]
    first_student = next(at for at, (_, i, _) in enumerate(FORWARD_PLAN) if weights[i] >= B_QKV)

    def do(at):
        _, i, phase = FORWARD_PLAN[at]
        if at == first_student:
            binarize()
        phases[i][phase]()
        if phase == 4 and lands(i):
            landing(i).start()

    counts = (PAIRS * rows, PAIRS * rows, CHUNKS * rows)
    stage_two, stage_three, end = counts[0], counts[0] + counts[1], sum(counts)
    per = {weight: [i for i, w in enumerate(weights) if w == weight and lands(i)] for weight in set(weights)}

    def stage(slot):
        for at, (when, _, _) in enumerate(FORWARD_PLAN):
            if when == slot:
                do(at)

    def turn(first_slot, count, index):
        for slot in sorted({when for when, _, _ in FORWARD_PLAN if first_slot <= when < first_slot + count}):
            pl.when(index == slot - first_slot)(functools.partial(stage, slot))

    def await_parts(weight, pair, row):
        pairs_each = PAIRS // len(per[weight])
        for n, part in enumerate(per[weight]):
            pl.when(jnp.logical_and(pair == n * pairs_each, row == 0))(landing(part).wait)

    def out_copy(source, target, slot, row):
        return pltpu.make_async_copy(source.at[row], target.at[row], store.at[slot, row])

    inputs[0].wait()
    inputs[1].wait()

    @pl.loop(0, rows)
    def _(row):
        a_in[row] = jnp.clip(a_in[row].astype(F32), -clips[0], clips[0]).astype(BF16)

    @pl.loop(0, PAIRS)
    def _(pair):
        @pl.loop(0, rows)
        def _(row):
            turn(0, counts[0], pair * rows + row)
            await_parts(T_QKV, pair, row)
            teacher_pair(pair, t_x[row], lengths[row], near[T_QKV], tqk.at[row], t_context.at[row])

    for row in range(rows):
        out_copy(tqk, tqk_hbm, 0, row).start()

    @pl.loop(0, PAIRS)
    def _(pair):
        @pl.loop(0, rows)
        def _(row):
            turn(stage_two, counts[1], pair * rows + row)
            await_parts(B_QKV, pair, row)
            student_pair(
                pair, a_in[row], lengths[row], near[B_QKV], biases.at[0:1], biases.at[1:2],
                qkv.at[row], context.at[row], logs.at[row],
            )

    for row in range(rows):
        out_copy(qkv, qkv_hbm, 2, row).start()
        out_copy(context, context_hbm, 3, row).start()
        out_copy(logs, log_hbm, 4, row).start()
    stage(stage_three)
    for weight in (T_OUT, T_UP, T_DOWN):
        for part in per[weight]:
            landing(part).wait()

    @pl.loop(0, rows)
    def _(row):
        final[row] = teacher_last(
            t_x[row], t_context[row], near[T_OUT], near[T_UP], near[T_DOWN],
            lambda c: turn(stage_three + 1, counts[2] - 1, row * CHUNKS + c - 1),
        )
        out_copy(final, final_hbm, 1, row).start()

    stage(end)
    for trip in trips:
        trip.last()

    @pl.loop(0, rows)
    def _(row):
        for slot, (source, target) in enumerate(
            ((tqk, tqk_hbm), (final, final_hbm), (qkv, qkv_hbm), (context, context_hbm), (logs, log_hbm))
        ):
            out_copy(source, target, slot, row).wait()


def forward_pass(lengths, clips, teacher_input, hidden, teach, latent, bias_q, bias_v):
    rows, tokens, _ = hidden.shape
    anywhere, vmem = pl.BlockSpec(memory_space=pl.ANY), pl.BlockSpec(memory_space=pltpu.VMEM)
    gathered = [(PLANES, COLUMNS, CORES * w.shape[0], w.shape[1]) for w in teach] * 2
    made = [
        shaped((rows, tokens, 2 * D), BF16),
        shaped((rows, tokens, D), F32),
        shaped((rows, tokens, 3 * D), BF16),
        shaped((rows, tokens, D), F32),
        shaped((rows, PAIRS, 2, tokens), F32),
    ]
    parts = sum(pieces for _, pieces in TRAVEL)
    near = [(DEVICES * w.shape[0], w.shape[1]) for w in teach] + [(DEVICES * teach[0].shape[0], 3 * D)]
    x_scratch = pltpu.VMEM((rows, tokens, D), BF16)
    outs = pl.pallas_call(
        forward_kernel,
        in_specs=[smem_spec(), smem_spec()] + [anywhere] * 2 + [vmem] * 10,
        out_specs=[anywhere] * 13,
        out_shape=[shaped(shape, BF16) for shape in gathered] + made,
        scratch_shapes=[pltpu.VMEM(w.shape, BF16) for w in (*latent, teach[0])]
        + [pltpu.VMEM(shape, BF16) for shape in near]
        + [pltpu.VMEM((8, D), F32), x_scratch, x_scratch]
        + [pltpu.VMEM(made[0].shape, BF16), x_scratch]
        + [pltpu.VMEM(m.shape, m.dtype) for m in made[1:]]
        + [pltpu.SemaphoreType.DMA((parts, Trip.SEMAPHORES))] * 2
        + [pltpu.SemaphoreType.DMA((2 + parts,)), pltpu.SemaphoreType.DMA((5, rows))],
        compiler_params=params(collective_id=0, has_side_effects=True),
    )(lengths, clips, teacher_input, hidden, *teach, *latent, bias_q, bias_v)
    weights = [out.reshape(-1, out.shape[-1]) for out in outs[4:8]]
    return weights, outs[8:]


class Fold:
    SEMAPHORES = 8

    def __init__(self, place, grad, own, finish, buffers, send, receive):
        self.place, self.grad, self.own, self.finish = place, grad, own, finish
        self.from_core, self.to_p, self.from_p, self.to_q, self.from_q, self.to_z, self.from_z = buffers
        self.send, self.receive = send, receive
        core = place.core
        self.p_stride, self.q_stride = 1 + core, 2 - core
        self.p = place.x + (place.y - place.x) * core
        self.q = place.y + (place.x - place.y) * core

    def remote(self, source, target, slot, device):
        return pltpu.make_async_remote_copy(
            src_ref=source, dst_ref=target, send_sem=self.send.at[slot], recv_sem=self.receive.at[slot],
            device_id=(device,), device_id_type=MESH,
        )

    def column(self, p, q):
        return p * self.p_stride + q * self.q_stride

    def keep(self):
        return pltpu.make_async_copy(self.grad.at[:, :, self.place.core], self.own, self.send.at[0])

    def over_core(self):
        return self.remote(self.grad.at[:, :, 1 - self.place.core], self.from_core, 1, self.place.sibling)

    def over_p(self):
        return self.remote(self.to_p, self.from_p, 2, self.place.along_a)

    def over_q(self):
        return self.remote(self.to_q, self.from_q, 3, self.place.along_b)

    def over_z(self, step):
        return self.remote(self.to_z.at[step - 1], self.from_z.at[step - 1], 3 + step, self.place.plane(step))

    def mine(self, z, column):
        return self.grad[z, column, self.place.core] if self.own is None else self.own[z, column]

    def pair_sum(self, z, column):
        return self.mine(z, column).astype(F32) + self.from_core[z, column].astype(F32)

    def first(self):
        if self.own is not None:
            self.keep().start()
        self.over_core().start()

    def second(self):
        if self.own is not None:
            self.keep().wait()
        self.over_core().wait_recv()

        @pl.loop(0, 2 * PLANES)
        def _(i):
            z, q = i // 2, i % 2
            column = self.column(1 - self.p, q)
            self.to_p[z, q] = self.mine(z, column) + self.from_core[z, column]

        self.over_p().start()

    def third(self):
        self.over_p().wait_recv()

        @pl.loop(0, PLANES)
        def _(z):
            q = 1 - self.q
            total = self.pair_sum(z, self.column(self.p, q)) + self.from_p[z, q].astype(F32)
            self.to_q[z] = total.astype(BF16)

        self.over_q().start()

    def quad_sum(self, z):
        q = self.q
        total = self.pair_sum(z, self.column(self.p, q)) + self.from_p[z, q].astype(F32)
        return total + self.from_q[z].astype(F32)

    def fourth(self):
        self.over_q().wait_recv()
        for step in range(1, PLANES):
            self.to_z[step - 1] = self.quad_sum((self.place.z + step) % PLANES).astype(BF16)
            self.over_z(step).start()

    def fifth(self):
        total = self.quad_sum(self.place.z)
        for step in range(1, PLANES):
            self.over_z(step).wait_recv()
            total = total + self.from_z[step - 1].astype(F32)
        self.finish(total)

    def phases(self):
        return [self.first, self.second, self.third, self.fourth, self.fifth]

    def last(self):
        self.over_core().wait_send()
        self.over_p().wait_send()
        self.over_q().wait_send()
        for step in range(1, PLANES):
            self.over_z(step).wait_send()


FOLD_BUFFERS = ((4, 4), (4, 2), (4, 2), (4,), (4,), (3,), (3,))


class Share:
    SEMAPHORES = 7

    def __init__(self, place, value, out, partial, received, send, receive):
        self.place, self.value, self.out = place, value, out
        self.partial, self.received, self.send, self.receive = partial, received, send, receive

    def swap(self, slot, device):
        return pltpu.make_async_remote_copy(
            src_ref=self.partial.at[min(slot, 3)], dst_ref=self.received.at[slot], send_sem=self.send.at[slot],
            recv_sem=self.receive.at[slot], device_id=(device,), device_id_type=MESH,
        )

    def partners(self):
        place = self.place
        return [place.sibling, place.along_x, place.along_y] + [place.plane(k) for k in range(1, PLANES)]

    def first(self):
        self.partial[0] = self.value[...]
        self.swap(0, self.place.sibling).start()

    def step(self, at):
        partners = self.partners()
        self.swap(at, partners[at]).wait_recv()
        self.partial[at + 1] = self.partial[at] + self.received[at]
        for slot in (at + 1,) if at < 2 else (3, 4, 5):
            self.swap(slot, partners[slot]).start()

    def finish(self):
        partners = self.partners()
        for slot in (3, 4, 5):
            self.swap(slot, partners[slot]).wait_recv()
        place = self.place
        self.received[6] = self.partial[3]
        total = jnp.zeros(self.value.shape, F32)
        for z in range(PLANES):
            behind = (place.z + PLANES - z) % PLANES
            total = total + self.received[(behind + 3) % PLANES + 3]
        self.out[...] = total

    def phases(self):
        return [self.first] + [functools.partial(self.step, at) for at in range(3)] + [self.finish]

    def last(self):
        for slot, partner in enumerate(self.partners()):
            self.swap(slot, partner).wait_send()


GRAD_STEPS = 2 * CHUNKS + 1
FOLDED = ((0, 4), (1, 4), (2, 1))
FOLD_PARTS = sum(pieces for _, pieces in FOLDED)
BACKWARD_PLAN = (
    (5, 0, 0), (5, 1, 0), (5, 2, 0), (5, 3, 0), (6, 4, 0), (7, 5, 0), (8, 6, 0), (9, 0, 1), (9, 7, 0), (9, 8,
    0), (11, 1, 1), (12, 9, 0), (12, 0, 2), (12, 2, 1), (12, 15, 0), (14, 1, 2), (14, 3, 1), (14, 9, 1), (14,
    15, 1), (15, 10, 0), (15, 0, 3), (15, 2, 2), (16, 15, 2), (17, 1, 3), (17, 4, 1), (17, 10, 1), (17, 9, 2),
    (18, 11, 0), (18, 0, 4), (18, 2, 3), (18, 3, 2), (18, 15, 3), (19, 5, 1), (19, 1, 4), (19, 9, 3), (20, 10,
    2), (20, 11, 1), (21, 12, 0), (21, 3, 3), (21, 4, 2), (21, 6, 1), (21, 15, 4), (22, 2, 4), (22, 5, 2), (22,
    9, 4), (22, 10, 3), (22, 11, 2), (23, 12, 1), (24, 13, 0), (24, 3, 4), (24, 4, 3), (24, 7, 1), (24, 10, 4),
    (24, 11, 3), (25, 5, 3), (25, 6, 2), (25, 12, 2), (26, 8, 1), (26, 13, 1), (27, 14, 0), (27, 7, 2), (27, 6,
    3), (27, 11, 4), (27, 12, 3), (28, 4, 4), (29, 5, 4), (30, 8, 2), (30, 13, 2), (30, 14, 1), (30, 16, 0),
    (30, 7, 3), (30, 12, 4), (30, 16, 1), (30, 6, 4), (30, 13, 3), (30, 7, 4), (30, 16, 2), (30, 8, 3), (30, 14,
    2), (30, 13, 4), (30, 16, 3), (30, 14, 3), (30, 8, 4), (30, 16, 4), (30, 14, 4),
)


def fold_parts(shapes):
    parts = []
    for i, pieces in FOLDED:
        rows, width = shapes[i]
        for at in range(pieces):
            if i == 0:
                size = rows // pieces
                parts.append((i, slice(at * size, (at + 1) * size), slice(0, width), (size, width)))
            else:
                size = width // pieces
                parts.append((i, slice(0, rows), slice(at * size, (at + 1) * size), (rows, size)))
    return parts


def backward_kernel(*refs):
    lengths, clips = refs[:2]
    qkv, tqk, logs, dots, d_context, w_triple = refs[2:8]
    (x_hbm, d_res_hbm), (act, d_down, up_in, d_pre, cut, d_attn), sums = refs[8:10], refs[10:16], refs[16]
    input_hbm, grads = refs[17], refs[18:21]
    g_down, g_up, g_out, g_qkv, sums_out, q_sums_out = refs[21:27]
    x, a_in_t, d_pair, d_a, d_res, g_pair, q_sums, ring, stage_tall, stage_wide = refs[27:37]
    scratch = refs[37:]
    rows, tokens = qkv.shape[0], qkv.shape[1]
    place = Place()
    at_step = pl.program_id(0)
    at_pair = at_step - GRAD_STEPS
    parts = fold_parts([g_down.shape, g_up.shape, g_out.shape])
    owns, scratch = scratch[:FOLD_PARTS], scratch[FOLD_PARTS:]
    per = len(FOLD_BUFFERS)
    taken = (FOLD_PARTS + PAIRS) * per
    buffers, (s_partial, s_received, q_partial, q_received, send, receive, load) = scratch[:taken], scratch[taken:]

    def set_part(target, r, c):
        def finish(total):
            target[r, c] = total

        return finish

    def set_triple(pair):
        def finish(total):
            for i in range(3):
                at = D * i + PAIR * pair
                g_qkv[:, at : at + PAIR] = total[:, PAIR * i : PAIR * (i + 1)]

        return finish

    folds = []
    for n, (i, r, c, _) in enumerate(parts):
        target = (g_down, g_up, g_out)[i]
        source = grads[i].at[:, :, :, r, c]
        folds.append(
            Fold(place, source, owns[n], set_part(target, r, c), buffers[per * n : per * n + per], send.at[n], receive.at[n])
        )
    for pair in range(PAIRS):
        n = FOLD_PARTS + pair
        folds.append(
            Fold(
                place, g_pair.at[pair], None, set_triple(pair), buffers[per * n : per * n + per], send.at[n], receive.at[n]
            )
        )
    n = len(folds)
    share = Share(place, sums, sums_out, s_partial, s_received, send.at[n], receive.at[n])
    q_share = Share(place, q_sums, q_sums_out, q_partial, q_received, send.at[n + 1], receive.at[n + 1])
    inputs = [pltpu.make_async_copy(x_hbm, x, load.at[0]), pltpu.make_async_copy(d_res_hbm, d_res, load.at[1])]

    slots = GRAD_STEPS + PAIRS * rows
    phases = [fold.phases() for fold in folds] + [share.phases(), q_share.phases()]
    timed = [
        (slot, phases[i][phase]) for slot, i, phase in BACKWARD_PLAN if phase or not FOLD_PARTS <= i < FOLD_PARTS + PAIRS
    ]

    def stage(slot):
        for when, act in timed:
            if when == slot:
                act()

    def turn(index):
        for slot in sorted({when for when, _ in timed if when < slots}):
            pl.when(index == slot)(functools.partial(stage, slot))

    def load_left(source):
        return pltpu.make_async_copy(source, x, load.at[2])

    def chunk(source, c, step):
        part = source.at[:, :, pl.ds(pl.multiple_of(c * D, D), D)]
        return pltpu.make_async_copy(part, ring.at[step % 2], load.at[3 + step % 2])

    def load_chunk(step):
        pl.when(step < CHUNKS)(lambda: chunk(act, step, step).start())
        pl.when(jnp.logical_and(step >= CHUNKS, step < 2 * CHUNKS))(lambda: chunk(d_pre, step - CHUNKS, step).start())
        pl.when(step == 2 * CHUNKS)(lambda: chunk(d_attn, 0, step).start())

    def tall_out(c):
        return pltpu.make_async_copy(stage_tall, grads[0].at[c], load.at[5])

    def wide_out(c):
        columns = pl.ds(pl.multiple_of(c * D, D), D)
        return pltpu.make_async_copy(stage_wide, grads[1].at[:, :, :, :, columns], load.at[6])

    out_out = pltpu.make_async_copy(stage_wide, grads[2], load.at[6])

    @pl.when(at_step == 0)
    def _():
        load_left(d_down).start()
        load_chunk(0)
        inputs[1].start()
        place.meet()
        q_sums[...] = jnp.zeros_like(q_sums)
        d_a[...] = jnp.zeros_like(d_a)

    @pl.when(at_step < GRAD_STEPS)
    def _():
        turn(at_step)
        for step, following in ((0, up_in), (CHUNKS, cut), (2 * CHUNKS, None)):

            @pl.when(at_step == step)
            def _():
                load_left(d_down).wait()
                a_in_t[...] = x[...].reshape(rows * tokens, D).T
                (inputs[0] if following is None else load_left(following)).start()

        chunk(act, 0, at_step).wait()
        load_chunk(at_step + 1)
        product = nn(a_in_t[...], ring[at_step % 2].reshape(rows * tokens, D))

        @pl.when(at_step < CHUNKS)
        def _():
            pl.when(at_step > 0)(tall_out(0).wait)
            stage_tall[...] = product.T.reshape(stage_tall.shape).astype(BF16)
            tall_out(at_step).start()

        @pl.when(at_step >= CHUNKS)
        def _():
            pl.when(at_step == CHUNKS)(tall_out(0).wait)
            pl.when(at_step > CHUNKS)(wide_out(0).wait)
            height = stage_wide.shape[3]
            for device in range(DEVICES):
                z, column, core = device // 8, device // 2 % COLUMNS, device % CORES
                stage_wide[z, column, core] = product[height * device : height * (device + 1)].astype(BF16)
            pl.when(at_step < 2 * CHUNKS)(lambda: wide_out(at_step - CHUNKS).start())
            pl.when(at_step == 2 * CHUNKS)(out_out.start)

    pl.when(at_step == GRAD_STEPS)(out_out.wait)

    def pair_step():
        one_pair(
            lengths, clips, at_pair, turn, stage, slots, folds, timed, share, q_share, inputs, input_hbm, load,
            qkv, tqk, logs, dots, d_context, w_triple, g_qkv.shape[0], x, a_in_t, d_pair, d_a, d_res, g_pair, q_sums,
        )

    pl.when(at_pair >= 0)(pair_step)


def one_pair(
    lengths, clips, at_pair, turn, stage, slots, folds, timed, share, q_share, inputs, input_hbm, load,
    qkv, tqk, logs, dots, d_context, w_triple, height, x, a_in_t, d_pair, d_a, d_res, g_pair, q_sums,
):
    rows, tokens = qkv.shape[0], qkv.shape[1]

    @pl.loop(0, rows)
    def _(row):
        turn(GRAD_STEPS + at_pair * rows + row)
        queries, keys, values = (qkv[row, :, PAIR * i : PAIR * (i + 1)] for i in range(3))
        t_queries, t_keys = (tqk[row, :, PAIR * i : PAIR * (i + 1)] for i in range(2))
        grads_here = attend_pair_back(
            queries, keys, values, t_queries, t_keys, logs[row, 0], dots[row, 0], d_context[row], lengths[row]
        )
        here = pl.ds(pl.multiple_of(row * tokens, tokens), tokens)
        for i in range(3):
            d_pair[here, PAIR * i : PAIR * (i + 1)] = grads_here[i]

    bound = clips[0]

    @pl.when(at_pair == 0)
    def _():
        inputs[0].wait()
        for row in range(rows):
            clipped = jnp.clip(x[row].astype(F32), -bound, bound)
            a_in_t[:, tokens * row : tokens * (row + 1)] = clipped.T.astype(BF16)

    g_now = nn(a_in_t[...], d_pair[...])
    for device in range(DEVICES):
        z, column, core = device // 8, device // 2 % COLUMNS, device % CORES
        g_pair[at_pair, z, column, core] = g_now[height * device : height * (device + 1)].astype(BF16)
    for pair, fold in enumerate(folds[FOLD_PARTS:]):
        pl.when(at_pair == pair)(fold.first)
    here = pair_columns(at_pair)
    q_sums[Q_QUERY : Q_QUERY + 1, here] = column_sum(d_pair[:, :PAIR].astype(F32))
    q_sums[Q_VALUE : Q_VALUE + 1, here] = column_sum(d_pair[:, 2 * PAIR :].astype(F32))
    d_a[...] += nt(d_pair[...], w_triple[...])

    @pl.when(at_pair == PAIRS - 1)
    def _():
        inputs[1].wait()
        for row in range(rows):
            stage(slots + row)
            value = x[row].astype(F32)
            d_row = d_a[tokens * row : tokens * (row + 1)]
            inside = jnp.where(jnp.abs(value) < bound, 1.0, jnp.where(jnp.abs(value) == bound, 0.5, 0.0))
            outside = (1.0 - inside) * d_row
            q_sums[Q_CLIP : Q_CLIP + 1] += column_sum(jnp.where(value > 0, outside, -outside))
            x[row] = (d_res[row] + d_row * inside).astype(BF16)
        out = pltpu.make_async_copy(x, input_hbm, load.at[0])
        out.start()
        for when, act in timed:
            if when >= slots + rows:
                act()
        for fold in folds:
            fold.last()
        share.last()
        q_share.last()
        out.wait()


def backward_pass(lengths, clips, hidden, qkv, tqk, logs, dots, d_context, d_res, w_qkv, made_by, sums):
    rows, tokens, _ = hidden.shape
    shapes = [(FF // DEVICES, D), (D // DEVICES, FF), (D // DEVICES, D)]
    height = w_qkv.shape[0] // DEVICES
    part_shapes = [part[3] for part in fold_parts(shapes)]
    fold_shapes = part_shapes + [(height, TRIPLE)] * PAIRS
    anywhere = pl.BlockSpec(memory_space=pl.ANY)

    def of_pair(width):
        return pl.BlockSpec((rows, tokens, width), lambda s: (0, 0, pair_at(s)))

    def pair_at(step):
        return step // GRAD_STEPS * (step - GRAD_STEPS)

    stat = pl.BlockSpec((rows, 1, 2, tokens), lambda s: (0, pair_at(s), 0, 0))
    small = [shaped(sums.shape, F32), shaped((Q_ROWS, D), F32)]
    made = [shaped(s, F32) for s in shapes] + [shaped((height, 3 * D), F32)] + small
    return pl.pallas_call(
        backward_kernel,
        grid=(GRAD_STEPS + PAIRS,),
        in_specs=[smem_spec(), smem_spec()]
        + [of_pair(TRIPLE), of_pair(DOUBLE), stat, stat, of_pair(PAIR), pl.BlockSpec((D, TRIPLE), lambda s: (0, pair_at(s)))]
        + [anywhere] * 8
        + [whole_spec(sums.shape)],
        out_specs=[anywhere] * 4 + [whole_spec(m.shape) for m in made],
        out_shape=[shaped(hidden.shape, BF16)]
        + [shaped((PLANES, COLUMNS, CORES) + shape, BF16) for shape in shapes]
        + made,
        scratch_shapes=[
            pltpu.VMEM((rows, tokens, D), BF16),
            pltpu.VMEM((D, rows * tokens), BF16),
            pltpu.VMEM((rows * tokens, TRIPLE), BF16),
            pltpu.VMEM((rows * tokens, D), F32),
            pltpu.VMEM((rows, tokens, D), F32),
            pltpu.VMEM((PAIRS, PLANES, COLUMNS, CORES, height, TRIPLE), BF16),
            pltpu.VMEM((Q_ROWS, D), F32),
            pltpu.VMEM((2, rows, tokens, D), BF16),
            pltpu.VMEM((COLUMNS, CORES) + shapes[0], BF16),
            pltpu.VMEM((PLANES, COLUMNS, CORES) + shapes[2], BF16),
        ]
        + [pltpu.VMEM((PLANES, COLUMNS) + s, BF16) for s in part_shapes]
        + [pltpu.VMEM(lead + s, BF16) for s in fold_shapes for lead in FOLD_BUFFERS]
        + [pltpu.VMEM((n,) + m.shape, F32) for m in small for n in (4, 7)]
        + [pltpu.SemaphoreType.DMA((len(fold_shapes) + 2, Fold.SEMAPHORES))] * 2
        + [pltpu.SemaphoreType.DMA((7,))],
        compiler_params=params(collective_id=1, has_side_effects=True),
    )(
        lengths, clips, qkv, tqk, logs, dots, d_context, w_qkv, hidden, d_res, *made_by, sums
    )


def finish_kernel(sums, q_sums, *refs):
    grads, input_hbm = refs[:4], refs[4]
    outs, input_out = refs[5:9], refs[9]
    b_q, b_v, b_out, b_up, b_down, gain_one, shift_one, gain_two, shift_two, clips = refs[10:20]
    held, arrive = refs[20:]
    copy = pltpu.make_async_copy(input_hbm, held, arrive)
    copy.start()

    def row(ref, at):
        return ref[at : at + 1].reshape(D)

    for source, target in zip(grads, outs):
        target[...] = source[...]
    b_q[...] = row(q_sums, Q_QUERY)
    b_v[...] = row(q_sums, Q_VALUE)
    b_out[...] = row(sums, S_OUT)
    b_up[...] = jnp.concatenate([sums[S_UP + c : S_UP + c + 1] for c in range(CHUNKS)], axis=1).reshape(FF)
    b_down[...] = row(sums, S_DOWN)
    gain_one[...] = row(sums, S_GAIN_ONE)
    shift_one[...] = row(sums, S_SHIFT_ONE)
    gain_two[...] = row(sums, S_GAIN_TWO)
    shift_two[...] = row(sums, S_SHIFT_TWO)
    clips[0] = jnp.sum(q_sums[Q_CLIP : Q_CLIP + 1])
    for i, at in enumerate((S_CLIP_ONE, S_CLIP_TWO, S_CLIP_THREE)):
        clips[1 + i] = jnp.sum(sums[at : at + 1])
    copy.wait()
    back = pltpu.make_async_copy(held, input_out, arrive)
    back.start()
    back.wait()


def finish(sums, q_sums, grads, input_grad):
    vmem, anywhere = pl.BlockSpec(memory_space=pltpu.VMEM), pl.BlockSpec(memory_space=pl.ANY)
    lengths = [D, D, D, FF, D, D, D, D, D]
    return pl.pallas_call(
        finish_kernel,
        in_specs=[vmem] * 6 + [anywhere],
        out_specs=[vmem] * 4 + [anywhere] + [vmem] * 9 + [smem_spec()],
        out_shape=[shaped(g.shape, F32) for g in grads]
        + [shaped(input_grad.shape, BF16)]
        + [shaped((n,), F32) for n in lengths]
        + [shaped((4,), F32)],
        scratch_shapes=[pltpu.VMEM(input_grad.shape, BF16), pltpu.SemaphoreType.DMA],
        compiler_params=params(),
    )(sums, q_sums, *grads, input_grad)


def on_device(
    by_kernel,
    hidden, teacher_input, cotangent, lengths, lat_qkv, lat_out, lat_up, lat_down,
    bias_q, bias_v, bias_out, bias_up, bias_down, gain_one, shift_one, gain_two, shift_two, clips,
    teach_qkv, teach_out, teach_up, teach_down,
):
    latent = (lat_qkv, lat_out, lat_up, lat_down)
    teach = (teach_qkv, teach_out, teach_up, teach_down)
    if by_kernel:
        (w_qkv, *weights), (tqk, final, qkv, context, logs) = forward_pass(
            lengths, clips, teacher_input, hidden, teach, latent, bias_q, bias_v
        )
    else:
        gather = functools.partial(lax.all_gather, axis_name="shard", axis=0, tiled=True)
        w_qkv, *weights = (gather(signed_mean(w)) for w in latent)
        w_qkv = by_pairs(w_qkv)
        t_qkv, *t_weights = (gather(w) for w in teach)
        tqk, final = teacher_pass(lengths, teacher_input, by_pairs(t_qkv), *t_weights)
        qkv, context, logs = student_attend(lengths, clips, hidden, w_qkv, bias_q, bias_v)
    vectors = (bias_out, bias_up, bias_down, gain_one, shift_one, gain_two, shift_two)
    mixed, act, d_pre, up_in, d_down, cut, d_attn, d_res, d_context, dots, sums = student_middle(
        lengths, clips, hidden, cotangent, final, context, weights, vectors
    )
    made_by = (act, d_down, up_in, d_pre, cut, d_attn)
    if by_kernel:
        input_grad, _, _, _, g_down, g_up, g_out, g_qkv, sums, q_sums = backward_pass(
            lengths, clips, hidden, qkv, tqk, logs, dots, d_context, d_res, w_qkv, made_by, sums
        )
    else:
        g_down, g_up, g_out = weight_grads(*made_by)
        input_grad, g_qkv, q_sums = student_back(lengths, clips, hidden, qkv, tqk, logs, dots, d_context, d_res, w_qkv)
        scatter = functools.partial(lax.psum_scatter, axis_name="shard", scatter_dimension=0, tiled=True)
        g_down, g_up, g_qkv, g_out = (scatter(g.astype(F32)) for g in (g_down, g_up, by_kinds(g_qkv), g_out))
        sums, q_sums = lax.psum((sums, q_sums), "shard")
    g_qkv, g_out, g_up, g_down, input_grad, *small = finish(sums, q_sums, (g_qkv, g_out, g_up, g_down), input_grad)
    return mixed, input_grad, g_qkv, g_out, g_up, g_down, *small


def solution(mesh):
    split, rows, same = P("shard", None), P("shard", None, None), P()
    return jax.shard_map(
        functools.partial(on_device, mesh.shape["shard"] == DEVICES),
        mesh=mesh,
        in_specs=(rows, rows, rows, P("shard")) + (split,) * 4 + (same,) * 10 + (split,) * 4,
        out_specs=(rows, rows) + (split,) * 4 + (same,) * 10,
        check_vma=False,
    )
```

```python
import functools
import math

import jax
import jax.numpy as jnp
from jax import lax
from jax.experimental import pallas as pl
from jax.experimental.pallas import tpu as pltpu
from jax.sharding import PartitionSpec as P

D = 768
FF = 3072
HEAD_DIM = 64
PAIR = 2 * HEAD_DIM
PAIRS = D // PAIR
DOUBLE, TRIPLE = 2 * PAIR, 3 * PAIR
CHUNKS = FF // D

EPSILON = 1e-05
MASKED = -1000000000.0
SCALE = 1.0 / math.sqrt(HEAD_DIM)

F32 = jnp.float32
BF16 = jnp.bfloat16
MESH = pl.DeviceIdType.MESH
VMEM_LIMIT = 63 * 1024 * 1024


def nn(left, right):
    return lax.dot_general(left, right, (((1,), (0,)), ((), ())), preferred_element_type=F32)


def nt(left, right):
    return lax.dot_general(left, right, (((1,), (1,)), ((), ())), preferred_element_type=F32)


def tn(left, right):
    return lax.dot_general(left, right, (((0,), (0,)), ((), ())), preferred_element_type=F32)


def signed_mean(latent):
    factor = jnp.mean(jnp.abs(latent), axis=1, keepdims=True)
    sign = jnp.where(latent > 0, 1.0, jnp.where(latent < 0, -1.0, 0.0))
    return (factor * sign).astype(BF16)


def normalize(value):
    center = value - jnp.mean(value, axis=-1, keepdims=True)
    inverse = lax.rsqrt(jnp.mean(center * center, axis=-1, keepdims=True) + EPSILON)
    return center * inverse, inverse


def norm_back(d_normed, normed, inverse):
    first = jnp.mean(d_normed, axis=-1, keepdims=True)
    second = jnp.mean(d_normed * normed, axis=-1, keepdims=True)
    return inverse * (d_normed - first - normed * second)


def normal_cdf(value):
    return 0.5 * (1.0 + lax.erf(value * (1.0 / math.sqrt(2.0))))


def column_sum(value):
    return jnp.sum(value, axis=0, keepdims=True)


def head_halves(pair):
    first = lax.broadcasted_iota(jnp.int32, pair.shape, 1) < HEAD_DIM
    zero = jnp.zeros_like(pair)
    return jnp.where(first, pair, zero), jnp.where(first, zero, pair)


def mask_columns(tokens, length):
    shape = (tokens, PAIR)
    first = lax.broadcasted_iota(jnp.int32, shape, 1) == 0
    dead = jnp.logical_and(first, lax.broadcasted_iota(jnp.int32, shape, 0) >= length)
    return jnp.where(dead, MASKED, 0.0).astype(BF16), jnp.where(first, 1.0, 0.0).astype(BF16)


def attend_pair(queries, keys, values, length):
    values_t = values.T
    beside_keys, beside_queries = mask_columns(queries.shape[0], length)
    wide_keys = jnp.concatenate([keys, beside_keys], axis=1)
    contexts, log_totals = [], []
    for head, one in enumerate(head_halves(queries)):
        masked = nt(wide_keys, jnp.concatenate([one, beside_queries], axis=1))
        top = jnp.max(masked, axis=0, keepdims=True)
        expo = jnp.exp(masked - top)
        total = jnp.sum(expo, axis=0, keepdims=True)
        probs = (expo * (1.0 / total)).astype(BF16)
        contexts.append(nn(values_t[HEAD_DIM * head : HEAD_DIM * (head + 1)], probs))
        log_totals.append(top + jnp.log(total))
    return jnp.concatenate(contexts, axis=0).T, jnp.concatenate(log_totals, axis=0)


def attend_pair_back(queries, keys, values, t_queries, t_keys, log_totals, row_dots, d_context, length):
    tokens = queries.shape[0]
    beside_keys, beside_queries = mask_columns(tokens, length)
    wide_keys = jnp.concatenate([keys, beside_keys], axis=1)
    live = lax.broadcasted_iota(jnp.int32, (tokens, DOUBLE), 0) < length
    both_keys = jnp.where(live, jnp.concatenate([keys, -t_keys], axis=1), 0.0).astype(BF16)
    share = jnp.where(live, 1.0 / tokens, 0.0).astype(BF16)
    keys_t = keys.T
    d_queries, d_keys, d_values = [], [], []
    heads = zip(head_halves(queries), head_halves(d_context), head_halves(t_queries))
    for head, (one, d_one, t_one) in enumerate(heads):
        masked = nt(wide_keys, jnp.concatenate([one, beside_queries], axis=1))
        extra = nt(both_keys, jnp.concatenate([one, t_one], axis=1) * share)
        probs = jnp.exp(masked - log_totals[head : head + 1])
        d_probs = nt(values, d_one)
        d_values.append(nn(probs.astype(BF16), d_one))
        d_scores = (probs * (d_probs - row_dots[head : head + 1]) + extra).astype(BF16)
        d_keys.append(nn(d_scores, one))
        d_queries.append(nn(keys_t[HEAD_DIM * head : HEAD_DIM * (head + 1)], d_scores))
    d_q = (jnp.concatenate(d_queries, axis=0).T * SCALE).astype(BF16)
    return d_q, (d_keys[0] + d_keys[1]).astype(BF16), (d_values[0] + d_values[1]).astype(BF16)


def pair_columns(pair, width=PAIR):
    return pl.ds(pl.multiple_of(pair * width, PAIR), width)


def by_pairs(matrix):
    split = matrix.reshape(matrix.shape[0], 3, PAIRS, PAIR)
    return split.transpose(0, 2, 1, 3).reshape(matrix.shape[0], 3 * D)


def by_kinds(matrix):
    split = matrix.reshape(matrix.shape[0], PAIRS, 3, PAIR)
    return split.transpose(0, 2, 1, 3).reshape(matrix.shape[0], 3 * D)


def teacher_pair(pair, x, length, w_qkv, tqk_ref, context_ref):
    joined = nn(x, w_qkv[:, pair_columns(pair, TRIPLE)]).astype(BF16)
    queries, keys, values = (joined[:, PAIR * i : PAIR * (i + 1)] for i in range(3))
    queries = (queries.astype(F32) * SCALE).astype(BF16)
    tqk_ref[:, pair_columns(pair, DOUBLE)] = jnp.concatenate([queries, keys], axis=1)
    mixed, _ = attend_pair(queries, keys, values, length)
    context_ref[:, pair_columns(pair)] = mixed.astype(BF16)


def teacher_last(x, context, w_out, w_up, w_down, between):
    first, _ = normalize(x.astype(F32) + nn(context, w_out[...]))
    first_low = first.astype(BF16)
    total = first
    for c in range(CHUNKS):
        between(c)
        inner = nn(first_low, w_up[:, D * c : D * (c + 1)])
        total = total + nn((inner * normal_cdf(inner)).astype(BF16), w_down[D * c : D * (c + 1), :])
    return normalize(total)[0]


def student_pair(pair, a_in, length, w_qkv, bias_q, bias_v, qkv_ref, context_ref, log_ref):
    joined = nn(a_in, w_qkv[:, pair_columns(pair, TRIPLE)])
    queries = (joined[:, :PAIR] + bias_q[:, pair_columns(pair)]).astype(BF16)
    queries = (queries.astype(F32) * SCALE).astype(BF16)
    keys = joined[:, PAIR:DOUBLE].astype(BF16)
    values = (joined[:, DOUBLE:] + bias_v[:, pair_columns(pair)]).astype(BF16)
    qkv_ref[:, pair_columns(pair, TRIPLE)] = jnp.concatenate([queries, keys, values], axis=1)
    mixed, log_totals = attend_pair(queries, keys, values, length)
    context_ref[:, pair_columns(pair)] = mixed
    log_ref[pair] = log_totals


def teacher_kernel(lengths, x_ref, w_qkv, w_out, w_up, w_down, tqk_ref, final_ref, context):
    length = lengths[pl.program_id(0)]

    @pl.loop(0, PAIRS)
    def _(pair):
        teacher_pair(pair, x_ref[0], length, w_qkv, tqk_ref.at[0], context)

    final_ref[0] = teacher_last(x_ref[0], context[...], w_out, w_up, w_down, lambda c: None)


def student_attend_kernel(lengths, clips, x_ref, w_qkv, bias_q, bias_v, qkv_ref, context_ref, log_ref, a_in):
    length = lengths[pl.program_id(0)]
    a_in[...] = jnp.clip(x_ref[0].astype(F32), -clips[0], clips[0]).astype(BF16)

    @pl.loop(0, PAIRS)
    def _(pair):
        student_pair(
            pair, a_in[...], length, w_qkv, bias_q, bias_v, qkv_ref.at[0], context_ref.at[0], log_ref.at[0]
        )


(S_OUT, S_UP, S_DOWN, S_GAIN_ONE, S_SHIFT_ONE, S_GAIN_TWO, S_SHIFT_TWO, S_CLIP_ONE, S_CLIP_TWO, S_CLIP_THREE) = (
    0, 1, 5, 6, 7, 8, 9, 10, 11, 12,
)
S_ROWS = 16
(Q_QUERY, Q_VALUE, Q_CLIP) = (0, 1, 2)
Q_ROWS = 8
ABOVE, BELOW = 4.0, -4.0


def student_middle_kernel(
    lengths, clips, x_ref, cotangent_ref, final_ref, context_ref, w_out, w_up, w_down,
    bias_out, bias_up, bias_down, gain_one, shift_one, gain_two, shift_two,
    mixed_ref, act_ref, d_pre_ref, up_in_ref, d_down_ref, cut_ref, d_attn_ref, d_res_ref, d_context_ref, dots_ref,
    sums_ref, slope,
):
    block = x_ref.shape[1]
    row, part = pl.program_id(0), pl.program_id(1)
    length = lengths[row] - part * block

    @pl.when(jnp.logical_and(row == 0, part == 0))
    def _():
        sums_ref[...] = jnp.zeros_like(sums_ref)

    def add(at, value):
        sums_ref[at : at + 1] += value

    def vector(ref):
        return ref[...].reshape(1, ref.shape[0])

    cut = jnp.clip(context_ref[0], -clips[1], clips[1]).astype(BF16)
    cut_ref[0] = cut
    normed_one, inverse_one = normalize(x_ref[0].astype(F32) + nn(cut, w_out[...]) + vector(bias_out))
    h_one = normed_one * vector(gain_one) + vector(shift_one)
    up_in = jnp.clip(h_one, -clips[2], clips[2]).astype(BF16)
    up_in_ref[0] = up_in
    total = h_one + vector(bias_down)
    for c in range(CHUNKS):
        columns = slice(D * c, D * (c + 1))
        pre = nn(up_in, w_up[:, columns]) + vector(bias_up)[:, columns]
        cdf = normal_cdf(pre)
        value = pre * cdf
        rise = cdf + pre * jnp.exp(-0.5 * pre * pre) * (1.0 / math.sqrt(2.0 * math.pi))
        rise = jnp.where(value > clips[3], ABOVE, jnp.where(value < -clips[3], BELOW, rise))
        slope[:, columns] = rise
        act = jnp.clip(value, -clips[3], clips[3]).astype(BF16)
        act_ref[0, :, columns] = act
        total = total + nn(act, w_down[columns, :])
    normed_two, inverse_two = normalize(total)
    out = normed_two * vector(gain_two) + vector(shift_two)
    mixed_ref[0] = out.astype(BF16)
    live = lax.broadcasted_iota(jnp.int32, (block, 1), 0) < length
    d_out = jnp.where(live, cotangent_ref[0].astype(F32) + out - final_ref[0], 0.0)
    add(S_GAIN_TWO, column_sum(d_out * normed_two))
    add(S_SHIFT_TWO, column_sum(d_out))
    d_res_two = norm_back(d_out * vector(gain_two), normed_two, inverse_two)
    d_down = d_res_two.astype(BF16)
    d_down_ref[0] = d_down
    add(S_DOWN, column_sum(d_down.astype(F32)))
    d_up_in = jnp.zeros((block, D), F32)
    for c in range(CHUNKS):
        columns = slice(D * c, D * (c + 1))
        d_act = nt(d_down, w_down[columns, :])
        rise = slope[:, columns]
        above, below = rise > 2.0, rise < -2.0
        d_pre = jnp.where(jnp.logical_or(above, below), 0.0, rise * d_act).astype(BF16)
        d_pre_ref[0, :, columns] = d_pre
        add(S_CLIP_THREE, column_sum(jnp.where(above, d_act, jnp.where(below, -d_act, 0.0))))
        add(S_UP + c, column_sum(d_pre.astype(F32)))
        d_up_in = d_up_in + nt(d_pre, w_up[:, columns])
    above, below = h_one > clips[2], h_one < -clips[2]
    add(S_CLIP_TWO, column_sum(jnp.where(above, d_up_in, jnp.where(below, -d_up_in, 0.0))))
    d_h_one = d_res_two + jnp.where(jnp.abs(h_one) < clips[2], d_up_in, 0.0)
    add(S_GAIN_ONE, column_sum(d_h_one * normed_one))
    add(S_SHIFT_ONE, column_sum(d_h_one))
    d_res_one = norm_back(d_h_one * vector(gain_one), normed_one, inverse_one)
    d_res_ref[0] = d_res_one
    d_attn = d_res_one.astype(BF16)
    d_attn_ref[0] = d_attn
    add(S_OUT, column_sum(d_attn.astype(F32)))
    d_cut = nt(d_attn, w_out[...])
    context = context_ref[0]
    above, below = context > clips[1], context < -clips[1]
    add(S_CLIP_ONE, column_sum(jnp.where(above, d_cut, jnp.where(below, -d_cut, 0.0))))
    d_context = jnp.where(jnp.abs(context) < clips[1], d_cut, 0.0).astype(BF16)
    d_context_ref[0] = d_context
    product = d_context.astype(F32) * context
    high = product.astype(BF16)
    low = (product - high.astype(F32)).astype(BF16)
    shape = (S_ROWS, D)
    heads = lax.broadcasted_iota(jnp.int32, shape, 1) // HEAD_DIM == lax.broadcasted_iota(jnp.int32, shape, 0)
    ones = heads.astype(F32).astype(BF16)
    dots = nt(ones, high) + nt(ones, low)
    for pair in range(PAIRS):
        dots_ref[0, pair] = dots[2 * pair : 2 * pair + 2]


def weight_grads_kernel(act, d_down, up_in, d_pre, cut, d_attn, g_down, g_up, g_out):
    g_down[...] = tn(act[...], d_down[...]).astype(BF16)
    g_up[...] = tn(up_in[...], d_pre[...]).astype(BF16)

    @pl.when(pl.program_id(0) == 0)
    def _():
        g_out[...] = tn(cut[...], d_attn[...]).astype(BF16)


def student_back_kernel(
    lengths, clips, x_ref, qkv_ref, tqk_ref, log_ref, dots_ref, d_context_ref, d_res_ref, w_qkv,
    input_ref, g_qkv, sums_ref, a_in, d_joined,
):
    row = pl.program_id(0)
    tokens = x_ref.shape[1]
    length = lengths[row]
    here = pl.ds(pl.multiple_of(row * tokens, tokens), tokens)

    @pl.when(row == 0)
    def _():
        sums_ref[...] = jnp.zeros_like(sums_ref)

    @pl.loop(0, PAIRS)
    def _(pair):
        queries, keys, values = (qkv_ref[0, :, pair_columns(3 * pair + i)] for i in range(3))
        t_queries, t_keys = (tqk_ref[0, :, pair_columns(2 * pair + i)] for i in range(2))
        d_context = d_context_ref[0, :, pair_columns(pair)]
        grads = attend_pair_back(
            queries, keys, values, t_queries, t_keys, log_ref[0, pair], dots_ref[0, pair], d_context, length
        )
        for i in range(3):
            d_joined[here, pair_columns(3 * pair + i)] = grads[i]
        for i, at in ((0, Q_QUERY), (2, Q_VALUE)):
            sums_ref[at : at + 1, pair_columns(pair)] += column_sum(grads[i].astype(F32))

    bound = clips[0]
    x = x_ref[0].astype(F32)
    a_in[here, :] = jnp.clip(x, -bound, bound).astype(BF16)
    d_a = nt(d_joined[here, :], w_qkv[...])
    inside = jnp.where(jnp.abs(x) < bound, 1.0, jnp.where(jnp.abs(x) == bound, 0.5, 0.0))
    input_ref[0] = (d_res_ref[0] + d_a * inside).astype(BF16)
    outside = (1.0 - inside) * d_a
    sums_ref[Q_CLIP : Q_CLIP + 1] += column_sum(jnp.where(x > 0, outside, -outside))

    @pl.when(row == pl.num_programs(0) - 1)
    def _():
        for i in range(3):
            g_qkv[:, D * i : D * (i + 1)] = tn(a_in[...], d_joined[:, D * i : D * (i + 1)]).astype(BF16)


def rows_spec(tokens, width):
    return pl.BlockSpec((1, tokens, width), lambda r, *_: (r, 0, 0))


def whole_spec(shape):
    return pl.BlockSpec(shape, lambda *_: (0,) * len(shape), pipeline_mode=pl.Buffered(1))


def smem_spec():
    return pl.BlockSpec(memory_space=pltpu.SMEM)


def params(**more):
    return pltpu.CompilerParams(vmem_limit_bytes=VMEM_LIMIT, **more)


def shaped(shape, dtype):
    return jax.ShapeDtypeStruct(shape, dtype)


def teacher_pass(lengths, x, w_qkv, w_out, w_up, w_down):
    rows, tokens, _ = x.shape
    return pl.pallas_call(
        teacher_kernel,
        grid=(rows,),
        in_specs=[smem_spec(), rows_spec(tokens, D)] + [whole_spec(w.shape) for w in (w_qkv, w_out, w_up, w_down)],
        out_specs=[rows_spec(tokens, 2 * D), rows_spec(tokens, D)],
        out_shape=[shaped((rows, tokens, 2 * D), BF16), shaped((rows, tokens, D), F32)],
        scratch_shapes=[pltpu.VMEM((tokens, D), BF16)],
        compiler_params=params(),
    )(lengths, x, w_qkv, w_out, w_up, w_down)


def student_attend(lengths, clips, x, w_qkv, bias_q, bias_v):
    rows, tokens, _ = x.shape
    logs = (1, PAIRS, 2, tokens)
    return pl.pallas_call(
        student_attend_kernel,
        grid=(rows,),
        in_specs=[smem_spec(), smem_spec(), rows_spec(tokens, D), whole_spec(w_qkv.shape)] + [whole_spec((1, D))] * 2,
        out_specs=[
            rows_spec(tokens, 3 * D),
            rows_spec(tokens, D),
            pl.BlockSpec(logs, lambda r: (r, 0, 0, 0)),
        ],
        out_shape=[
            shaped((rows, tokens, 3 * D), BF16),
            shaped((rows, tokens, D), F32),
            shaped((rows,) + logs[1:], F32),
        ],
        scratch_shapes=[pltpu.VMEM((tokens, D), BF16)],
        compiler_params=params(),
    )(lengths, clips, x, w_qkv, bias_q.reshape(1, D), bias_v.reshape(1, D))


def student_middle(lengths, clips, x, cotangent, final, context, weights, vectors):
    rows, tokens, _ = x.shape
    block = tokens // 2 if tokens % 32 == 0 else tokens
    wide = {"act": FF, "d_pre": FF}
    names = ("mixed", "act", "d_pre", "up_in", "d_down", "cut", "d_attn", "d_res", "d_context")

    def spec(width):
        return pl.BlockSpec((1, block, width), lambda r, i: (r, i, 0))

    return pl.pallas_call(
        student_middle_kernel,
        grid=(rows, tokens // block),
        in_specs=[smem_spec(), smem_spec()]
        + [spec(D)] * 4
        + [whole_spec(w.shape) for w in (*weights, *vectors)],
        out_specs=[spec(wide.get(name, D)) for name in names]
        + [pl.BlockSpec((1, PAIRS, 2, block), lambda r, i: (r, 0, 0, i)), whole_spec((S_ROWS, D))],
        out_shape=[
            shaped((rows, tokens, wide.get(name, D)), F32 if name == "d_res" else BF16) for name in names
        ]
        + [shaped((rows, PAIRS, 2, tokens), F32), shaped((S_ROWS, D), F32)],
        scratch_shapes=[pltpu.VMEM((block, FF), F32)],
        compiler_params=params(),
    )(lengths, clips, x, cotangent, final, context, *weights, *vectors)


def weight_grads(act, d_down, up_in, d_pre, cut, d_attn):
    flat = [v.reshape(-1, v.shape[-1]) for v in (act, d_down, up_in, d_pre, cut, d_attn)]
    tokens = flat[0].shape[0]
    chunk = pl.BlockSpec((tokens, D), lambda c: (0, c))
    same = whole_spec((tokens, D))
    return pl.pallas_call(
        weight_grads_kernel,
        grid=(CHUNKS,),
        in_specs=[chunk, same, same, chunk, same, same],
        out_specs=[
            pl.BlockSpec((D, D), lambda c: (c, 0)),
            pl.BlockSpec((D, D), lambda c: (0, c)),
            whole_spec((D, D)),
        ],
        out_shape=[shaped((FF, D), BF16), shaped((D, FF), BF16), shaped((D, D), BF16)],
        compiler_params=params(),
    )(*flat)


def student_back(lengths, clips, x, qkv, tqk, logs, dots, d_context, d_res, w_qkv):
    rows, tokens, _ = x.shape
    return pl.pallas_call(
        student_back_kernel,
        grid=(rows,),
        in_specs=[smem_spec(), smem_spec(), rows_spec(tokens, D), rows_spec(tokens, 3 * D), rows_spec(tokens, 2 * D)]
        + [pl.BlockSpec((1,) + logs.shape[1:], lambda r: (r, 0, 0, 0))] * 2
        + [rows_spec(tokens, D), rows_spec(tokens, D), whole_spec(w_qkv.shape)],
        out_specs=[rows_spec(tokens, D), whole_spec((D, 3 * D)), whole_spec((Q_ROWS, D))],
        out_shape=[shaped((rows, tokens, D), BF16), shaped((D, 3 * D), BF16), shaped((Q_ROWS, D), F32)],
        scratch_shapes=[pltpu.VMEM((rows * tokens, D), BF16), pltpu.VMEM((rows * tokens, 3 * D), BF16)],
        compiler_params=params(),
    )(lengths, clips, x, qkv, tqk, logs, dots, d_context, d_res, w_qkv)


PLANES, COLUMNS, CORES = 4, 4, 2
DEVICES = PLANES * COLUMNS * CORES


class Place:
    def __init__(self):
        self.me = lax.axis_index("shard")
        self.core = self.me % 2
        self.x = (self.me // 2) % 2
        self.y = (self.me // 4) % 2
        self.z = self.me // 8
        self.column = (self.me // 2) % 4
        self.along_x = self.me + 2 - 4 * self.x
        self.along_y = self.me + 4 - 8 * self.y
        self.sibling = self.me + 1 - 2 * self.core
        self.along_a = self.along_x + (self.along_y - self.along_x) * self.core
        self.along_b = self.along_y + (self.along_x - self.along_y) * self.core

    def plane(self, step):
        return (self.me + 8 * step) % DEVICES

    def meet(self):
        partners = [self.sibling, self.along_x, self.along_y] + [self.plane(k) for k in range(1, PLANES)]
        barrier = pltpu.get_barrier_semaphore()
        for partner in partners:
            pl.semaphore_signal(barrier, inc=1, device_id=(partner,), device_id_type=MESH)
        return functools.partial(pl.semaphore_wait, barrier, len(partners))


class Trip:
    SEMAPHORES = 14

    def __init__(self, place, source, out, rows, columns, early, send, receive):
        self.place, self.early, self.send, self.receive = place, early, send, receive
        self.source = source.at[rows, columns]
        height, size = source.shape[0], rows.stop - rows.start

        def where(column):
            start = pl.multiple_of(height * (column % CORES) + rows.start, 8)
            return column // CORES, pl.ds(start, size)

        def one(z, column):
            chip, inside = where(column)
            return out.at[z, chip, inside, columns]

        def slab_of(column):
            chip, inside = where(column)
            return out.at[:, chip, inside, columns]

        self.one, self.all = one, slab_of
        self.mine = place.me % 8
        self.at_a = self.mine + place.along_a - place.me
        self.at_b = self.mine + place.along_b - place.me
        self.at_ab = self.at_a + self.at_b - self.mine

    def remote(self, source, target, slot, device):
        return pltpu.make_async_remote_copy(
            src_ref=source, dst_ref=target, send_sem=self.send.at[slot], recv_sem=self.receive.at[slot],
            device_id=(device,), device_id_type=MESH,
        )

    def own(self):
        return pltpu.make_async_copy(self.source, self.one(self.place.z, self.mine), self.send.at[0])

    def line(self, step, source, column, slot):
        return self.remote(source, self.one(self.place.z, column), slot, self.place.plane(step))

    def line_from(self, step, column, slot):
        part = self.one((self.place.z + PLANES - step) % PLANES, column)
        return self.remote(part, part, slot, self.place.plane(step))

    def slab(self, column, slot, device):
        part = self.all(column)
        return self.remote(part, part, slot, device)

    def across(self, source, column):
        return self.remote(source, self.one(self.place.z, column), 4, self.place.along_a)

    def first(self):
        self.own().start()
        if self.early:
            self.across(self.source, self.mine).start()
        for step in range(1, PLANES):
            self.line(step, self.source, self.mine, step).start()

    def second(self):
        place = self.place
        self.own().wait()
        if self.early:
            part = self.one(place.z, self.at_a)
            self.across(part, self.at_a).wait_recv()
            for step in range(1, PLANES):
                self.line(step, part, self.at_a, 10 + step).start()
            return
        for step in range(1, PLANES):
            self.line_from(step, self.mine, step).wait_recv()
        self.slab(self.mine, 4, place.along_a).start()
        self.slab(self.mine, 5, place.along_b).start()
        self.slab(self.mine, 7, place.sibling).start()

    def third(self):
        place = self.place
        if self.early:
            for step in range(1, PLANES):
                self.line_from(step, self.mine, step).wait_recv()
                self.line_from(step, self.at_a, 10 + step).wait_recv()
            self.slab(self.mine, 5, place.along_b).start()
            self.slab(self.mine, 7, place.sibling).start()
        else:
            self.slab(self.at_a, 4, place.along_a).wait_recv()
        self.slab(self.at_a, 6, place.along_b).start()
        self.slab(self.at_a, 8, place.sibling).start()

    def fourth(self):
        place = self.place
        self.slab(self.at_b, 5, place.along_b).wait_recv()
        self.slab(self.at_b, 9, place.sibling).start()
        self.slab(self.at_ab, 6, place.along_b).wait_recv()
        self.slab(self.at_ab, 10, place.sibling).start()

    def fifth(self):
        for slot in range(7, 11):
            self.slab(self.mine, slot, self.place.sibling).wait_recv()

    def phases(self):
        return [self.first, self.second, self.third, self.fourth, self.fifth]

    def last(self):
        one = self.one(self.place.z, self.mine)
        for step in range(1, PLANES):
            self.line(step, one, self.mine, step).wait_send()
            if self.early:
                self.line(step, one, self.mine, 10 + step).wait_send()
        if self.early:
            self.across(one, self.mine).wait_send()
        for slot in range(5 if self.early else 4, 11):
            self.slab(self.mine, slot, self.place.sibling).wait_send()


T_QKV, T_OUT, T_UP, T_DOWN, B_QKV, B_OUT, B_UP, B_DOWN = range(8)
TRAVEL = ((T_QKV, 6), (B_QKV, 2), (T_DOWN, 2), (T_OUT, 1), (T_UP, 2), (B_OUT, 1), (B_DOWN, 1), (B_UP, 2))
EARLY = (T_OUT, B_OUT, B_UP,)
TALL = (T_DOWN, B_DOWN)
FORWARD_PLAN = (
    (0, 0, 0), (0, 1, 0), (0, 2, 0), (0, 3, 0), (0, 0, 1), (0, 4, 0), (0, 1, 1), (0, 5, 0), (0, 2, 1), (0, 6,
    0), (0, 0, 2), (0, 3, 1), (0, 1, 2), (0, 4, 1), (0, 2, 2), (0, 5, 1), (0, 0, 3), (0, 7, 0), (0, 3, 2), (0,
    6, 1), (0, 1, 3), (0, 0, 4), (0, 2, 3), (0, 4, 2), (0, 5, 2), (0, 8, 0), (0, 3, 3), (0, 1, 4), (1, 7, 1),
    (2, 2, 4), (2, 3, 4), (2, 6, 2), (3, 4, 3), (3, 5, 3), (3, 9, 0), (4, 8, 1), (5, 4, 4), (5, 5, 4), (5, 7,
    2), (6, 6, 3), (6, 10, 0), (8, 6, 4), (8, 9, 1), (8, 11, 0), (9, 10, 1), (10, 7, 3), (10, 8, 2), (13, 7, 4),
    (13, 12, 0), (14, 9, 2), (14, 10, 2), (14, 8, 3), (14, 11, 1), (16, 13, 0), (17, 8, 4), (18, 12, 1), (18,
    14, 0), (19, 13, 1), (19, 10, 3), (21, 10, 4), (23, 9, 3), (23, 11, 2), (24, 13, 2), (25, 12, 2), (25, 9,
    4), (25, 15, 0), (27, 11, 3), (27, 14, 1), (28, 13, 3), (28, 15, 1), (29, 11, 4), (30, 12, 3), (30, 13, 4),
    (31, 16, 0), (32, 12, 4), (33, 15, 2), (34, 16, 1), (36, 14, 2), (39, 15, 3), (39, 16, 2), (42, 14, 3), (42,
    15, 4), (44, 16, 3), (45, 14, 4), (46, 16, 4),
)


def travel_parts(shapes):
    parts = []
    for weight, pieces in TRAVEL:
        rows, width = shapes[weight]
        for i in range(pieces):
            if weight in TALL:
                parts.append((weight, slice(i * rows // pieces, (i + 1) * rows // pieces), slice(0, width)))
            else:
                lanes = width // 128
                columns = slice(i * lanes // pieces * 128, (i + 1) * lanes // pieces * 128)
                parts.append((weight, slice(0, rows), columns))
    return parts


def choose(index, slots, stage):
    if len(slots) == 1:
        pl.when(index == slots[0])(functools.partial(stage, slots[0]))
    elif slots:
        low, high = slots[: len(slots) // 2], slots[len(slots) // 2 :]
        pl.when(index < high[0])(functools.partial(choose, index, low, stage))
        pl.when(index >= high[0])(functools.partial(choose, index, high, stage))


def forward_kernel(*refs):
    lengths, clips = refs[:2]
    teacher_hbm, hidden_hbm = refs[2:4]
    teach, latent, (bias_q, bias_v) = refs[4:8], refs[8:12], refs[12:14]
    outs = refs[14:22]
    tqk_hbm, final_hbm, qkv_hbm, context_hbm, log_hbm = refs[22:27]
    low, near, biases = refs[27:32], refs[32:37], refs[37]
    t_x, a_in, tqk, t_context, final, qkv, context, logs = refs[38:46]
    send, receive, load, store = refs[46:]
    rows = t_x.shape[0]
    place = Place()
    all_here = place.meet()
    inputs = [pltpu.make_async_copy(teacher_hbm, t_x, load.at[0]), pltpu.make_async_copy(hidden_hbm, a_in, load.at[1])]
    for copy in inputs:
        copy.start()
    for pair in range(PAIRS):
        for i in range(3):
            to, at = TRIPLE * pair + PAIR * i, D * i + PAIR * pair
            low[4][:, to : to + PAIR] = teach[0][:, at : at + PAIR]
    all_here()
    sources = [low[4], *teach[1:], *low[:4]]
    parts = travel_parts([source.shape for source in sources])
    trips = [
        Trip(place, sources[w], outs[w], r, c, w in EARLY, send.at[i], receive.at[i])
        for i, (w, r, c) in enumerate(parts)
    ]
    weights = [w for w, _, _ in parts]

    def landing(i):
        weight, r, c = parts[i]
        if weight in TALL:
            c = slice(0, near[weight].shape[1])
        flat = outs[weight].reshape(near[weight].shape)
        return pltpu.make_async_copy(flat.at[:, c], near[weight].at[:, c], load.at[2 + i])

    def lands(i):
        weight = weights[i]
        return weight <= B_QKV and (weight not in TALL or weight not in weights[i + 1 :])

    def binarize():
        for i in range(1, 4):
            low[i][...] = signed_mean(latent[i][...])
        b_qkv = signed_mean(latent[0][...])
        for pair in range(PAIRS):
            for i in range(3):
                to, at = TRIPLE * pair + PAIR * i, D * i + PAIR * pair
                low[0][:, to : to + PAIR] = b_qkv[:, at : at + PAIR]
        biases[0:1] = bias_q[...].reshape(1, D)
        biases[1:2] = bias_v[...].reshape(1, D)

    phases = [trip.phases() for trip in trips]
    first_student = next(at for at, (_, i, _) in enumerate(FORWARD_PLAN) if weights[i] >= B_QKV)

    def do(at):
        _, i, phase = FORWARD_PLAN[at]
        if at == first_student:
            binarize()
        phases[i][phase]()
        if phase == 4 and lands(i):
            landing(i).start()

    counts = (PAIRS * rows, PAIRS * rows, CHUNKS * rows)
    stage_two, stage_three, end = counts[0], counts[0] + counts[1], sum(counts)
    per = {weight: [i for i, w in enumerate(weights) if w == weight and lands(i)] for weight in set(weights)}

    def stage(slot):
        for at, (when, _, _) in enumerate(FORWARD_PLAN):
            if when == slot:
                do(at)

    def turn(first_slot, count, index):
        planned = sorted({when for when, _, _ in FORWARD_PLAN if first_slot <= when < first_slot + count})
        choose(index + first_slot, planned, stage)

    def await_parts(weight, pair, row):
        pairs_each = PAIRS // len(per[weight])
        for n, part in enumerate(per[weight]):
            pl.when(jnp.logical_and(pair == n * pairs_each, row == 0))(landing(part).wait)

    def out_copy(source, target, slot, row):
        return pltpu.make_async_copy(source.at[row], target.at[row], store.at[slot, row])

    inputs[0].wait()
    inputs[1].wait()

    @pl.loop(0, rows)
    def _(row):
        a_in[row] = jnp.clip(a_in[row].astype(F32), -clips[0], clips[0]).astype(BF16)

    @pl.loop(0, PAIRS)
    def _(pair):
        @pl.loop(0, rows)
        def _(row):
            turn(0, counts[0], pair * rows + row)
            await_parts(T_QKV, pair, row)
            teacher_pair(pair, t_x[row], lengths[row], near[T_QKV], tqk.at[row], t_context.at[row])

    for row in range(rows):
        out_copy(tqk, tqk_hbm, 0, row).start()

    @pl.loop(0, PAIRS)
    def _(pair):
        @pl.loop(0, rows)
        def _(row):
            turn(stage_two, counts[1], pair * rows + row)
            await_parts(B_QKV, pair, row)
            student_pair(
                pair, a_in[row], lengths[row], near[B_QKV], biases.at[0:1], biases.at[1:2],
                qkv.at[row], context.at[row], logs.at[row],
            )

    for row in range(rows):
        out_copy(qkv, qkv_hbm, 2, row).start()
        out_copy(context, context_hbm, 3, row).start()
        out_copy(logs, log_hbm, 4, row).start()
    stage(stage_three)
    for weight in (T_OUT, T_UP, T_DOWN):
        for part in per[weight]:
            landing(part).wait()

    @pl.loop(0, rows)
    def _(row):
        final[row] = teacher_last(
            t_x[row], t_context[row], near[T_OUT], near[T_UP], near[T_DOWN],
            lambda c: turn(stage_three + 1, counts[2] - 1, row * CHUNKS + c - 1),
        )
        out_copy(final, final_hbm, 1, row).start()

    stage(end)
    for trip in trips:
        trip.last()

    @pl.loop(0, rows)
    def _(row):
        for slot, (source, target) in enumerate(
            ((tqk, tqk_hbm), (final, final_hbm), (qkv, qkv_hbm), (context, context_hbm), (logs, log_hbm))
        ):
            out_copy(source, target, slot, row).wait()


def forward_pass(lengths, clips, teacher_input, hidden, teach, latent, bias_q, bias_v):
    rows, tokens, _ = hidden.shape
    anywhere, vmem = pl.BlockSpec(memory_space=pl.ANY), pl.BlockSpec(memory_space=pltpu.VMEM)
    gathered = [(PLANES, COLUMNS, CORES * w.shape[0], w.shape[1]) for w in teach] * 2
    made = [
        shaped((rows, tokens, 2 * D), BF16),
        shaped((rows, tokens, D), F32),
        shaped((rows, tokens, 3 * D), BF16),
        shaped((rows, tokens, D), F32),
        shaped((rows, PAIRS, 2, tokens), F32),
    ]
    parts = sum(pieces for _, pieces in TRAVEL)
    near = [(DEVICES * w.shape[0], w.shape[1]) for w in teach] + [(DEVICES * teach[0].shape[0], 3 * D)]
    x_scratch = pltpu.VMEM((rows, tokens, D), BF16)
    outs = pl.pallas_call(
        forward_kernel,
        in_specs=[smem_spec(), smem_spec()] + [anywhere] * 2 + [vmem] * 10,
        out_specs=[anywhere] * 13,
        out_shape=[shaped(shape, BF16) for shape in gathered] + made,
        scratch_shapes=[pltpu.VMEM(w.shape, BF16) for w in (*latent, teach[0])]
        + [pltpu.VMEM(shape, BF16) for shape in near]
        + [pltpu.VMEM((8, D), F32), x_scratch, x_scratch]
        + [pltpu.VMEM(made[0].shape, BF16), x_scratch]
        + [pltpu.VMEM(m.shape, m.dtype) for m in made[1:]]
        + [pltpu.SemaphoreType.DMA((parts, Trip.SEMAPHORES))] * 2
        + [pltpu.SemaphoreType.DMA((2 + parts,)), pltpu.SemaphoreType.DMA((5, rows))],
        compiler_params=params(collective_id=0, has_side_effects=True),
    )(lengths, clips, teacher_input, hidden, *teach, *latent, bias_q, bias_v)
    weights = [out.reshape(-1, out.shape[-1]) for out in outs[4:8]]
    return weights, outs[8:]


class Fold:
    SEMAPHORES = 8

    def __init__(self, place, grad, own, finish, buffers, send, receive):
        self.place, self.grad, self.own, self.finish = place, grad, own, finish
        self.from_core, self.to_p, self.from_p, self.to_q, self.from_q, self.to_z, self.from_z = buffers
        self.send, self.receive = send, receive
        core = place.core
        self.p_stride, self.q_stride = 1 + core, 2 - core
        self.p = place.x + (place.y - place.x) * core
        self.q = place.y + (place.x - place.y) * core

    def remote(self, source, target, slot, device):
        return pltpu.make_async_remote_copy(
            src_ref=source, dst_ref=target, send_sem=self.send.at[slot], recv_sem=self.receive.at[slot],
            device_id=(device,), device_id_type=MESH,
        )

    def column(self, p, q):
        return p * self.p_stride + q * self.q_stride

    def keep(self):
        return pltpu.make_async_copy(self.grad.at[:, :, self.place.core], self.own, self.send.at[0])

    def over_core(self):
        return self.remote(self.grad.at[:, :, 1 - self.place.core], self.from_core, 1, self.place.sibling)

    def over_p(self):
        return self.remote(self.to_p, self.from_p, 2, self.place.along_a)

    def over_q(self):
        return self.remote(self.to_q, self.from_q, 3, self.place.along_b)

    def over_z(self, step):
        return self.remote(self.to_z.at[step - 1], self.from_z.at[step - 1], 3 + step, self.place.plane(step))

    def mine(self, z, column):
        return self.grad[z, column, self.place.core] if self.own is None else self.own[z, column]

    def pair_sum(self, z, column):
        return self.mine(z, column).astype(F32) + self.from_core[z, column].astype(F32)

    def first(self):
        if self.own is not None:
            self.keep().start()
        self.over_core().start()

    def second(self):
        if self.own is not None:
            self.keep().wait()
        self.over_core().wait_recv()

        @pl.loop(0, 2 * PLANES)
        def _(i):
            z, q = i // 2, i % 2
            column = self.column(1 - self.p, q)
            self.to_p[z, q] = self.mine(z, column) + self.from_core[z, column]

        self.over_p().start()

    def third(self):
        self.over_p().wait_recv()

        @pl.loop(0, PLANES)
        def _(z):
            q = 1 - self.q
            total = self.pair_sum(z, self.column(self.p, q)) + self.from_p[z, q].astype(F32)
            self.to_q[z] = total.astype(BF16)

        self.over_q().start()

    def quad_sum(self, z):
        q = self.q
        total = self.pair_sum(z, self.column(self.p, q)) + self.from_p[z, q].astype(F32)
        return total + self.from_q[z].astype(F32)

    def fourth(self):
        self.over_q().wait_recv()
        for step in range(1, PLANES):
            self.to_z[step - 1] = self.quad_sum((self.place.z + step) % PLANES).astype(BF16)
            self.over_z(step).start()

    def fifth(self):
        total = self.quad_sum(self.place.z)
        for step in range(1, PLANES):
            self.over_z(step).wait_recv()
            total = total + self.from_z[step - 1].astype(F32)
        self.finish(total)

    def phases(self):
        return [self.first, self.second, self.third, self.fourth, self.fifth]

    def last(self):
        self.over_core().wait_send()
        self.over_p().wait_send()
        self.over_q().wait_send()
        for step in range(1, PLANES):
            self.over_z(step).wait_send()


FOLD_BUFFERS = ((4, 4), (4, 2), (4, 2), (4,), (4,), (3,), (3,))


class Share:
    SEMAPHORES = 7

    def __init__(self, place, value, out, partial, received, send, receive):
        self.place, self.value, self.out = place, value, out
        self.partial, self.received, self.send, self.receive = partial, received, send, receive

    def swap(self, slot, device):
        return pltpu.make_async_remote_copy(
            src_ref=self.partial.at[min(slot, 3)], dst_ref=self.received.at[slot], send_sem=self.send.at[slot],
            recv_sem=self.receive.at[slot], device_id=(device,), device_id_type=MESH,
        )

    def partners(self):
        place = self.place
        return [place.sibling, place.along_x, place.along_y] + [place.plane(k) for k in range(1, PLANES)]

    def first(self):
        self.partial[0] = self.value[...]
        self.swap(0, self.place.sibling).start()

    def step(self, at):
        partners = self.partners()
        self.swap(at, partners[at]).wait_recv()
        self.partial[at + 1] = self.partial[at] + self.received[at]
        for slot in (at + 1,) if at < 2 else (3, 4, 5):
            self.swap(slot, partners[slot]).start()

    def finish(self):
        partners = self.partners()
        for slot in (3, 4, 5):
            self.swap(slot, partners[slot]).wait_recv()
        place = self.place
        self.received[6] = self.partial[3]
        total = jnp.zeros(self.value.shape, F32)
        for z in range(PLANES):
            behind = (place.z + PLANES - z) % PLANES
            total = total + self.received[(behind + 3) % PLANES + 3]
        self.out[...] = total

    def phases(self):
        return [self.first] + [functools.partial(self.step, at) for at in range(3)] + [self.finish]

    def last(self):
        for slot, partner in enumerate(self.partners()):
            self.swap(slot, partner).wait_send()


GRAD_STEPS = 2 * CHUNKS + 1
FOLDED = ((0, 4), (1, 4), (2, 1))
FOLD_PARTS = sum(pieces for _, pieces in FOLDED)
BACKWARD_PLAN = (
    (5, 0, 0), (5, 1, 0), (5, 2, 0), (5, 3, 0), (6, 4, 0), (7, 5, 0), (8, 6, 0), (9, 0, 1), (9, 7, 0), (9, 8,
    0), (11, 1, 1), (12, 9, 0), (12, 0, 2), (12, 2, 1), (12, 15, 0), (13, 1, 2), (14, 9, 1), (14, 15, 1), (15,
    10, 0), (15, 0, 3), (15, 1, 3), (15, 2, 2), (15, 3, 1), (16, 9, 2), (16, 15, 2), (17, 10, 1), (18, 11, 0),
    (18, 0, 4), (18, 1, 4), (18, 2, 3), (18, 3, 2), (18, 4, 1), (18, 9, 3), (18, 15, 3), (19, 10, 2), (20, 5,
    1), (20, 11, 1), (21, 12, 0), (21, 2, 4), (21, 3, 3), (21, 4, 2), (21, 6, 1), (21, 9, 4), (21, 10, 3), (21,
    15, 4), (22, 11, 2), (23, 5, 2), (23, 7, 1), (23, 12, 1), (24, 13, 0), (24, 3, 4), (24, 4, 3), (24, 6, 2),
    (24, 10, 4), (24, 11, 3), (25, 8, 1), (26, 5, 3), (26, 12, 2), (26, 13, 1), (26, 7, 2), (27, 14, 0), (27, 4,
    4), (27, 6, 3), (27, 8, 2), (27, 11, 4), (28, 12, 3), (29, 5, 4), (30, 7, 3), (30, 8, 3), (30, 13, 2), (30,
    14, 1), (30, 16, 0), (30, 6, 4), (30, 12, 4), (30, 16, 1), (30, 13, 3), (30, 14, 2), (30, 16, 2), (30, 14,
    3), (30, 16, 3), (30, 7, 4), (30, 8, 4), (30, 13, 4), (30, 16, 4), (30, 14, 4),
)


def fold_parts(shapes):
    parts = []
    for i, pieces in FOLDED:
        rows, width = shapes[i]
        for at in range(pieces):
            if i == 0:
                size = rows // pieces
                parts.append((i, slice(at * size, (at + 1) * size), slice(0, width), (size, width)))
            else:
                size = width // pieces
                parts.append((i, slice(0, rows), slice(at * size, (at + 1) * size), (rows, size)))
    return parts


def backward_kernel(*refs):
    lengths, clips = refs[:2]
    qkv, tqk, logs, dots, d_context, w_triple = refs[2:8]
    (x_hbm, d_res_hbm), (act, d_down, up_in, d_pre, cut, d_attn), sums = refs[8:10], refs[10:16], refs[16]
    input_hbm, grads = refs[17], refs[18:21]
    g_down, g_up, g_out, g_qkv, sums_out, q_sums_out = refs[21:27]
    x, a_in_t, d_pair, d_a, d_res, g_pair, q_sums, ring, stage_tall, stage_wide = refs[27:37]
    scratch = refs[37:]
    rows, tokens = qkv.shape[0], qkv.shape[1]
    place = Place()
    at_step = pl.program_id(0)
    at_pair = at_step - GRAD_STEPS
    parts = fold_parts([g_down.shape, g_up.shape, g_out.shape])
    owns, scratch = scratch[:FOLD_PARTS], scratch[FOLD_PARTS:]
    per = len(FOLD_BUFFERS)
    taken = (FOLD_PARTS + PAIRS) * per
    buffers, (s_partial, s_received, q_partial, q_received, send, receive, load) = scratch[:taken], scratch[taken:]

    def set_part(target, r, c):
        def finish(total):
            target[r, c] = total

        return finish

    def set_triple(pair):
        def finish(total):
            for i in range(3):
                at = D * i + PAIR * pair
                g_qkv[:, at : at + PAIR] = total[:, PAIR * i : PAIR * (i + 1)]

        return finish

    folds = []
    for n, (i, r, c, _) in enumerate(parts):
        target = (g_down, g_up, g_out)[i]
        source = grads[i].at[:, :, :, r, c]
        folds.append(
            Fold(place, source, owns[n], set_part(target, r, c), buffers[per * n : per * n + per], send.at[n], receive.at[n])
        )
    for pair in range(PAIRS):
        n = FOLD_PARTS + pair
        folds.append(
            Fold(
                place, g_pair.at[pair], None, set_triple(pair), buffers[per * n : per * n + per], send.at[n], receive.at[n]
            )
        )
    n = len(folds)
    share = Share(place, sums, sums_out, s_partial, s_received, send.at[n], receive.at[n])
    q_share = Share(place, q_sums, q_sums_out, q_partial, q_received, send.at[n + 1], receive.at[n + 1])
    inputs = [pltpu.make_async_copy(x_hbm, x, load.at[0]), pltpu.make_async_copy(d_res_hbm, d_res, load.at[1])]

    slots = GRAD_STEPS + PAIRS * rows
    phases = [fold.phases() for fold in folds] + [share.phases(), q_share.phases()]
    timed = [
        (slot, phases[i][phase]) for slot, i, phase in BACKWARD_PLAN if phase or not FOLD_PARTS <= i < FOLD_PARTS + PAIRS
    ]

    def stage(slot):
        for when, act in timed:
            if when == slot:
                act()

    def turn(index):
        choose(index, sorted({when for when, _ in timed if when < slots}), stage)

    def load_left(source):
        return pltpu.make_async_copy(source, x, load.at[2])

    def chunk(source, c, step):
        part = source.at[:, :, pl.ds(pl.multiple_of(c * D, D), D)]
        return pltpu.make_async_copy(part, ring.at[step % 2], load.at[3 + step % 2])

    def load_chunk(step):
        pl.when(step < CHUNKS)(lambda: chunk(act, step, step).start())
        pl.when(jnp.logical_and(step >= CHUNKS, step < 2 * CHUNKS))(lambda: chunk(d_pre, step - CHUNKS, step).start())
        pl.when(step == 2 * CHUNKS)(lambda: chunk(d_attn, 0, step).start())

    def tall_out(c):
        return pltpu.make_async_copy(stage_tall, grads[0].at[c], load.at[5])

    def wide_out(c):
        columns = pl.ds(pl.multiple_of(c * D, D), D)
        return pltpu.make_async_copy(stage_wide, grads[1].at[:, :, :, :, columns], load.at[6])

    out_out = pltpu.make_async_copy(stage_wide, grads[2], load.at[6])

    @pl.when(at_step == 0)
    def _():
        all_here = place.meet()
        load_left(d_down).start()
        load_chunk(0)
        inputs[1].start()
        q_sums[...] = jnp.zeros_like(q_sums)
        d_a[...] = jnp.zeros_like(d_a)
        all_here()

    @pl.when(at_step < GRAD_STEPS)
    def _():
        turn(at_step)
        for step, following in ((0, up_in), (CHUNKS, cut), (2 * CHUNKS, None)):

            @pl.when(at_step == step)
            def _():
                load_left(d_down).wait()
                a_in_t[...] = x[...].reshape(rows * tokens, D).T
                (inputs[0] if following is None else load_left(following)).start()

        chunk(act, 0, at_step).wait()
        load_chunk(at_step + 1)
        product = nn(a_in_t[...], ring[at_step % 2].reshape(rows * tokens, D))

        @pl.when(at_step < CHUNKS)
        def _():
            pl.when(at_step > 0)(tall_out(0).wait)
            stage_tall[...] = product.T.reshape(stage_tall.shape).astype(BF16)
            tall_out(at_step).start()

        @pl.when(at_step >= CHUNKS)
        def _():
            pl.when(at_step == CHUNKS)(tall_out(0).wait)
            pl.when(at_step > CHUNKS)(wide_out(0).wait)
            height = stage_wide.shape[3]
            for device in range(DEVICES):
                z, column, core = device // 8, device // 2 % COLUMNS, device % CORES
                stage_wide[z, column, core] = product[height * device : height * (device + 1)].astype(BF16)
            pl.when(at_step < 2 * CHUNKS)(lambda: wide_out(at_step - CHUNKS).start())
            pl.when(at_step == 2 * CHUNKS)(out_out.start)

    pl.when(at_step == GRAD_STEPS)(out_out.wait)

    def pair_step():
        one_pair(
            lengths, clips, at_pair, turn, stage, slots, folds, timed, share, q_share, inputs, input_hbm, load,
            qkv, tqk, logs, dots, d_context, w_triple, g_qkv.shape[0], x, a_in_t, d_pair, d_a, d_res, g_pair, q_sums,
        )

    pl.when(at_pair >= 0)(pair_step)


def one_pair(
    lengths, clips, at_pair, turn, stage, slots, folds, timed, share, q_share, inputs, input_hbm, load,
    qkv, tqk, logs, dots, d_context, w_triple, height, x, a_in_t, d_pair, d_a, d_res, g_pair, q_sums,
):
    rows, tokens = qkv.shape[0], qkv.shape[1]

    @pl.loop(0, rows)
    def _(row):
        turn(GRAD_STEPS + at_pair * rows + row)
        queries, keys, values = (qkv[row, :, PAIR * i : PAIR * (i + 1)] for i in range(3))
        t_queries, t_keys = (tqk[row, :, PAIR * i : PAIR * (i + 1)] for i in range(2))
        grads_here = attend_pair_back(
            queries, keys, values, t_queries, t_keys, logs[row, 0], dots[row, 0], d_context[row], lengths[row]
        )
        here = pl.ds(pl.multiple_of(row * tokens, tokens), tokens)
        for i in range(3):
            d_pair[here, PAIR * i : PAIR * (i + 1)] = grads_here[i]

    bound = clips[0]

    @pl.when(at_pair == 0)
    def _():
        inputs[0].wait()
        for row in range(rows):
            clipped = jnp.clip(x[row].astype(F32), -bound, bound)
            a_in_t[:, tokens * row : tokens * (row + 1)] = clipped.T.astype(BF16)

    g_now = nn(a_in_t[...], d_pair[...])
    for device in range(DEVICES):
        z, column, core = device // 8, device // 2 % COLUMNS, device % CORES
        g_pair[at_pair, z, column, core] = g_now[height * device : height * (device + 1)].astype(BF16)
    for pair, fold in enumerate(folds[FOLD_PARTS:]):
        pl.when(at_pair == pair)(fold.first)
    here = pair_columns(at_pair)
    q_sums[Q_QUERY : Q_QUERY + 1, here] = column_sum(d_pair[:, :PAIR].astype(F32))
    q_sums[Q_VALUE : Q_VALUE + 1, here] = column_sum(d_pair[:, 2 * PAIR :].astype(F32))
    d_a[...] += nt(d_pair[...], w_triple[...])

    @pl.when(at_pair == PAIRS - 1)
    def _():
        inputs[1].wait()
        for row in range(rows):
            stage(slots + row)
            value = x[row].astype(F32)
            d_row = d_a[tokens * row : tokens * (row + 1)]
            inside = jnp.where(jnp.abs(value) < bound, 1.0, jnp.where(jnp.abs(value) == bound, 0.5, 0.0))
            outside = (1.0 - inside) * d_row
            q_sums[Q_CLIP : Q_CLIP + 1] += column_sum(jnp.where(value > 0, outside, -outside))
            x[row] = (d_res[row] + d_row * inside).astype(BF16)
        out = pltpu.make_async_copy(x, input_hbm, load.at[0])
        out.start()
        for when, act in timed:
            if when >= slots + rows:
                act()
        for fold in folds:
            fold.last()
        share.last()
        q_share.last()
        out.wait()


def backward_pass(lengths, clips, hidden, qkv, tqk, logs, dots, d_context, d_res, w_qkv, made_by, sums):
    rows, tokens, _ = hidden.shape
    shapes = [(FF // DEVICES, D), (D // DEVICES, FF), (D // DEVICES, D)]
    height = w_qkv.shape[0] // DEVICES
    part_shapes = [part[3] for part in fold_parts(shapes)]
    fold_shapes = part_shapes + [(height, TRIPLE)] * PAIRS
    anywhere = pl.BlockSpec(memory_space=pl.ANY)

    def of_pair(width):
        return pl.BlockSpec((rows, tokens, width), lambda s: (0, 0, pair_at(s)))

    def pair_at(step):
        return step // GRAD_STEPS * (step - GRAD_STEPS)

    stat = pl.BlockSpec((rows, 1, 2, tokens), lambda s: (0, pair_at(s), 0, 0))
    small = [shaped(sums.shape, F32), shaped((Q_ROWS, D), F32)]
    made = [shaped(s, F32) for s in shapes] + [shaped((height, 3 * D), F32)] + small
    return pl.pallas_call(
        backward_kernel,
        grid=(GRAD_STEPS + PAIRS,),
        in_specs=[smem_spec(), smem_spec()]
        + [of_pair(TRIPLE), of_pair(DOUBLE), stat, stat, of_pair(PAIR), pl.BlockSpec((D, TRIPLE), lambda s: (0, pair_at(s)))]
        + [anywhere] * 8
        + [whole_spec(sums.shape)],
        out_specs=[anywhere] * 4 + [whole_spec(m.shape) for m in made],
        out_shape=[shaped(hidden.shape, BF16)]
        + [shaped((PLANES, COLUMNS, CORES) + shape, BF16) for shape in shapes]
        + made,
        scratch_shapes=[
            pltpu.VMEM((rows, tokens, D), BF16),
            pltpu.VMEM((D, rows * tokens), BF16),
            pltpu.VMEM((rows * tokens, TRIPLE), BF16),
            pltpu.VMEM((rows * tokens, D), F32),
            pltpu.VMEM((rows, tokens, D), F32),
            pltpu.VMEM((PAIRS, PLANES, COLUMNS, CORES, height, TRIPLE), BF16),
            pltpu.VMEM((Q_ROWS, D), F32),
            pltpu.VMEM((2, rows, tokens, D), BF16),
            pltpu.VMEM((COLUMNS, CORES) + shapes[0], BF16),
            pltpu.VMEM((PLANES, COLUMNS, CORES) + shapes[2], BF16),
        ]
        + [pltpu.VMEM((PLANES, COLUMNS) + s, BF16) for s in part_shapes]
        + [pltpu.VMEM(lead + s, BF16) for s in fold_shapes for lead in FOLD_BUFFERS]
        + [pltpu.VMEM((n,) + m.shape, F32) for m in small for n in (4, 7)]
        + [pltpu.SemaphoreType.DMA((len(fold_shapes) + 2, Fold.SEMAPHORES))] * 2
        + [pltpu.SemaphoreType.DMA((7,))],
        compiler_params=params(collective_id=1, has_side_effects=True),
    )(
        lengths, clips, qkv, tqk, logs, dots, d_context, w_qkv, hidden, d_res, *made_by, sums
    )


def finish_kernel(sums, q_sums, *refs):
    grads, input_hbm = refs[:4], refs[4]
    outs, input_out = refs[5:9], refs[9]
    b_q, b_v, b_out, b_up, b_down, gain_one, shift_one, gain_two, shift_two, clips = refs[10:20]
    held, arrive = refs[20:]
    rows = held.shape[0]
    copies = [pltpu.make_async_copy(input_hbm.at[i], held.at[i], arrive.at[i]) for i in range(rows)]
    for copy in copies:
        copy.start()

    def row(ref, at):
        return ref[at : at + 1].reshape(D)

    for source, target in zip(grads, outs):
        target[...] = source[...]
    backs = [pltpu.make_async_copy(held.at[i], input_out.at[i], arrive.at[rows + i]) for i in range(rows)]
    for copy, back in zip(copies, backs):
        copy.wait()
        back.start()
    b_q[...] = row(q_sums, Q_QUERY)
    b_v[...] = row(q_sums, Q_VALUE)
    b_out[...] = row(sums, S_OUT)
    b_up[...] = jnp.concatenate([sums[S_UP + c : S_UP + c + 1] for c in range(CHUNKS)], axis=1).reshape(FF)
    b_down[...] = row(sums, S_DOWN)
    gain_one[...] = row(sums, S_GAIN_ONE)
    shift_one[...] = row(sums, S_SHIFT_ONE)
    gain_two[...] = row(sums, S_GAIN_TWO)
    shift_two[...] = row(sums, S_SHIFT_TWO)
    clips[0] = jnp.sum(q_sums[Q_CLIP : Q_CLIP + 1])
    for i, at in enumerate((S_CLIP_ONE, S_CLIP_TWO, S_CLIP_THREE)):
        clips[1 + i] = jnp.sum(sums[at : at + 1])
    for copy in backs:
        copy.wait()


def finish(sums, q_sums, grads, input_grad):
    vmem, anywhere = pl.BlockSpec(memory_space=pltpu.VMEM), pl.BlockSpec(memory_space=pl.ANY)
    lengths = [D, D, D, FF, D, D, D, D, D]
    return pl.pallas_call(
        finish_kernel,
        in_specs=[vmem] * 6 + [anywhere],
        out_specs=[vmem] * 4 + [anywhere] + [vmem] * 9 + [smem_spec()],
        out_shape=[shaped(g.shape, F32) for g in grads]
        + [shaped(input_grad.shape, BF16)]
        + [shaped((n,), F32) for n in lengths]
        + [shaped((4,), F32)],
        scratch_shapes=[pltpu.VMEM(input_grad.shape, BF16), pltpu.SemaphoreType.DMA((2 * input_grad.shape[0],))],
        compiler_params=params(),
    )(sums, q_sums, *grads, input_grad)


def on_device(
    by_kernel,
    hidden, teacher_input, cotangent, lengths, lat_qkv, lat_out, lat_up, lat_down,
    bias_q, bias_v, bias_out, bias_up, bias_down, gain_one, shift_one, gain_two, shift_two, clips,
    teach_qkv, teach_out, teach_up, teach_down,
):
    latent = (lat_qkv, lat_out, lat_up, lat_down)
    teach = (teach_qkv, teach_out, teach_up, teach_down)
    if by_kernel:
        (w_qkv, *weights), (tqk, final, qkv, context, logs) = forward_pass(
            lengths, clips, teacher_input, hidden, teach, latent, bias_q, bias_v
        )
    else:
        gather = functools.partial(lax.all_gather, axis_name="shard", axis=0, tiled=True)
        w_qkv, *weights = (gather(signed_mean(w)) for w in latent)
        w_qkv = by_pairs(w_qkv)
        t_qkv, *t_weights = (gather(w) for w in teach)
        tqk, final = teacher_pass(lengths, teacher_input, by_pairs(t_qkv), *t_weights)
        qkv, context, logs = student_attend(lengths, clips, hidden, w_qkv, bias_q, bias_v)
    vectors = (bias_out, bias_up, bias_down, gain_one, shift_one, gain_two, shift_two)
    mixed, act, d_pre, up_in, d_down, cut, d_attn, d_res, d_context, dots, sums = student_middle(
        lengths, clips, hidden, cotangent, final, context, weights, vectors
    )
    made_by = (act, d_down, up_in, d_pre, cut, d_attn)
    if by_kernel:
        input_grad, _, _, _, g_down, g_up, g_out, g_qkv, sums, q_sums = backward_pass(
            lengths, clips, hidden, qkv, tqk, logs, dots, d_context, d_res, w_qkv, made_by, sums
        )
    else:
        g_down, g_up, g_out = weight_grads(*made_by)
        input_grad, g_qkv, q_sums = student_back(lengths, clips, hidden, qkv, tqk, logs, dots, d_context, d_res, w_qkv)
        scatter = functools.partial(lax.psum_scatter, axis_name="shard", scatter_dimension=0, tiled=True)
        g_down, g_up, g_qkv, g_out = (scatter(g.astype(F32)) for g in (g_down, g_up, by_kinds(g_qkv), g_out))
        sums, q_sums = lax.psum((sums, q_sums), "shard")
    g_qkv, g_out, g_up, g_down, input_grad, *small = finish(sums, q_sums, (g_qkv, g_out, g_up, g_down), input_grad)
    return mixed, input_grad, g_qkv, g_out, g_up, g_down, *small


def solution(mesh):
    split, rows, same = P("shard", None), P("shard", None, None), P()
    return jax.shard_map(
        functools.partial(on_device, mesh.shape["shard"] == DEVICES),
        mesh=mesh,
        in_specs=(rows, rows, rows, P("shard")) + (split,) * 4 + (same,) * 10 + (split,) * 4,
        out_specs=(rows, rows) + (split,) * 4 + (same,) * 10,
        check_vma=False,
    )
```

```python
import functools
import math

import jax
import jax.numpy as jnp
from jax import lax
from jax.experimental import pallas as pl
from jax.experimental.pallas import tpu as pltpu
from jax.sharding import PartitionSpec as P

D = 768
FF = 3072
HEAD_DIM = 64
PAIR = 2 * HEAD_DIM
PAIRS = D // PAIR
DOUBLE, TRIPLE = 2 * PAIR, 3 * PAIR
CHUNKS = FF // D

EPSILON = 1e-05
MASKED = -1000000000.0
SCALE = 1.0 / math.sqrt(HEAD_DIM)

F32 = jnp.float32
BF16 = jnp.bfloat16
MESH = pl.DeviceIdType.MESH
VMEM_LIMIT = 63 * 1024 * 1024


def nn(left, right):
    return lax.dot_general(left, right, (((1,), (0,)), ((), ())), preferred_element_type=F32)


def nt(left, right):
    return lax.dot_general(left, right, (((1,), (1,)), ((), ())), preferred_element_type=F32)


def tn(left, right):
    return lax.dot_general(left, right, (((0,), (0,)), ((), ())), preferred_element_type=F32)


def signed_mean(latent):
    factor = jnp.mean(jnp.abs(latent), axis=1, keepdims=True)
    sign = jnp.where(latent > 0, 1.0, jnp.where(latent < 0, -1.0, 0.0))
    return (factor * sign).astype(BF16)


def normalize(value):
    center = value - jnp.mean(value, axis=-1, keepdims=True)
    inverse = lax.rsqrt(jnp.mean(center * center, axis=-1, keepdims=True) + EPSILON)
    return center * inverse, inverse


def norm_back(d_normed, normed, inverse):
    first = jnp.mean(d_normed, axis=-1, keepdims=True)
    second = jnp.mean(d_normed * normed, axis=-1, keepdims=True)
    return inverse * (d_normed - first - normed * second)


def normal_cdf(value):
    return 0.5 * (1.0 + lax.erf(value * (1.0 / math.sqrt(2.0))))


def column_sum(value):
    return jnp.sum(value, axis=0, keepdims=True)


def head_halves(pair):
    first = lax.broadcasted_iota(jnp.int32, pair.shape, 1) < HEAD_DIM
    zero = jnp.zeros_like(pair)
    return jnp.where(first, pair, zero), jnp.where(first, zero, pair)


def mask_columns(tokens, length):
    shape = (tokens, PAIR)
    first = lax.broadcasted_iota(jnp.int32, shape, 1) == 0
    dead = jnp.logical_and(first, lax.broadcasted_iota(jnp.int32, shape, 0) >= length)
    return jnp.where(dead, MASKED, 0.0).astype(BF16), jnp.where(first, 1.0, 0.0).astype(BF16)


def attend_pair(queries, keys, values, length):
    values_t = values.T
    beside_keys, beside_queries = mask_columns(queries.shape[0], length)
    wide_keys = jnp.concatenate([keys, beside_keys], axis=1)
    contexts, log_totals = [], []
    for head, one in enumerate(head_halves(queries)):
        masked = nt(wide_keys, jnp.concatenate([one, beside_queries], axis=1))
        top = jnp.max(masked, axis=0, keepdims=True)
        expo = jnp.exp(masked - top)
        total = jnp.sum(expo, axis=0, keepdims=True)
        probs = (expo * (1.0 / total)).astype(BF16)
        contexts.append(nn(values_t[HEAD_DIM * head : HEAD_DIM * (head + 1)], probs))
        log_totals.append(top + jnp.log(total))
    return jnp.concatenate(contexts, axis=0).T, jnp.concatenate(log_totals, axis=0)


def attend_pair_back(queries, keys, values, t_queries, t_keys, log_totals, row_dots, d_context, length):
    tokens = queries.shape[0]
    beside_keys, beside_queries = mask_columns(tokens, length)
    wide_keys = jnp.concatenate([keys, beside_keys], axis=1)
    live = lax.broadcasted_iota(jnp.int32, (tokens, DOUBLE), 0) < length
    both_keys = jnp.where(live, jnp.concatenate([keys, -t_keys], axis=1), 0.0).astype(BF16)
    share = jnp.where(live, 1.0 / tokens, 0.0).astype(BF16)
    keys_t = keys.T
    d_queries, d_keys, d_values = [], [], []
    heads = zip(head_halves(queries), head_halves(d_context), head_halves(t_queries))
    for head, (one, d_one, t_one) in enumerate(heads):
        masked = nt(wide_keys, jnp.concatenate([one, beside_queries], axis=1))
        extra = nt(both_keys, jnp.concatenate([one, t_one], axis=1) * share)
        probs = jnp.exp(masked - log_totals[head : head + 1])
        d_probs = nt(values, d_one)
        d_values.append(nn(probs.astype(BF16), d_one))
        d_scores = (probs * (d_probs - row_dots[head : head + 1]) + extra).astype(BF16)
        d_keys.append(nn(d_scores, one))
        d_queries.append(nn(keys_t[HEAD_DIM * head : HEAD_DIM * (head + 1)], d_scores))
    d_q = (jnp.concatenate(d_queries, axis=0).T * SCALE).astype(BF16)
    return d_q, (d_keys[0] + d_keys[1]).astype(BF16), (d_values[0] + d_values[1]).astype(BF16)


def pair_columns(pair, width=PAIR):
    return pl.ds(pl.multiple_of(pair * width, PAIR), width)


def by_pairs(matrix):
    split = matrix.reshape(matrix.shape[0], 3, PAIRS, PAIR)
    return split.transpose(0, 2, 1, 3).reshape(matrix.shape[0], 3 * D)


def by_kinds(matrix):
    split = matrix.reshape(matrix.shape[0], PAIRS, 3, PAIR)
    return split.transpose(0, 2, 1, 3).reshape(matrix.shape[0], 3 * D)


def teacher_pair(pair, x, length, w_qkv, tqk_ref, context_ref):
    joined = nn(x, w_qkv[:, pair_columns(pair, TRIPLE)]).astype(BF16)
    queries, keys, values = (joined[:, PAIR * i : PAIR * (i + 1)] for i in range(3))
    queries = (queries.astype(F32) * SCALE).astype(BF16)
    tqk_ref[:, pair_columns(pair, DOUBLE)] = jnp.concatenate([queries, keys], axis=1)
    mixed, _ = attend_pair(queries, keys, values, length)
    context_ref[:, pair_columns(pair)] = mixed.astype(BF16)


def teacher_last(x, context, w_out, w_up, w_down, between):
    first, _ = normalize(x.astype(F32) + nn(context, w_out[...]))
    first_low = first.astype(BF16)
    total = first
    for c in range(CHUNKS):
        between(c)
        inner = nn(first_low, w_up[:, D * c : D * (c + 1)])
        total = total + nn((inner * normal_cdf(inner)).astype(BF16), w_down[D * c : D * (c + 1), :])
    return normalize(total)[0]


def student_pair(pair, a_in, length, w_qkv, bias_q, bias_v, qkv_ref, context_ref, log_ref):
    joined = nn(a_in, w_qkv[:, pair_columns(pair, TRIPLE)])
    queries = (joined[:, :PAIR] + bias_q[:, pair_columns(pair)]).astype(BF16)
    queries = (queries.astype(F32) * SCALE).astype(BF16)
    keys = joined[:, PAIR:DOUBLE].astype(BF16)
    values = (joined[:, DOUBLE:] + bias_v[:, pair_columns(pair)]).astype(BF16)
    qkv_ref[:, pair_columns(pair, TRIPLE)] = jnp.concatenate([queries, keys, values], axis=1)
    mixed, log_totals = attend_pair(queries, keys, values, length)
    context_ref[:, pair_columns(pair)] = mixed
    log_ref[pair] = log_totals


def teacher_kernel(lengths, x_ref, w_qkv, w_out, w_up, w_down, tqk_ref, final_ref, context):
    length = lengths[pl.program_id(0)]

    @pl.loop(0, PAIRS)
    def _(pair):
        teacher_pair(pair, x_ref[0], length, w_qkv, tqk_ref.at[0], context)

    final_ref[0] = teacher_last(x_ref[0], context[...], w_out, w_up, w_down, lambda c: None)


def student_attend_kernel(lengths, clips, x_ref, w_qkv, bias_q, bias_v, qkv_ref, context_ref, log_ref, a_in):
    length = lengths[pl.program_id(0)]
    a_in[...] = jnp.clip(x_ref[0].astype(F32), -clips[0], clips[0]).astype(BF16)

    @pl.loop(0, PAIRS)
    def _(pair):
        student_pair(
            pair, a_in[...], length, w_qkv, bias_q, bias_v, qkv_ref.at[0], context_ref.at[0], log_ref.at[0]
        )


(S_OUT, S_UP, S_DOWN, S_GAIN_ONE, S_SHIFT_ONE, S_GAIN_TWO, S_SHIFT_TWO, S_CLIP_ONE, S_CLIP_TWO, S_CLIP_THREE) = (
    0, 1, 5, 6, 7, 8, 9, 10, 11, 12,
)
S_ROWS = 16
(Q_QUERY, Q_VALUE, Q_CLIP) = (0, 1, 2)
Q_ROWS = 8
ABOVE, BELOW = 4.0, -4.0


def student_middle_kernel(
    lengths, clips, x_ref, cotangent_ref, final_ref, context_ref, w_out, w_up, w_down,
    bias_out, bias_up, bias_down, gain_one, shift_one, gain_two, shift_two,
    mixed_ref, act_ref, d_pre_ref, up_in_ref, d_down_ref, cut_ref, d_attn_ref, d_res_ref, d_context_ref, dots_ref,
    sums_ref, slope,
):
    block = x_ref.shape[1]
    row, part = pl.program_id(0), pl.program_id(1)
    length = lengths[row] - part * block

    @pl.when(jnp.logical_and(row == 0, part == 0))
    def _():
        sums_ref[...] = jnp.zeros_like(sums_ref)

    def add(at, value):
        sums_ref[at : at + 1] += value

    def vector(ref):
        return ref[...].reshape(1, ref.shape[0])

    cut = jnp.clip(context_ref[0], -clips[1], clips[1]).astype(BF16)
    cut_ref[0] = cut
    normed_one, inverse_one = normalize(x_ref[0].astype(F32) + nn(cut, w_out[...]) + vector(bias_out))
    h_one = normed_one * vector(gain_one) + vector(shift_one)
    up_in = jnp.clip(h_one, -clips[2], clips[2]).astype(BF16)
    up_in_ref[0] = up_in
    total = h_one + vector(bias_down)
    for c in range(CHUNKS):
        columns = slice(D * c, D * (c + 1))
        pre = nn(up_in, w_up[:, columns]) + vector(bias_up)[:, columns]
        cdf = normal_cdf(pre)
        value = pre * cdf
        rise = cdf + pre * jnp.exp(-0.5 * pre * pre) * (1.0 / math.sqrt(2.0 * math.pi))
        rise = jnp.where(value > clips[3], ABOVE, jnp.where(value < -clips[3], BELOW, rise))
        slope[:, columns] = rise
        act = jnp.clip(value, -clips[3], clips[3]).astype(BF16)
        act_ref[0, :, columns] = act
        total = total + nn(act, w_down[columns, :])
    normed_two, inverse_two = normalize(total)
    out = normed_two * vector(gain_two) + vector(shift_two)
    mixed_ref[0] = out.astype(BF16)
    live = lax.broadcasted_iota(jnp.int32, (block, 1), 0) < length
    d_out = jnp.where(live, cotangent_ref[0].astype(F32) + out - final_ref[0], 0.0)
    add(S_GAIN_TWO, column_sum(d_out * normed_two))
    add(S_SHIFT_TWO, column_sum(d_out))
    d_res_two = norm_back(d_out * vector(gain_two), normed_two, inverse_two)
    d_down = d_res_two.astype(BF16)
    d_down_ref[0] = d_down
    add(S_DOWN, column_sum(d_down.astype(F32)))
    d_up_in = jnp.zeros((block, D), F32)
    for c in range(CHUNKS):
        columns = slice(D * c, D * (c + 1))
        d_act = nt(d_down, w_down[columns, :])
        rise = slope[:, columns]
        above, below = rise > 2.0, rise < -2.0
        d_pre = jnp.where(jnp.logical_or(above, below), 0.0, rise * d_act).astype(BF16)
        d_pre_ref[0, :, columns] = d_pre
        add(S_CLIP_THREE, column_sum(jnp.where(above, d_act, jnp.where(below, -d_act, 0.0))))
        add(S_UP + c, column_sum(d_pre.astype(F32)))
        d_up_in = d_up_in + nt(d_pre, w_up[:, columns])
    above, below = h_one > clips[2], h_one < -clips[2]
    add(S_CLIP_TWO, column_sum(jnp.where(above, d_up_in, jnp.where(below, -d_up_in, 0.0))))
    d_h_one = d_res_two + jnp.where(jnp.abs(h_one) < clips[2], d_up_in, 0.0)
    add(S_GAIN_ONE, column_sum(d_h_one * normed_one))
    add(S_SHIFT_ONE, column_sum(d_h_one))
    d_res_one = norm_back(d_h_one * vector(gain_one), normed_one, inverse_one)
    d_res_ref[0] = d_res_one
    d_attn = d_res_one.astype(BF16)
    d_attn_ref[0] = d_attn
    add(S_OUT, column_sum(d_attn.astype(F32)))
    d_cut = nt(d_attn, w_out[...])
    context = context_ref[0]
    above, below = context > clips[1], context < -clips[1]
    add(S_CLIP_ONE, column_sum(jnp.where(above, d_cut, jnp.where(below, -d_cut, 0.0))))
    d_context = jnp.where(jnp.abs(context) < clips[1], d_cut, 0.0).astype(BF16)
    d_context_ref[0] = d_context
    product = d_context.astype(F32) * context
    high = product.astype(BF16)
    low = (product - high.astype(F32)).astype(BF16)
    shape = (S_ROWS, D)
    heads = lax.broadcasted_iota(jnp.int32, shape, 1) // HEAD_DIM == lax.broadcasted_iota(jnp.int32, shape, 0)
    ones = heads.astype(F32).astype(BF16)
    dots = nt(ones, high) + nt(ones, low)
    for pair in range(PAIRS):
        dots_ref[0, pair] = dots[2 * pair : 2 * pair + 2]


def weight_grads_kernel(act, d_down, up_in, d_pre, cut, d_attn, g_down, g_up, g_out):
    g_down[...] = tn(act[...], d_down[...]).astype(BF16)
    g_up[...] = tn(up_in[...], d_pre[...]).astype(BF16)

    @pl.when(pl.program_id(0) == 0)
    def _():
        g_out[...] = tn(cut[...], d_attn[...]).astype(BF16)


def student_back_kernel(
    lengths, clips, x_ref, qkv_ref, tqk_ref, log_ref, dots_ref, d_context_ref, d_res_ref, w_qkv,
    input_ref, g_qkv, sums_ref, a_in, d_joined,
):
    row = pl.program_id(0)
    tokens = x_ref.shape[1]
    length = lengths[row]
    here = pl.ds(pl.multiple_of(row * tokens, tokens), tokens)

    @pl.when(row == 0)
    def _():
        sums_ref[...] = jnp.zeros_like(sums_ref)

    @pl.loop(0, PAIRS)
    def _(pair):
        queries, keys, values = (qkv_ref[0, :, pair_columns(3 * pair + i)] for i in range(3))
        t_queries, t_keys = (tqk_ref[0, :, pair_columns(2 * pair + i)] for i in range(2))
        d_context = d_context_ref[0, :, pair_columns(pair)]
        grads = attend_pair_back(
            queries, keys, values, t_queries, t_keys, log_ref[0, pair], dots_ref[0, pair], d_context, length
        )
        for i in range(3):
            d_joined[here, pair_columns(3 * pair + i)] = grads[i]
        for i, at in ((0, Q_QUERY), (2, Q_VALUE)):
            sums_ref[at : at + 1, pair_columns(pair)] += column_sum(grads[i].astype(F32))

    bound = clips[0]
    x = x_ref[0].astype(F32)
    a_in[here, :] = jnp.clip(x, -bound, bound).astype(BF16)
    d_a = nt(d_joined[here, :], w_qkv[...])
    inside = jnp.where(jnp.abs(x) < bound, 1.0, jnp.where(jnp.abs(x) == bound, 0.5, 0.0))
    input_ref[0] = (d_res_ref[0] + d_a * inside).astype(BF16)
    outside = (1.0 - inside) * d_a
    sums_ref[Q_CLIP : Q_CLIP + 1] += column_sum(jnp.where(x > 0, outside, -outside))

    @pl.when(row == pl.num_programs(0) - 1)
    def _():
        for i in range(3):
            g_qkv[:, D * i : D * (i + 1)] = tn(a_in[...], d_joined[:, D * i : D * (i + 1)]).astype(BF16)


def rows_spec(tokens, width):
    return pl.BlockSpec((1, tokens, width), lambda r, *_: (r, 0, 0))


def whole_spec(shape):
    return pl.BlockSpec(shape, lambda *_: (0,) * len(shape), pipeline_mode=pl.Buffered(1))


def smem_spec():
    return pl.BlockSpec(memory_space=pltpu.SMEM)


def params(**more):
    return pltpu.CompilerParams(vmem_limit_bytes=VMEM_LIMIT, **more)


def shaped(shape, dtype):
    return jax.ShapeDtypeStruct(shape, dtype)


def teacher_pass(lengths, x, w_qkv, w_out, w_up, w_down):
    rows, tokens, _ = x.shape
    return pl.pallas_call(
        teacher_kernel,
        grid=(rows,),
        in_specs=[smem_spec(), rows_spec(tokens, D)] + [whole_spec(w.shape) for w in (w_qkv, w_out, w_up, w_down)],
        out_specs=[rows_spec(tokens, 2 * D), rows_spec(tokens, D)],
        out_shape=[shaped((rows, tokens, 2 * D), BF16), shaped((rows, tokens, D), F32)],
        scratch_shapes=[pltpu.VMEM((tokens, D), BF16)],
        compiler_params=params(),
    )(lengths, x, w_qkv, w_out, w_up, w_down)


def student_attend(lengths, clips, x, w_qkv, bias_q, bias_v):
    rows, tokens, _ = x.shape
    logs = (1, PAIRS, 2, tokens)
    return pl.pallas_call(
        student_attend_kernel,
        grid=(rows,),
        in_specs=[smem_spec(), smem_spec(), rows_spec(tokens, D), whole_spec(w_qkv.shape)] + [whole_spec((1, D))] * 2,
        out_specs=[
            rows_spec(tokens, 3 * D),
            rows_spec(tokens, D),
            pl.BlockSpec(logs, lambda r: (r, 0, 0, 0)),
        ],
        out_shape=[
            shaped((rows, tokens, 3 * D), BF16),
            shaped((rows, tokens, D), F32),
            shaped((rows,) + logs[1:], F32),
        ],
        scratch_shapes=[pltpu.VMEM((tokens, D), BF16)],
        compiler_params=params(),
    )(lengths, clips, x, w_qkv, bias_q.reshape(1, D), bias_v.reshape(1, D))


def student_middle(lengths, clips, x, cotangent, final, context, weights, vectors):
    rows, tokens, _ = x.shape
    block = tokens // 2 if tokens % 32 == 0 else tokens
    wide = {"act": FF, "d_pre": FF}
    names = ("mixed", "act", "d_pre", "up_in", "d_down", "cut", "d_attn", "d_res", "d_context")

    def spec(width):
        return pl.BlockSpec((1, block, width), lambda r, i: (r, i, 0))

    return pl.pallas_call(
        student_middle_kernel,
        grid=(rows, tokens // block),
        in_specs=[smem_spec(), smem_spec()]
        + [spec(D)] * 4
        + [whole_spec(w.shape) for w in (*weights, *vectors)],
        out_specs=[spec(wide.get(name, D)) for name in names]
        + [pl.BlockSpec((1, PAIRS, 2, block), lambda r, i: (r, 0, 0, i)), whole_spec((S_ROWS, D))],
        out_shape=[
            shaped((rows, tokens, wide.get(name, D)), F32 if name == "d_res" else BF16) for name in names
        ]
        + [shaped((rows, PAIRS, 2, tokens), F32), shaped((S_ROWS, D), F32)],
        scratch_shapes=[pltpu.VMEM((block, FF), F32)],
        compiler_params=params(),
    )(lengths, clips, x, cotangent, final, context, *weights, *vectors)


def weight_grads(act, d_down, up_in, d_pre, cut, d_attn):
    flat = [v.reshape(-1, v.shape[-1]) for v in (act, d_down, up_in, d_pre, cut, d_attn)]
    tokens = flat[0].shape[0]
    chunk = pl.BlockSpec((tokens, D), lambda c: (0, c))
    same = whole_spec((tokens, D))
    return pl.pallas_call(
        weight_grads_kernel,
        grid=(CHUNKS,),
        in_specs=[chunk, same, same, chunk, same, same],
        out_specs=[
            pl.BlockSpec((D, D), lambda c: (c, 0)),
            pl.BlockSpec((D, D), lambda c: (0, c)),
            whole_spec((D, D)),
        ],
        out_shape=[shaped((FF, D), BF16), shaped((D, FF), BF16), shaped((D, D), BF16)],
        compiler_params=params(),
    )(*flat)


def student_back(lengths, clips, x, qkv, tqk, logs, dots, d_context, d_res, w_qkv):
    rows, tokens, _ = x.shape
    return pl.pallas_call(
        student_back_kernel,
        grid=(rows,),
        in_specs=[smem_spec(), smem_spec(), rows_spec(tokens, D), rows_spec(tokens, 3 * D), rows_spec(tokens, 2 * D)]
        + [pl.BlockSpec((1,) + logs.shape[1:], lambda r: (r, 0, 0, 0))] * 2
        + [rows_spec(tokens, D), rows_spec(tokens, D), whole_spec(w_qkv.shape)],
        out_specs=[rows_spec(tokens, D), whole_spec((D, 3 * D)), whole_spec((Q_ROWS, D))],
        out_shape=[shaped((rows, tokens, D), BF16), shaped((D, 3 * D), BF16), shaped((Q_ROWS, D), F32)],
        scratch_shapes=[pltpu.VMEM((rows * tokens, D), BF16), pltpu.VMEM((rows * tokens, 3 * D), BF16)],
        compiler_params=params(),
    )(lengths, clips, x, qkv, tqk, logs, dots, d_context, d_res, w_qkv)


PLANES, COLUMNS, CORES = 4, 4, 2
DEVICES = PLANES * COLUMNS * CORES


class Place:
    def __init__(self):
        self.me = lax.axis_index("shard")
        self.core = self.me % 2
        self.x = (self.me // 2) % 2
        self.y = (self.me // 4) % 2
        self.z = self.me // 8
        self.column = (self.me // 2) % 4
        self.along_x = self.me + 2 - 4 * self.x
        self.along_y = self.me + 4 - 8 * self.y
        self.sibling = self.me + 1 - 2 * self.core
        self.along_a = self.along_x + (self.along_y - self.along_x) * self.core
        self.along_b = self.along_y + (self.along_x - self.along_y) * self.core

    def plane(self, step):
        return (self.me + 8 * step) % DEVICES

    def meet(self):
        partners = [self.sibling, self.along_x, self.along_y] + [self.plane(k) for k in range(1, PLANES)]
        barrier = pltpu.get_barrier_semaphore()
        for partner in partners:
            pl.semaphore_signal(barrier, inc=1, device_id=(partner,), device_id_type=MESH)
        return functools.partial(pl.semaphore_wait, barrier, len(partners))


class Trip:
    SEMAPHORES = 14

    def __init__(self, place, source, out, rows, columns, early, send, receive):
        self.place, self.early, self.send, self.receive = place, early, send, receive
        self.source = source.at[rows, columns]
        height, size = source.shape[0], rows.stop - rows.start

        def where(column):
            start = pl.multiple_of(height * (column % CORES) + rows.start, 8)
            return column // CORES, pl.ds(start, size)

        def one(z, column):
            chip, inside = where(column)
            return out.at[z, chip, inside, columns]

        def slab_of(column):
            chip, inside = where(column)
            return out.at[:, chip, inside, columns]

        self.one, self.all = one, slab_of
        self.mine = place.me % 8
        self.at_a = self.mine + place.along_a - place.me
        self.at_b = self.mine + place.along_b - place.me
        self.at_ab = self.at_a + self.at_b - self.mine

    def remote(self, source, target, slot, device):
        return pltpu.make_async_remote_copy(
            src_ref=source, dst_ref=target, send_sem=self.send.at[slot], recv_sem=self.receive.at[slot],
            device_id=(device,), device_id_type=MESH,
        )

    def own(self):
        return pltpu.make_async_copy(self.source, self.one(self.place.z, self.mine), self.send.at[0])

    def line(self, step, source, column, slot):
        return self.remote(source, self.one(self.place.z, column), slot, self.place.plane(step))

    def line_from(self, step, column, slot):
        part = self.one((self.place.z + PLANES - step) % PLANES, column)
        return self.remote(part, part, slot, self.place.plane(step))

    def slab(self, column, slot, device):
        part = self.all(column)
        return self.remote(part, part, slot, device)

    def across(self, source, column):
        return self.remote(source, self.one(self.place.z, column), 4, self.place.along_a)

    def first(self):
        self.own().start()
        if self.early:
            self.across(self.source, self.mine).start()
        for step in range(1, PLANES):
            self.line(step, self.source, self.mine, step).start()

    def second(self):
        place = self.place
        self.own().wait()
        if self.early:
            part = self.one(place.z, self.at_a)
            self.across(part, self.at_a).wait_recv()
            for step in range(1, PLANES):
                self.line(step, part, self.at_a, 10 + step).start()
            return
        for step in range(1, PLANES):
            self.line_from(step, self.mine, step).wait_recv()
        self.slab(self.mine, 4, place.along_a).start()
        self.slab(self.mine, 5, place.along_b).start()
        self.slab(self.mine, 7, place.sibling).start()

    def third(self):
        place = self.place
        if self.early:
            for step in range(1, PLANES):
                self.line_from(step, self.mine, step).wait_recv()
                self.line_from(step, self.at_a, 10 + step).wait_recv()
            self.slab(self.mine, 5, place.along_b).start()
            self.slab(self.mine, 7, place.sibling).start()
        else:
            self.slab(self.at_a, 4, place.along_a).wait_recv()
        self.slab(self.at_a, 6, place.along_b).start()
        self.slab(self.at_a, 8, place.sibling).start()

    def fourth(self):
        place = self.place
        self.slab(self.at_b, 5, place.along_b).wait_recv()
        self.slab(self.at_b, 9, place.sibling).start()
        self.slab(self.at_ab, 6, place.along_b).wait_recv()
        self.slab(self.at_ab, 10, place.sibling).start()

    def fifth(self):
        for slot in range(7, 11):
            self.slab(self.mine, slot, self.place.sibling).wait_recv()

    def phases(self):
        return [self.first, self.second, self.third, self.fourth, self.fifth]

    def last(self):
        one = self.one(self.place.z, self.mine)
        for step in range(1, PLANES):
            self.line(step, one, self.mine, step).wait_send()
            if self.early:
                self.line(step, one, self.mine, 10 + step).wait_send()
        if self.early:
            self.across(one, self.mine).wait_send()
        for slot in range(5 if self.early else 4, 11):
            self.slab(self.mine, slot, self.place.sibling).wait_send()


T_QKV, T_OUT, T_UP, T_DOWN, B_QKV, B_OUT, B_UP, B_DOWN = range(8)
TRAVEL = ((T_QKV, 6), (B_QKV, 2), (T_OUT, 1), (T_DOWN, 1), (T_UP, 2), (B_OUT, 1), (B_DOWN, 1), (B_UP, 2))
EARLY = (T_UP, B_UP,)
TALL = (T_DOWN, B_DOWN)
FORWARD_PLAN = (
    (0, 0, 0), (0, 1, 0), (0, 2, 0), (0, 3, 0), (0, 4, 0), (0, 0, 1), (0, 5, 0), (0, 1, 1), (0, 6, 0), (0, 2,
    1), (0, 3, 1), (0, 0, 2), (0, 4, 1), (0, 1, 2), (0, 5, 1), (0, 2, 2), (0, 3, 2), (0, 0, 3), (0, 7, 0), (0,
    6, 1), (0, 4, 2), (0, 1, 3), (0, 0, 4), (0, 2, 3), (0, 3, 3), (0, 5, 2), (0, 8, 0), (0, 1, 4), (1, 4, 3),
    (1, 7, 1), (1, 9, 0), (2, 2, 4), (2, 3, 4), (2, 5, 3), (2, 6, 2), (3, 4, 4), (3, 8, 1), (4, 5, 4), (6, 7,
    2), (7, 10, 0), (8, 6, 3), (8, 8, 2), (9, 7, 3), (9, 9, 1), (9, 10, 1), (10, 6, 4), (11, 7, 4), (11, 8, 3),
    (13, 8, 4), (13, 11, 0), (15, 10, 2), (16, 11, 1), (18, 9, 2), (19, 12, 0), (21, 10, 3), (21, 13, 0), (21,
    11, 2), (23, 12, 1), (24, 9, 3), (24, 10, 4), (27, 9, 4), (27, 14, 0), (28, 11, 3), (28, 12, 2), (29, 13,
    1), (29, 14, 1), (31, 11, 4), (31, 12, 3), (33, 12, 4), (33, 15, 0), (35, 14, 2), (36, 15, 1), (37, 13, 2),
    (41, 14, 3), (41, 15, 2), (43, 13, 3), (44, 14, 4), (46, 13, 4), (46, 15, 3), (48, 15, 4),
)


def travel_parts(shapes):
    parts = []
    for weight, pieces in TRAVEL:
        rows, width = shapes[weight]
        for i in range(pieces):
            if weight in TALL:
                parts.append((weight, slice(i * rows // pieces, (i + 1) * rows // pieces), slice(0, width)))
            else:
                lanes = width // 128
                columns = slice(i * lanes // pieces * 128, (i + 1) * lanes // pieces * 128)
                parts.append((weight, slice(0, rows), columns))
    return parts


def choose(index, slots, stage):
    if len(slots) == 1:
        pl.when(index == slots[0])(functools.partial(stage, slots[0]))
    elif slots:
        low, high = slots[: len(slots) // 2], slots[len(slots) // 2 :]
        pl.when(index < high[0])(functools.partial(choose, index, low, stage))
        pl.when(index >= high[0])(functools.partial(choose, index, high, stage))


def forward_kernel(*refs):
    lengths, clips = refs[:2]
    teacher_hbm, hidden_hbm = refs[2:4]
    teach, latent, (bias_q, bias_v) = refs[4:8], refs[8:12], refs[12:14]
    outs = refs[14:22]
    tqk_hbm, final_hbm, qkv_hbm, context_hbm, log_hbm = refs[22:27]
    low, near, biases = refs[27:32], refs[32:37], refs[37]
    t_x, a_in, tqk, t_context, final, qkv, context, logs = refs[38:46]
    send, receive, load, store = refs[46:]
    rows = t_x.shape[0]
    place = Place()
    all_here = place.meet()
    inputs = [pltpu.make_async_copy(teacher_hbm, t_x, load.at[0]), pltpu.make_async_copy(hidden_hbm, a_in, load.at[1])]
    for copy in inputs:
        copy.start()
    for pair in range(PAIRS):
        for i in range(3):
            to, at = TRIPLE * pair + PAIR * i, D * i + PAIR * pair
            low[4][:, to : to + PAIR] = teach[0][:, at : at + PAIR]
    all_here()
    sources = [low[4], *teach[1:], *low[:4]]
    parts = travel_parts([source.shape for source in sources])
    trips = [
        Trip(place, sources[w], outs[w], r, c, w in EARLY, send.at[i], receive.at[i])
        for i, (w, r, c) in enumerate(parts)
    ]
    weights = [w for w, _, _ in parts]

    def landing(i):
        weight, r, c = parts[i]
        if weight in TALL:
            c = slice(0, near[weight].shape[1])
        flat = outs[weight].reshape(near[weight].shape)
        return pltpu.make_async_copy(flat.at[:, c], near[weight].at[:, c], load.at[2 + i])

    def lands(i):
        weight = weights[i]
        return weight <= B_QKV and (weight not in TALL or weight not in weights[i + 1 :])

    def binarize():
        for i in range(1, 4):
            low[i][...] = signed_mean(latent[i][...])
        b_qkv = signed_mean(latent[0][...])
        for pair in range(PAIRS):
            for i in range(3):
                to, at = TRIPLE * pair + PAIR * i, D * i + PAIR * pair
                low[0][:, to : to + PAIR] = b_qkv[:, at : at + PAIR]
        biases[0:1] = bias_q[...].reshape(1, D)
        biases[1:2] = bias_v[...].reshape(1, D)

    phases = [trip.phases() for trip in trips]
    first_student = next(at for at, (_, i, _) in enumerate(FORWARD_PLAN) if weights[i] >= B_QKV)

    def do(at):
        _, i, phase = FORWARD_PLAN[at]
        if at == first_student:
            binarize()
        phases[i][phase]()
        if phase == 4 and lands(i):
            landing(i).start()

    counts = (PAIRS * rows, PAIRS * rows, CHUNKS * rows)
    stage_two, stage_three, end = counts[0], counts[0] + counts[1], sum(counts)
    per = {weight: [i for i, w in enumerate(weights) if w == weight and lands(i)] for weight in set(weights)}

    def stage(slot):
        for at, (when, _, _) in enumerate(FORWARD_PLAN):
            if when == slot:
                do(at)

    def turn(first_slot, count, index):
        planned = sorted({when for when, _, _ in FORWARD_PLAN if first_slot <= when < first_slot + count})
        choose(index + first_slot, planned, stage)

    def await_parts(weight, pair, row):
        pairs_each = PAIRS // len(per[weight])
        for n, part in enumerate(per[weight]):
            pl.when(jnp.logical_and(pair == n * pairs_each, row == 0))(landing(part).wait)

    def out_copy(source, target, slot, row):
        return pltpu.make_async_copy(source.at[row], target.at[row], store.at[slot, row])

    inputs[0].wait()
    inputs[1].wait()

    @pl.loop(0, rows)
    def _(row):
        a_in[row] = jnp.clip(a_in[row].astype(F32), -clips[0], clips[0]).astype(BF16)

    @pl.loop(0, PAIRS)
    def _(pair):
        @pl.loop(0, rows)
        def _(row):
            turn(0, counts[0], pair * rows + row)
            await_parts(T_QKV, pair, row)
            teacher_pair(pair, t_x[row], lengths[row], near[T_QKV], tqk.at[row], t_context.at[row])

    for row in range(rows):
        out_copy(tqk, tqk_hbm, 0, row).start()

    @pl.loop(0, PAIRS)
    def _(pair):
        @pl.loop(0, rows)
        def _(row):
            turn(stage_two, counts[1], pair * rows + row)
            await_parts(B_QKV, pair, row)
            student_pair(
                pair, a_in[row], lengths[row], near[B_QKV], biases.at[0:1], biases.at[1:2],
                qkv.at[row], context.at[row], logs.at[row],
            )

    for row in range(rows):
        out_copy(qkv, qkv_hbm, 2, row).start()
        out_copy(context, context_hbm, 3, row).start()
        out_copy(logs, log_hbm, 4, row).start()
    stage(stage_three)
    for weight in (T_OUT, T_UP, T_DOWN):
        for part in per[weight]:
            landing(part).wait()

    @pl.loop(0, rows)
    def _(row):
        final[row] = teacher_last(
            t_x[row], t_context[row], near[T_OUT], near[T_UP], near[T_DOWN],
            lambda c: turn(stage_three + 1, counts[2] - 1, row * CHUNKS + c - 1),
        )
        out_copy(final, final_hbm, 1, row).start()

    stage(end)
    for trip in trips:
        trip.last()

    @pl.loop(0, rows)
    def _(row):
        for slot, (source, target) in enumerate(
            ((tqk, tqk_hbm), (final, final_hbm), (qkv, qkv_hbm), (context, context_hbm), (logs, log_hbm))
        ):
            out_copy(source, target, slot, row).wait()


def forward_pass(lengths, clips, teacher_input, hidden, teach, latent, bias_q, bias_v):
    rows, tokens, _ = hidden.shape
    anywhere, vmem = pl.BlockSpec(memory_space=pl.ANY), pl.BlockSpec(memory_space=pltpu.VMEM)
    gathered = [(PLANES, COLUMNS, CORES * w.shape[0], w.shape[1]) for w in teach] * 2
    made = [
        shaped((rows, tokens, 2 * D), BF16),
        shaped((rows, tokens, D), F32),
        shaped((rows, tokens, 3 * D), BF16),
        shaped((rows, tokens, D), F32),
        shaped((rows, PAIRS, 2, tokens), F32),
    ]
    parts = sum(pieces for _, pieces in TRAVEL)
    near = [(DEVICES * w.shape[0], w.shape[1]) for w in teach] + [(DEVICES * teach[0].shape[0], 3 * D)]
    x_scratch = pltpu.VMEM((rows, tokens, D), BF16)
    outs = pl.pallas_call(
        forward_kernel,
        in_specs=[smem_spec(), smem_spec()] + [anywhere] * 2 + [vmem] * 10,
        out_specs=[anywhere] * 13,
        out_shape=[shaped(shape, BF16) for shape in gathered] + made,
        scratch_shapes=[pltpu.VMEM(w.shape, BF16) for w in (*latent, teach[0])]
        + [pltpu.VMEM(shape, BF16) for shape in near]
        + [pltpu.VMEM((8, D), F32), x_scratch, x_scratch]
        + [pltpu.VMEM(made[0].shape, BF16), x_scratch]
        + [pltpu.VMEM(m.shape, m.dtype) for m in made[1:]]
        + [pltpu.SemaphoreType.DMA((parts, Trip.SEMAPHORES))] * 2
        + [pltpu.SemaphoreType.DMA((2 + parts,)), pltpu.SemaphoreType.DMA((5, rows))],
        compiler_params=params(collective_id=0, has_side_effects=True),
    )(lengths, clips, teacher_input, hidden, *teach, *latent, bias_q, bias_v)
    weights = [out.reshape(-1, out.shape[-1]) for out in outs[4:8]]
    return weights, outs[8:]


class Fold:
    SEMAPHORES = 8

    def __init__(self, place, grad, own, finish, buffers, send, receive):
        self.place, self.grad, self.own, self.finish = place, grad, own, finish
        self.from_core, self.to_p, self.from_p, self.to_q, self.from_q, self.to_z, self.from_z = buffers
        self.send, self.receive = send, receive
        core = place.core
        self.p_stride, self.q_stride = 1 + core, 2 - core
        self.p = place.x + (place.y - place.x) * core
        self.q = place.y + (place.x - place.y) * core

    def remote(self, source, target, slot, device):
        return pltpu.make_async_remote_copy(
            src_ref=source, dst_ref=target, send_sem=self.send.at[slot], recv_sem=self.receive.at[slot],
            device_id=(device,), device_id_type=MESH,
        )

    def column(self, p, q):
        return p * self.p_stride + q * self.q_stride

    def keep(self):
        return pltpu.make_async_copy(self.grad.at[:, :, self.place.core], self.own, self.send.at[0])

    def over_core(self):
        return self.remote(self.grad.at[:, :, 1 - self.place.core], self.from_core, 1, self.place.sibling)

    def over_p(self):
        return self.remote(self.to_p, self.from_p, 2, self.place.along_a)

    def over_q(self):
        return self.remote(self.to_q, self.from_q, 3, self.place.along_b)

    def over_z(self, step):
        return self.remote(self.to_z.at[step - 1], self.from_z.at[step - 1], 3 + step, self.place.plane(step))

    def mine(self, z, column):
        return self.grad[z, column, self.place.core] if self.own is None else self.own[z, column]

    def pair_sum(self, z, column):
        return self.mine(z, column).astype(F32) + self.from_core[z, column].astype(F32)

    def first(self):
        if self.own is not None:
            self.keep().start()
        self.over_core().start()

    def second(self):
        if self.own is not None:
            self.keep().wait()
        self.over_core().wait_recv()

        @pl.loop(0, 2 * PLANES)
        def _(i):
            z, q = i // 2, i % 2
            column = self.column(1 - self.p, q)
            self.to_p[z, q] = self.mine(z, column) + self.from_core[z, column]

        self.over_p().start()

    def third(self):
        self.over_p().wait_recv()

        @pl.loop(0, PLANES)
        def _(z):
            q = 1 - self.q
            total = self.pair_sum(z, self.column(self.p, q)) + self.from_p[z, q].astype(F32)
            self.to_q[z] = total.astype(BF16)

        self.over_q().start()

    def quad_sum(self, z):
        q = self.q
        total = self.pair_sum(z, self.column(self.p, q)) + self.from_p[z, q].astype(F32)
        return total + self.from_q[z].astype(F32)

    def fourth(self):
        self.over_q().wait_recv()
        for step in range(1, PLANES):
            self.to_z[step - 1] = self.quad_sum((self.place.z + step) % PLANES).astype(BF16)
            self.over_z(step).start()

    def fifth(self):
        total = self.quad_sum(self.place.z)
        for step in range(1, PLANES):
            self.over_z(step).wait_recv()
            total = total + self.from_z[step - 1].astype(F32)
        self.finish(total)

    def phases(self):
        return [self.first, self.second, self.third, self.fourth, self.fifth]

    def last(self):
        self.over_core().wait_send()
        self.over_p().wait_send()
        self.over_q().wait_send()
        for step in range(1, PLANES):
            self.over_z(step).wait_send()


FOLD_BUFFERS = ((4, 4), (4, 2), (4, 2), (4,), (4,), (3,), (3,))


class Share:
    SEMAPHORES = 7

    def __init__(self, place, value, out, partial, received, send, receive):
        self.place, self.value, self.out = place, value, out
        self.partial, self.received, self.send, self.receive = partial, received, send, receive

    def swap(self, slot, device):
        return pltpu.make_async_remote_copy(
            src_ref=self.partial.at[min(slot, 3)], dst_ref=self.received.at[slot], send_sem=self.send.at[slot],
            recv_sem=self.receive.at[slot], device_id=(device,), device_id_type=MESH,
        )

    def partners(self):
        place = self.place
        return [place.sibling, place.along_x, place.along_y] + [place.plane(k) for k in range(1, PLANES)]

    def first(self):
        self.partial[0] = self.value[...]
        self.swap(0, self.place.sibling).start()

    def step(self, at):
        partners = self.partners()
        self.swap(at, partners[at]).wait_recv()
        self.partial[at + 1] = self.partial[at] + self.received[at]
        for slot in (at + 1,) if at < 2 else (3, 4, 5):
            self.swap(slot, partners[slot]).start()

    def finish(self):
        partners = self.partners()
        for slot in (3, 4, 5):
            self.swap(slot, partners[slot]).wait_recv()
        place = self.place
        self.received[6] = self.partial[3]
        total = jnp.zeros(self.value.shape, F32)
        for z in range(PLANES):
            behind = (place.z + PLANES - z) % PLANES
            total = total + self.received[(behind + 3) % PLANES + 3]
        self.out[...] = total

    def phases(self):
        return [self.first] + [functools.partial(self.step, at) for at in range(3)] + [self.finish]

    def last(self):
        for slot, partner in enumerate(self.partners()):
            self.swap(slot, partner).wait_send()


GRAD_STEPS = 2 * CHUNKS + 1
FOLDED = ((0, 4), (1, 4), (2, 1))
FOLD_PARTS = sum(pieces for _, pieces in FOLDED)
BACKWARD_PLAN = (
    (5, 0, 0), (5, 1, 0), (5, 2, 0), (5, 3, 0), (6, 4, 0), (7, 5, 0), (8, 6, 0), (9, 0, 1), (9, 7, 0), (9, 8,
    0), (11, 1, 1), (12, 9, 0), (12, 0, 2), (12, 2, 1), (12, 15, 0), (13, 1, 2), (14, 9, 1), (14, 15, 1), (15,
    10, 0), (15, 0, 3), (15, 1, 3), (15, 2, 2), (15, 3, 1), (16, 9, 2), (16, 15, 2), (17, 10, 1), (18, 11, 0),
    (18, 0, 4), (18, 1, 4), (18, 2, 3), (18, 3, 2), (18, 4, 1), (18, 9, 3), (18, 15, 3), (19, 10, 2), (20, 5,
    1), (20, 11, 1), (21, 12, 0), (21, 2, 4), (21, 3, 3), (21, 4, 2), (21, 6, 1), (21, 9, 4), (21, 10, 3), (21,
    15, 4), (22, 11, 2), (23, 5, 2), (23, 7, 1), (23, 12, 1), (24, 13, 0), (24, 3, 4), (24, 4, 3), (24, 6, 2),
    (24, 10, 4), (24, 11, 3), (25, 8, 1), (26, 5, 3), (26, 12, 2), (26, 13, 1), (26, 7, 2), (27, 14, 0), (27, 4,
    4), (27, 6, 3), (27, 8, 2), (27, 11, 4), (28, 12, 3), (29, 5, 4), (30, 7, 3), (30, 8, 3), (30, 13, 2), (30,
    14, 1), (30, 16, 0), (30, 6, 4), (30, 12, 4), (30, 16, 1), (30, 13, 3), (30, 14, 2), (30, 16, 2), (30, 14,
    3), (30, 16, 3), (30, 7, 4), (30, 8, 4), (30, 13, 4), (30, 16, 4), (30, 14, 4),
)


def fold_parts(shapes):
    parts = []
    for i, pieces in FOLDED:
        rows, width = shapes[i]
        for at in range(pieces):
            if i == 0:
                size = rows // pieces
                parts.append((i, slice(at * size, (at + 1) * size), slice(0, width), (size, width)))
            else:
                size = width // pieces
                parts.append((i, slice(0, rows), slice(at * size, (at + 1) * size), (rows, size)))
    return parts


def backward_kernel(*refs):
    lengths, clips = refs[:2]
    qkv, tqk, logs, dots, d_context, w_triple = refs[2:8]
    (x_hbm, d_res_hbm), (act, d_down, up_in, d_pre, cut, d_attn), sums = refs[8:10], refs[10:16], refs[16]
    input_hbm, grads = refs[17], refs[18:21]
    g_down, g_up, g_out, g_qkv, sums_out, q_sums_out = refs[21:27]
    x, a_in_t, d_pair, d_a, d_res, g_pair, q_sums, ring, stage_tall, stage_wide = refs[27:37]
    scratch = refs[37:]
    rows, tokens = qkv.shape[0], qkv.shape[1]
    place = Place()
    at_step = pl.program_id(0)
    at_pair = at_step - GRAD_STEPS
    parts = fold_parts([g_down.shape, g_up.shape, g_out.shape])
    owns, scratch = scratch[:FOLD_PARTS], scratch[FOLD_PARTS:]
    per = len(FOLD_BUFFERS)
    taken = (FOLD_PARTS + PAIRS) * per
    buffers, (s_partial, s_received, q_partial, q_received, send, receive, load) = scratch[:taken], scratch[taken:]

    def set_part(target, r, c):
        def finish(total):
            target[r, c] = total

        return finish

    def set_triple(pair):
        def finish(total):
            for i in range(3):
                at = D * i + PAIR * pair
                g_qkv[:, at : at + PAIR] = total[:, PAIR * i : PAIR * (i + 1)]

        return finish

    folds = []
    for n, (i, r, c, _) in enumerate(parts):
        target = (g_down, g_up, g_out)[i]
        source = grads[i].at[:, :, :, r, c]
        folds.append(
            Fold(place, source, owns[n], set_part(target, r, c), buffers[per * n : per * n + per], send.at[n], receive.at[n])
        )
    for pair in range(PAIRS):
        n = FOLD_PARTS + pair
        folds.append(
            Fold(
                place, g_pair.at[pair], None, set_triple(pair), buffers[per * n : per * n + per], send.at[n], receive.at[n]
            )
        )
    n = len(folds)
    share = Share(place, sums, sums_out, s_partial, s_received, send.at[n], receive.at[n])
    q_share = Share(place, q_sums, q_sums_out, q_partial, q_received, send.at[n + 1], receive.at[n + 1])
    inputs = [pltpu.make_async_copy(x_hbm, x, load.at[0]), pltpu.make_async_copy(d_res_hbm, d_res, load.at[1])]

    slots = GRAD_STEPS + PAIRS * rows
    phases = [fold.phases() for fold in folds] + [share.phases(), q_share.phases()]
    timed = [
        (slot, phases[i][phase]) for slot, i, phase in BACKWARD_PLAN if phase or not FOLD_PARTS <= i < FOLD_PARTS + PAIRS
    ]

    def stage(slot):
        for when, act in timed:
            if when == slot:
                act()

    def turn(index):
        choose(index, sorted({when for when, _ in timed if when < slots}), stage)

    def load_left(source):
        return pltpu.make_async_copy(source, x, load.at[2])

    def chunk(source, c, step):
        part = source.at[:, :, pl.ds(pl.multiple_of(c * D, D), D)]
        return pltpu.make_async_copy(part, ring.at[step % 2], load.at[3 + step % 2])

    def load_chunk(step):
        pl.when(step < CHUNKS)(lambda: chunk(act, step, step).start())
        pl.when(jnp.logical_and(step >= CHUNKS, step < 2 * CHUNKS))(lambda: chunk(d_pre, step - CHUNKS, step).start())
        pl.when(step == 2 * CHUNKS)(lambda: chunk(d_attn, 0, step).start())

    def tall_out(c):
        return pltpu.make_async_copy(stage_tall, grads[0].at[c], load.at[5])

    def wide_out(c):
        columns = pl.ds(pl.multiple_of(c * D, D), D)
        return pltpu.make_async_copy(stage_wide, grads[1].at[:, :, :, :, columns], load.at[6])

    out_out = pltpu.make_async_copy(stage_wide, grads[2], load.at[6])

    @pl.when(at_step == 0)
    def _():
        all_here = place.meet()
        load_left(d_down).start()
        load_chunk(0)
        inputs[1].start()
        q_sums[...] = jnp.zeros_like(q_sums)
        d_a[...] = jnp.zeros_like(d_a)
        all_here()

    @pl.when(at_step < GRAD_STEPS)
    def _():
        turn(at_step)
        for step, following in ((0, up_in), (CHUNKS, cut), (2 * CHUNKS, None)):

            @pl.when(at_step == step)
            def _():
                load_left(d_down).wait()
                a_in_t[...] = x[...].reshape(rows * tokens, D).T
                (inputs[0] if following is None else load_left(following)).start()

        chunk(act, 0, at_step).wait()
        load_chunk(at_step + 1)
        product = nn(a_in_t[...], ring[at_step % 2].reshape(rows * tokens, D))

        @pl.when(at_step < CHUNKS)
        def _():
            pl.when(at_step > 0)(tall_out(0).wait)
            stage_tall[...] = product.T.reshape(stage_tall.shape).astype(BF16)
            tall_out(at_step).start()

        @pl.when(at_step >= CHUNKS)
        def _():
            pl.when(at_step == CHUNKS)(tall_out(0).wait)
            pl.when(at_step > CHUNKS)(wide_out(0).wait)
            height = stage_wide.shape[3]
            for device in range(DEVICES):
                z, column, core = device // 8, device // 2 % COLUMNS, device % CORES
                stage_wide[z, column, core] = product[height * device : height * (device + 1)].astype(BF16)
            pl.when(at_step < 2 * CHUNKS)(lambda: wide_out(at_step - CHUNKS).start())
            pl.when(at_step == 2 * CHUNKS)(out_out.start)

    pl.when(at_step == GRAD_STEPS)(out_out.wait)

    def pair_step():
        one_pair(
            lengths, clips, at_pair, turn, stage, slots, folds, timed, share, q_share, inputs, input_hbm, load,
            qkv, tqk, logs, dots, d_context, w_triple, g_qkv.shape[0], x, a_in_t, d_pair, d_a, d_res, g_pair, q_sums,
        )

    pl.when(at_pair >= 0)(pair_step)


def one_pair(
    lengths, clips, at_pair, turn, stage, slots, folds, timed, share, q_share, inputs, input_hbm, load,
    qkv, tqk, logs, dots, d_context, w_triple, height, x, a_in_t, d_pair, d_a, d_res, g_pair, q_sums,
):
    rows, tokens = qkv.shape[0], qkv.shape[1]

    @pl.loop(0, rows)
    def _(row):
        turn(GRAD_STEPS + at_pair * rows + row)
        queries, keys, values = (qkv[row, :, PAIR * i : PAIR * (i + 1)] for i in range(3))
        t_queries, t_keys = (tqk[row, :, PAIR * i : PAIR * (i + 1)] for i in range(2))
        grads_here = attend_pair_back(
            queries, keys, values, t_queries, t_keys, logs[row, 0], dots[row, 0], d_context[row], lengths[row]
        )
        here = pl.ds(pl.multiple_of(row * tokens, tokens), tokens)
        for i in range(3):
            d_pair[here, PAIR * i : PAIR * (i + 1)] = grads_here[i]

    bound = clips[0]

    @pl.when(at_pair == 0)
    def _():
        inputs[0].wait()
        for row in range(rows):
            clipped = jnp.clip(x[row].astype(F32), -bound, bound)
            a_in_t[:, tokens * row : tokens * (row + 1)] = clipped.T.astype(BF16)

    g_now = nn(a_in_t[...], d_pair[...])
    for device in range(DEVICES):
        z, column, core = device // 8, device // 2 % COLUMNS, device % CORES
        g_pair[at_pair, z, column, core] = g_now[height * device : height * (device + 1)].astype(BF16)
    for pair, fold in enumerate(folds[FOLD_PARTS:]):
        pl.when(at_pair == pair)(fold.first)
    here = pair_columns(at_pair)
    q_sums[Q_QUERY : Q_QUERY + 1, here] = column_sum(d_pair[:, :PAIR].astype(F32))
    q_sums[Q_VALUE : Q_VALUE + 1, here] = column_sum(d_pair[:, 2 * PAIR :].astype(F32))
    d_a[...] += nt(d_pair[...], w_triple[...])

    @pl.when(at_pair == PAIRS - 1)
    def _():
        inputs[1].wait()
        for row in range(rows):
            stage(slots + row)
            value = x[row].astype(F32)
            d_row = d_a[tokens * row : tokens * (row + 1)]
            inside = jnp.where(jnp.abs(value) < bound, 1.0, jnp.where(jnp.abs(value) == bound, 0.5, 0.0))
            outside = (1.0 - inside) * d_row
            q_sums[Q_CLIP : Q_CLIP + 1] += column_sum(jnp.where(value > 0, outside, -outside))
            x[row] = (d_res[row] + d_row * inside).astype(BF16)
        out = pltpu.make_async_copy(x, input_hbm, load.at[0])
        out.start()
        for when, act in timed:
            if when >= slots + rows:
                act()
        for fold in folds:
            fold.last()
        share.last()
        q_share.last()
        out.wait()


def backward_pass(lengths, clips, hidden, qkv, tqk, logs, dots, d_context, d_res, w_qkv, made_by, sums):
    rows, tokens, _ = hidden.shape
    shapes = [(FF // DEVICES, D), (D // DEVICES, FF), (D // DEVICES, D)]
    height = w_qkv.shape[0] // DEVICES
    part_shapes = [part[3] for part in fold_parts(shapes)]
    fold_shapes = part_shapes + [(height, TRIPLE)] * PAIRS
    anywhere = pl.BlockSpec(memory_space=pl.ANY)

    def of_pair(width):
        return pl.BlockSpec((rows, tokens, width), lambda s: (0, 0, pair_at(s)))

    def pair_at(step):
        return step // GRAD_STEPS * (step - GRAD_STEPS)

    stat = pl.BlockSpec((rows, 1, 2, tokens), lambda s: (0, pair_at(s), 0, 0))
    small = [shaped(sums.shape, F32), shaped((Q_ROWS, D), F32)]
    made = [shaped(s, F32) for s in shapes] + [shaped((height, 3 * D), F32)] + small
    return pl.pallas_call(
        backward_kernel,
        grid=(GRAD_STEPS + PAIRS,),
        in_specs=[smem_spec(), smem_spec()]
        + [of_pair(TRIPLE), of_pair(DOUBLE), stat, stat, of_pair(PAIR), pl.BlockSpec((D, TRIPLE), lambda s: (0, pair_at(s)))]
        + [anywhere] * 8
        + [whole_spec(sums.shape)],
        out_specs=[anywhere] * 4 + [whole_spec(m.shape) for m in made],
        out_shape=[shaped(hidden.shape, BF16)]
        + [shaped((PLANES, COLUMNS, CORES) + shape, BF16) for shape in shapes]
        + made,
        scratch_shapes=[
            pltpu.VMEM((rows, tokens, D), BF16),
            pltpu.VMEM((D, rows * tokens), BF16),
            pltpu.VMEM((rows * tokens, TRIPLE), BF16),
            pltpu.VMEM((rows * tokens, D), F32),
            pltpu.VMEM((rows, tokens, D), F32),
            pltpu.VMEM((PAIRS, PLANES, COLUMNS, CORES, height, TRIPLE), BF16),
            pltpu.VMEM((Q_ROWS, D), F32),
            pltpu.VMEM((2, rows, tokens, D), BF16),
            pltpu.VMEM((COLUMNS, CORES) + shapes[0], BF16),
            pltpu.VMEM((PLANES, COLUMNS, CORES) + shapes[2], BF16),
        ]
        + [pltpu.VMEM((PLANES, COLUMNS) + s, BF16) for s in part_shapes]
        + [pltpu.VMEM(lead + s, BF16) for s in fold_shapes for lead in FOLD_BUFFERS]
        + [pltpu.VMEM((n,) + m.shape, F32) for m in small for n in (4, 7)]
        + [pltpu.SemaphoreType.DMA((len(fold_shapes) + 2, Fold.SEMAPHORES))] * 2
        + [pltpu.SemaphoreType.DMA((7,))],
        compiler_params=params(collective_id=1, has_side_effects=True),
    )(
        lengths, clips, qkv, tqk, logs, dots, d_context, w_qkv, hidden, d_res, *made_by, sums
    )


def finish_kernel(sums, q_sums, *refs):
    grads, input_hbm = refs[:4], refs[4]
    outs, input_out = refs[5:9], refs[9]
    b_q, b_v, b_out, b_up, b_down, gain_one, shift_one, gain_two, shift_two, clips = refs[10:20]
    held, arrive = refs[20:]
    rows = held.shape[0]
    copies = [pltpu.make_async_copy(input_hbm.at[i], held.at[i], arrive.at[i]) for i in range(rows)]
    for copy in copies:
        copy.start()

    def row(ref, at):
        return ref[at : at + 1].reshape(D)

    for source, target in zip(grads, outs):
        target[...] = source[...]
    backs = [pltpu.make_async_copy(held.at[i], input_out.at[i], arrive.at[rows + i]) for i in range(rows)]
    for copy, back in zip(copies, backs):
        copy.wait()
        back.start()
    b_q[...] = row(q_sums, Q_QUERY)
    b_v[...] = row(q_sums, Q_VALUE)
    b_out[...] = row(sums, S_OUT)
    b_up[...] = jnp.concatenate([sums[S_UP + c : S_UP + c + 1] for c in range(CHUNKS)], axis=1).reshape(FF)
    b_down[...] = row(sums, S_DOWN)
    gain_one[...] = row(sums, S_GAIN_ONE)
    shift_one[...] = row(sums, S_SHIFT_ONE)
    gain_two[...] = row(sums, S_GAIN_TWO)
    shift_two[...] = row(sums, S_SHIFT_TWO)
    clips[0] = jnp.sum(q_sums[Q_CLIP : Q_CLIP + 1])
    for i, at in enumerate((S_CLIP_ONE, S_CLIP_TWO, S_CLIP_THREE)):
        clips[1 + i] = jnp.sum(sums[at : at + 1])
    for copy in backs:
        copy.wait()


def finish(sums, q_sums, grads, input_grad):
    vmem, anywhere = pl.BlockSpec(memory_space=pltpu.VMEM), pl.BlockSpec(memory_space=pl.ANY)
    lengths = [D, D, D, FF, D, D, D, D, D]
    return pl.pallas_call(
        finish_kernel,
        in_specs=[vmem] * 6 + [anywhere],
        out_specs=[vmem] * 4 + [anywhere] + [vmem] * 9 + [smem_spec()],
        out_shape=[shaped(g.shape, F32) for g in grads]
        + [shaped(input_grad.shape, BF16)]
        + [shaped((n,), F32) for n in lengths]
        + [shaped((4,), F32)],
        scratch_shapes=[pltpu.VMEM(input_grad.shape, BF16), pltpu.SemaphoreType.DMA((2 * input_grad.shape[0],))],
        compiler_params=params(),
    )(sums, q_sums, *grads, input_grad)


def on_device(
    by_kernel,
    hidden, teacher_input, cotangent, lengths, lat_qkv, lat_out, lat_up, lat_down,
    bias_q, bias_v, bias_out, bias_up, bias_down, gain_one, shift_one, gain_two, shift_two, clips,
    teach_qkv, teach_out, teach_up, teach_down,
):
    latent = (lat_qkv, lat_out, lat_up, lat_down)
    teach = (teach_qkv, teach_out, teach_up, teach_down)
    if by_kernel:
        (w_qkv, *weights), (tqk, final, qkv, context, logs) = forward_pass(
            lengths, clips, teacher_input, hidden, teach, latent, bias_q, bias_v
        )
    else:
        gather = functools.partial(lax.all_gather, axis_name="shard", axis=0, tiled=True)
        w_qkv, *weights = (gather(signed_mean(w)) for w in latent)
        w_qkv = by_pairs(w_qkv)
        t_qkv, *t_weights = (gather(w) for w in teach)
        tqk, final = teacher_pass(lengths, teacher_input, by_pairs(t_qkv), *t_weights)
        qkv, context, logs = student_attend(lengths, clips, hidden, w_qkv, bias_q, bias_v)
    vectors = (bias_out, bias_up, bias_down, gain_one, shift_one, gain_two, shift_two)
    mixed, act, d_pre, up_in, d_down, cut, d_attn, d_res, d_context, dots, sums = student_middle(
        lengths, clips, hidden, cotangent, final, context, weights, vectors
    )
    made_by = (act, d_down, up_in, d_pre, cut, d_attn)
    if by_kernel:
        input_grad, _, _, _, g_down, g_up, g_out, g_qkv, sums, q_sums = backward_pass(
            lengths, clips, hidden, qkv, tqk, logs, dots, d_context, d_res, w_qkv, made_by, sums
        )
    else:
        g_down, g_up, g_out = weight_grads(*made_by)
        input_grad, g_qkv, q_sums = student_back(lengths, clips, hidden, qkv, tqk, logs, dots, d_context, d_res, w_qkv)
        scatter = functools.partial(lax.psum_scatter, axis_name="shard", scatter_dimension=0, tiled=True)
        g_down, g_up, g_qkv, g_out = (scatter(g.astype(F32)) for g in (g_down, g_up, by_kinds(g_qkv), g_out))
        sums, q_sums = lax.psum((sums, q_sums), "shard")
    g_qkv, g_out, g_up, g_down, input_grad, *small = finish(sums, q_sums, (g_qkv, g_out, g_up, g_down), input_grad)
    return mixed, input_grad, g_qkv, g_out, g_up, g_down, *small


def solution(mesh):
    split, rows, same = P("shard", None), P("shard", None, None), P()
    return jax.shard_map(
        functools.partial(on_device, mesh.shape["shard"] == DEVICES),
        mesh=mesh,
        in_specs=(rows, rows, rows, P("shard")) + (split,) * 4 + (same,) * 10 + (split,) * 4,
        out_specs=(rows, rows) + (split,) * 4 + (same,) * 10,
        check_vma=False,
    )
```
